32 devices in a mesh: tm: 8 (over z, y), patch: 4 (over x, core).
Axes of the slice: x: 2, y: 2, z: 4, core: 2. Of those that a mesh axis runs over, the one named last changes fastest.
Arguments:
- tokens: bfloat16 [64, 64, 1408], P(('tm', 'patch')), may hold values from -6 to 6
- ln_gain: float32 [1408], replicated, may hold values from 0.1 to 1.9
- ln_bias: float32 [1408], replicated, may hold values from -3 to 3
- w_qkv: bfloat16 [1408, 4224], replicated, may hold values from -0.15625 to 0.15625
- w_out: bfloat16 [1408, 1408], replicated, may hold values from -0.15625 to 0.15625
- q_time: bfloat16 [64, 64, 1408], P(None, 'tm', 'patch'), may hold values from -24 to 24
- k_time: bfloat16 [64, 64, 1408], P(None, 'tm', 'patch'), may hold values from -24 to 24
- v_time: bfloat16 [64, 64, 1408], P(None, 'tm', 'patch'), may hold values from -4 to 4
- grad_out: bfloat16 [64, 64, 1408], P(('tm', 'patch')), may hold values from -6 to 6
Outputs:
- grad_x: bfloat16 [64, 64, 1408], P(('tm', 'patch'))
- grad_w_qkv: float32 [1408, 4224], P(('tm', 'patch'))
The draws below stay inside these ranges and needn't reach their ends.
All inputs are finite; a program needn't handle non-finite values.
Results may differ from the reference program's by a relative error of at most 0.0061.
Values may be sent and summed in bfloat16 or wider, within the bound.
No kernel may reach another device: no remote copies, remote signals or barrier semaphores. Data moves between devices by JAX's collectives and lax.ppermute only.
A program may use at most 128 MiB of HBM per device.

```python
import math
import jax
import jax.numpy as jnp
from jax import lax

D = 1408
HEADS = 16
DH = 88
P_KEEP = 64
FRAMES = 64
TOKENS = 4096


def draw_q_time(key, part):
    result = jnp.clip(jax.random.normal(jax.random.fold_in(key, 1), (FRAMES, P_KEEP, D), jnp.float32), -4.0, 4.0)
    return result.astype(jnp.bfloat16)


def draw_k_time(key, part):
    result = jnp.clip(jax.random.normal(jax.random.fold_in(key, 2), (FRAMES, P_KEEP, D), jnp.float32), -4.0, 4.0)
    return result.astype(jnp.bfloat16)


def strengthened(drawn, stream_key, source, target, parts, factor):
    owner, partner = [(jnp.arange(drawn.shape[position]) // (drawn.shape[position] // parts)).reshape([-1 if axis == position else 1 for axis in range(drawn.ndim)]) for position in (source, target)]
    chosen = jax.random.permutation(stream_key, parts)[partner]
    strong = (owner == chosen) | (owner == (partner + parts // 2) % parts)
    return jnp.where(strong, factor * drawn, drawn)


def block_levels(own_key, dims, cuts, smallest, high):
    def one(dim, parts):
        heights = jax.random.uniform(jax.random.fold_in(jax.random.fold_in(own_key, 6), dim), (parts,), jnp.float32, smallest / len(cuts), high / len(cuts))
        return jnp.repeat(jnp.exp(heights), dims[dim] // parts).reshape((-1,) + (1,) * (len(dims) - dim - 1))

    level = one(*cuts[0])
    for cut in cuts[1:]:
        level = level * one(*cut)
    return level


def gaussian(rng, extent, scale, limit, shards=(), dtype=jnp.bfloat16):
    array = jax.random.normal(rng, extent, jnp.float32) * scale
    if len(shards) > 0:
        array = block_levels(rng, extent, shards, -0.22, 0.18) * array
    return jnp.clip(array, min=-limit, max=limit).astype(dtype)


def heavy_noise(own_key, shape, scale, reach, pieces, heavy, kind=jnp.bfloat16):
    values = scale * jax.random.normal(own_key, shape, jnp.float32)
    if pieces:
        values = values * block_levels(own_key, shape, pieces, -0.22, 0.18)
    return jnp.clip(strengthened(values, jax.random.fold_in(own_key, 3), *heavy), -reach, reach).astype(kind)


def setup_inputs(seed: int = 0) -> dict:
    splits = jax.random.split(jax.random.key(seed), 10)
    return {
        "tokens": heavy_noise(splits[0], (FRAMES, P_KEEP, D), 1.0, 6.0, ((0, 32),), (0, 2, 32, 2.75)),
        "ln_gain": jnp.clip(1.0 + 0.18 * jax.random.normal(splits[1], (D,), jnp.float32), 0.1, 1.9),
        "ln_bias": gaussian(splits[2], (D,), 0.5, 3.0, (), jnp.float32),
        "w_qkv": gaussian(splits[3], (D, 3 * D), D ** -0.5, 0.15625),
        "w_out": gaussian(splits[4], (D, D), D ** -0.5, 0.15625),
        "q_time": draw_q_time(jax.random.fold_in(splits[9], 71), 0),
        "k_time": draw_k_time(jax.random.fold_in(splits[9], 71), 0),
        "v_time": gaussian(splits[7], (FRAMES, P_KEEP, D), 1.0, 4.0, ((1, 8), (2, 4))),
        "grad_out": gaussian(splits[8], (FRAMES, P_KEEP, D), 1.0, 6.0, ((0, 32),)),
    }


def round_low(value):
    return lax.optimization_barrier(value.astype(jnp.bfloat16)).astype(jnp.float32)

def attend(items):
    query_rows, key_rows, value_rows, grad_rows = items
    factor = 1.0 / math.sqrt(DH)
    query_heads = query_rows.astype(jnp.float32).reshape(FRAMES, HEADS, DH)
    key_heads = key_rows.astype(jnp.float32).reshape(FRAMES, HEADS, DH)
    value_heads = value_rows.astype(jnp.float32).reshape(FRAMES, HEADS, DH)
    grad_heads = grad_rows.astype(jnp.float32).reshape(FRAMES, HEADS, DH)
    scores = jnp.einsum('thd,shd->hts', query_heads, key_heads) * factor
    row_max = lax.optimization_barrier(jnp.max(scores, axis=-1, keepdims=True))
    exponent = jnp.exp(scores - row_max)
    probability = exponent / lax.optimization_barrier(jnp.sum(exponent, axis=-1, keepdims=True))
    prob_grad = jnp.einsum('thd,shd->hts', grad_heads, value_heads)
    row_dot = lax.optimization_barrier(jnp.sum(probability * prob_grad, axis=-1, keepdims=True))
    score_grad = round_low(probability * (prob_grad - row_dot) * factor)
    prob_low = round_low(probability)
    grad_query = jnp.einsum('hts,shd->thd', score_grad, key_heads).astype(jnp.bfloat16).reshape(FRAMES, D)
    grad_key = jnp.einsum('hts,thd->shd', score_grad, query_heads).astype(jnp.bfloat16).reshape(FRAMES, D)
    grad_value = jnp.einsum('hts,thd->shd', prob_low, grad_heads).astype(jnp.bfloat16).reshape(FRAMES, D)
    return (grad_query, grad_key, grad_value)

def reference(tokens, ln_gain, ln_bias, w_qkv, w_out, q_time, k_time, v_time, grad_out):
    factor = 1.0 / math.sqrt(TOKENS)
    grad_rows = grad_out.reshape(-1, D)
    d_attn = jnp.dot(grad_rows, w_out.T, preferred_element_type=jnp.float32).astype(jnp.bfloat16)
    moved = (jnp.swapaxes(q_time, 0, 1), jnp.swapaxes(k_time, 0, 1), jnp.swapaxes(v_time, 0, 1), jnp.swapaxes(d_attn.reshape(FRAMES, P_KEEP, D), 0, 1))
    grad_query, grad_key, grad_value = lax.map(attend, moved)
    grad_qkv = jnp.concatenate([jnp.swapaxes(grad_query, 0, 1), jnp.swapaxes(grad_key, 0, 1), jnp.swapaxes(grad_value, 0, 1)], axis=-1).reshape(-1, 3 * D)
    as_float = tokens.reshape(-1, D).astype(jnp.float32)
    centered = as_float - lax.optimization_barrier(jnp.mean(as_float, axis=-1, keepdims=True))
    variance = lax.optimization_barrier(jnp.mean(centered * centered, axis=-1, keepdims=True))
    inverse = lax.rsqrt(variance + 1e-06)
    normed = centered * inverse
    norm_out = (normed * ln_gain + ln_bias).astype(jnp.bfloat16)
    grad_w_qkv = jnp.dot(norm_out.T, grad_qkv, preferred_element_type=jnp.float32) * factor
    d_norm = jnp.dot(grad_qkv, w_qkv.T, preferred_element_type=jnp.float32)
    scaled = d_norm * ln_gain
    branch = inverse * (scaled - lax.optimization_barrier(jnp.mean(scaled, axis=-1, keepdims=True)) - normed * lax.optimization_barrier(jnp.mean(scaled * normed, axis=-1, keepdims=True)))
    grad_x = (grad_rows.astype(jnp.float32) + branch).astype(jnp.bfloat16).reshape(FRAMES, P_KEEP, D)
    return (grad_x, grad_w_qkv)
```

```python
import functools
import math

import jax
import jax.numpy as jnp
from jax import lax
from jax.experimental import pallas as pl
from jax.experimental.pallas import tpu as pltpu
from jax.sharding import PartitionSpec as P

DH = 88
BF = jnp.bfloat16
F32 = jnp.float32
ROWS = (((0,), (0,)), ((), ()))
COLS = (((1,), (1,)), ((), ()))


def attend_kernel(q_ref, k_ref, v_ref, d_ref, out_ref, acc_ref, *, columns, block):
    head = pl.program_id(0)
    n_tok, width = q_ref.shape
    factor = 1.0 / math.sqrt(DH)
    lane = lax.broadcasted_iota(jnp.int32, (1, width), 1)
    keep = jnp.where((lane >= head * DH) & (lane < (head + 1) * DH), 1.0, 0.0).astype(BF)

    @pl.when(head == 0)
    def _():
        acc_ref[...] = jnp.zeros_like(acc_ref)

    k_head = k_ref[...] * keep
    v_head = v_ref[...] * keep
    source = lax.broadcasted_iota(jnp.int32, (n_tok, block), 0) % columns
    target = lax.broadcasted_iota(jnp.int32, (n_tok, block), 1) % columns
    same = source == target
    for start in range(0, n_tok, block):
        rows = pl.ds(start, block)
        q_rows = q_ref[rows, :]
        d_rows = d_ref[rows, :]
        scores = lax.dot_general(k_head, q_rows, COLS, preferred_element_type=F32) * factor
        scores = jnp.where(same, scores, -jnp.inf)
        exponent = jnp.exp(scores - jnp.max(scores, axis=0, keepdims=True))
        probability = exponent * (1.0 / jnp.sum(exponent, axis=0, keepdims=True))
        prob_grad = lax.dot_general(v_head, d_rows, COLS, preferred_element_type=F32)
        row_dot = jnp.sum(probability * prob_grad, axis=0, keepdims=True)
        score_grad = (probability * (prob_grad - row_dot) * factor).astype(BF)
        prob_low = probability.astype(BF)
        acc_ref[0, rows, :] += lax.dot_general(score_grad, k_head, ROWS, preferred_element_type=F32)
        acc_ref[1] += jnp.dot(score_grad, q_rows * keep, preferred_element_type=F32)
        acc_ref[2] += jnp.dot(prob_low, d_rows * keep, preferred_element_type=F32)

    @pl.when(head == pl.num_programs(0) - 1)
    def _():
        out_ref[...] = acc_ref[...].astype(BF)


def attend(query, key, value, grad, columns):
    n_tok, width = query.shape
    whole = pl.BlockSpec((n_tok, width), lambda h: (0, 0))
    block = min(256, n_tok)
    return pl.pallas_call(
        functools.partial(attend_kernel, columns=columns, block=block),
        grid=(width // DH,),
        in_specs=[whole] * 4,
        out_specs=pl.BlockSpec((3, n_tok, width), lambda h: (0, 0, 0)),
        out_shape=jax.ShapeDtypeStruct((3, n_tok, width), BF),
        scratch_shapes=[pltpu.VMEM((3, n_tok, width), F32)],
        compiler_params=pltpu.CompilerParams(vmem_limit_bytes=48 * 1024 * 1024),
    )(query, key, value, grad)


def per_device(tokens, ln_gain, ln_bias, w_qkv, w_out, q_time, k_time, v_time, grad_out):
    t_dev, patches, width = tokens.shape
    frames, columns, part = q_time.shape
    n_tm = lax.axis_size("tm")
    n_patch = lax.axis_size("patch")
    n_pair = n_tm // 2
    devices = n_tm * n_patch
    n_tok = frames * columns
    own_rows = width // devices
    tm = lax.axis_index("tm")
    patch = lax.axis_index("patch")
    side = tm % 2
    both = ("tm", "patch")

    def swap(values, axis, size, bit):
        return lax.ppermute(values, axis, [(i, i ^ bit) for i in range(size)])

    grad_rows = grad_out.reshape(-1, width)
    d_attn = jnp.einsum(
        "to,jfo->jtf", grad_rows, w_out.reshape(n_patch, part, width), preferred_element_type=F32
    ).astype(BF)
    d_attn = d_attn.reshape(n_patch, t_dev, n_tm, columns, part).transpose(2, 0, 1, 3, 4)
    d_time = lax.all_to_all(
        d_attn.reshape(devices, t_dev, columns, part), both, 0, 0, tiled=True
    ).reshape(n_tok, part)

    as_float = tokens.reshape(-1, width).astype(F32)
    centered = as_float - jnp.mean(as_float, axis=-1, keepdims=True)
    variance = jnp.mean(centered * centered, axis=-1, keepdims=True)
    inverse = lax.rsqrt(variance + 1e-06)
    normed = centered * inverse
    norm_out = (normed * ln_gain + ln_bias).astype(BF)

    half = width // 2
    sent = norm_out.reshape(t_dev, n_pair, 2 * columns, n_pair, 2, n_patch * own_rows)
    sent = sent.transpose(1, 4, 0, 2, 3, 5).reshape(n_tm, t_dev, 2 * columns, half)
    got = lax.all_to_all(sent, "tm", 0, 0, tiled=True)
    bits = [1 << n for n in reversed(range(n_patch.bit_length() - 1))]
    for bit in bits:
        other = swap(got, "patch", n_patch, bit)
        high = (patch & bit) != 0
        got = jnp.stack([jnp.where(high, other, got), jnp.where(high, got, other)])
    order = tuple(reversed(range(len(bits))))
    at = len(bits)
    got = got.transpose((at,) + order + tuple(range(at + 1, got.ndim)))
    got = got.reshape(n_tm, n_patch, t_dev, 2, columns, half)
    norm_own, norm_other = [
        lax.dynamic_index_in_dim(got, index, 3, keepdims=False).reshape(n_tok, half)
        for index in (side, 1 - side)
    ]

    grads = attend(
        q_time.reshape(n_tok, part),
        k_time.reshape(n_tok, part),
        v_time.reshape(n_tok, part),
        d_time,
        columns,
    )
    grads_other = swap(grads, "tm", n_tm, 1)

    factor = 1.0 / math.sqrt(frames * patches)
    partial = jnp.einsum("na,cnf->caf", norm_own, grads, preferred_element_type=F32) + jnp.einsum(
        "na,cnf->caf", norm_other, grads_other, preferred_element_type=F32
    )
    partial = (partial * factor).astype(BF).reshape(3, n_pair * n_patch, own_rows, part)
    groups = [
        [(2 * z + y) * n_patch + p for z in range(n_pair) for p in range(n_patch)] for y in range(2)
    ]
    pieces = lax.all_to_all(
        partial.transpose(1, 0, 2, 3), both, 0, 0, axis_index_groups=groups, tiled=True
    )
    pieces = pieces.reshape(n_pair, n_patch, 3, own_rows, part).astype(F32)
    grad_w_qkv = jnp.sum(pieces, axis=0).transpose(2, 1, 0, 3).reshape(own_rows, 3 * width)

    weights = jnp.stack(
        [lax.dynamic_slice_in_dim(w_qkv, c * width + patch * part, part, 1) for c in range(3)]
    )
    share = jnp.einsum("cnf,caf->na", grads, weights, preferred_element_type=F32)
    share = share.reshape((n_tm,) + (2,) * len(bits) + (t_dev * columns, width))
    for bit in reversed(bits):
        high = (patch & bit) != 0
        axis = share.ndim - 3
        low_part = lax.index_in_dim(share, 0, axis, keepdims=False)
        high_part = lax.index_in_dim(share, 1, axis, keepdims=False)
        leave = jnp.where(high, low_part, high_part).astype(BF)
        stay = jnp.where(high, high_part, low_part)
        share = stay + swap(leave, "patch", n_patch, bit).astype(F32)
    d_norm = lax.all_to_all(share.astype(BF), "tm", 0, 0, tiled=True)
    d_norm = d_norm.reshape(n_tm, t_dev, columns, width).transpose(1, 0, 2, 3)
    d_norm = d_norm.reshape(-1, width).astype(F32)
    scaled = d_norm * ln_gain
    branch = inverse * (
        scaled
        - jnp.mean(scaled, axis=-1, keepdims=True)
        - normed * jnp.mean(scaled * normed, axis=-1, keepdims=True)
    )
    grad_x = (grad_rows.astype(F32) + branch).astype(BF).reshape(t_dev, patches, width)
    return (grad_x, grad_w_qkv)


def solution(mesh):
    return jax.shard_map(
        per_device,
        mesh=mesh,
        in_specs=(
            P(("tm", "patch"), None, None),
            P(),
            P(),
            P(),
            P(),
            P(None, "tm", "patch"),
            P(None, "tm", "patch"),
            P(None, "tm", "patch"),
            P(("tm", "patch"), None, None),
        ),
        out_specs=(P(("tm", "patch"), None, None), P(("tm", "patch"), None)),
        check_vma=False,
    )
```

```python
import functools
import math

import jax
import jax.numpy as jnp
from jax import lax
from jax.experimental import pallas as pl
from jax.experimental.pallas import tpu as pltpu
from jax.sharding import PartitionSpec as P

DH = 88
BF = jnp.bfloat16
F32 = jnp.float32
ROWS = (((0,), (0,)), ((), ()))
COLS = (((1,), (1,)), ((), ()))


def attend_kernel(q_ref, k_ref, v_ref, d_ref, out_ref, acc_ref, *, columns, block):
    head = pl.program_id(0)
    n_tok, width = q_ref.shape
    factor = 1.0 / math.sqrt(DH)
    lane = lax.broadcasted_iota(jnp.int32, (1, width), 1)
    keep = jnp.where((lane >= head * DH) & (lane < (head + 1) * DH), 1.0, 0.0).astype(BF)

    @pl.when(head == 0)
    def _():
        acc_ref[...] = jnp.zeros_like(acc_ref)

    k_head = k_ref[...] * keep
    v_head = v_ref[...] * keep
    source = lax.broadcasted_iota(jnp.int32, (n_tok, block), 0) % columns
    target = lax.broadcasted_iota(jnp.int32, (n_tok, block), 1) % columns
    same = source == target
    for start in range(0, n_tok, block):
        rows = pl.ds(start, block)
        q_rows = q_ref[rows, :]
        d_rows = d_ref[rows, :]
        scores = lax.dot_general(k_head, q_rows, COLS, preferred_element_type=F32) * factor
        scores = jnp.where(same, scores, -jnp.inf)
        exponent = jnp.exp(scores - jnp.max(scores, axis=0, keepdims=True))
        probability = exponent * (1.0 / jnp.sum(exponent, axis=0, keepdims=True))
        prob_grad = lax.dot_general(v_head, d_rows, COLS, preferred_element_type=F32)
        row_dot = jnp.sum(probability * prob_grad, axis=0, keepdims=True)
        score_grad = (probability * (prob_grad - row_dot) * factor).astype(BF)
        prob_low = probability.astype(BF)
        acc_ref[0, rows, :] += lax.dot_general(score_grad, k_head, ROWS, preferred_element_type=F32)
        acc_ref[1] += jnp.dot(score_grad, q_rows * keep, preferred_element_type=F32)
        acc_ref[2] += jnp.dot(prob_low, d_rows * keep, preferred_element_type=F32)

    @pl.when(head == pl.num_programs(0) - 1)
    def _():
        out_ref[...] = acc_ref[...].astype(BF)


def attend(query, key, value, grad, columns):
    n_tok, width = query.shape
    whole = pl.BlockSpec((n_tok, width), lambda h: (0, 0))
    block = min(256, n_tok)
    return pl.pallas_call(
        functools.partial(attend_kernel, columns=columns, block=block),
        grid=(width // DH,),
        in_specs=[whole] * 4,
        out_specs=pl.BlockSpec((3, n_tok, width), lambda h: (0, 0, 0)),
        out_shape=jax.ShapeDtypeStruct((3, n_tok, width), BF),
        scratch_shapes=[pltpu.VMEM((3, n_tok, width), F32)],
        compiler_params=pltpu.CompilerParams(vmem_limit_bytes=48 * 1024 * 1024),
        cost_estimate=pl.CostEstimate(
            flops=10 * n_tok * n_tok * width * (width // DH),
            transcendentals=n_tok * n_tok * (width // DH),
            bytes_accessed=14 * n_tok * width,
        ),
    )(query, key, value, grad)


def per_device(tokens, ln_gain, ln_bias, w_qkv, w_out, q_time, k_time, v_time, grad_out):
    t_dev, patches, width = tokens.shape
    frames, columns, part = q_time.shape
    n_tm = lax.axis_size("tm")
    n_patch = lax.axis_size("patch")
    n_pair = n_tm // 2
    n_chip = n_patch // 2
    devices = n_tm * n_patch
    n_tok = frames * columns
    own_rows = width // devices
    tm = lax.axis_index("tm")
    patch = lax.axis_index("patch")
    side = tm % 2
    core = patch % 2
    both = ("tm", "patch")

    def swap(values, axis, size, bit):
        return lax.ppermute(values, axis, [(i, i ^ bit) for i in range(size)])

    grad_rows = grad_out.reshape(-1, width)
    d_attn = jnp.einsum(
        "to,jfo->jtf", grad_rows, w_out.reshape(n_patch, part, width), preferred_element_type=F32
    ).astype(BF)
    d_attn = d_attn.reshape(n_patch, t_dev, n_tm, columns, part).transpose(2, 0, 1, 3, 4)
    d_attn, tokens = lax.optimization_barrier((d_attn, tokens))
    d_time = lax.all_to_all(
        d_attn.reshape(devices, t_dev, columns, part), both, 0, 0, tiled=True
    ).reshape(n_tok, part)

    saved = [values.reshape(n_tok, part) for values in (q_time, k_time, v_time)]
    saved_other = [swap(values, "tm", n_tm, 1) for values in saved]

    as_float = tokens.reshape(-1, width).astype(F32)
    centered = as_float - jnp.mean(as_float, axis=-1, keepdims=True)
    variance = jnp.mean(centered * centered, axis=-1, keepdims=True)
    inverse = lax.rsqrt(variance + 1e-06)
    normed = centered * inverse
    norm_out = (normed * ln_gain + ln_bias).astype(BF)

    quarter = width // 4
    sent = norm_out.reshape(t_dev, n_pair, 2 * columns, n_pair, 2, n_chip, 2, own_rows)
    sent = sent.transpose(1, 4, 6, 0, 2, 3, 5, 7).reshape(
        n_pair, 2, 1, 2, t_dev, 2 * columns, quarter
    )
    sent = jnp.broadcast_to(sent, (n_pair, 2, n_chip, 2, t_dev, 2 * columns, quarter))
    weights = [
        lax.dynamic_slice_in_dim(w_qkv, c * width + patch * part, part, 1)
        for c in range(3)
    ]
    d_time, sent, saved_other, weights = lax.optimization_barrier(
        (d_time, sent, saved_other, weights)
    )
    d_other = swap(d_time, "tm", n_tm, 1)
    got = lax.all_to_all(
        sent.reshape(devices, t_dev, 2 * columns, quarter), both, 0, 0, tiled=True
    )
    got = got.reshape(frames, 2, columns, quarter)
    norm_own, norm_other = [
        lax.dynamic_index_in_dim(got, index, 1, keepdims=False).reshape(n_tok, quarter)
        for index in (side, 1 - side)
    ]

    grads = attend(*saved, d_time, columns)
    grads_other = attend(*saved_other, d_other, columns)
    grads_core = swap(grads, "patch", n_patch, 1)
    grads_other_core = swap(grads_other, "patch", n_patch, 1)
    grads, grads_other, grads_core, grads_other_core, norm_own, norm_other = (
        lax.optimization_barrier(
            (grads, grads_other, grads_core, grads_other_core, norm_own, norm_other)
        )
    )

    factor = 1.0 / math.sqrt(frames * patches)

    def product(one, other):
        total = jnp.einsum("na,cnf->caf", norm_own, one, preferred_element_type=F32)
        total += jnp.einsum("na,cnf->caf", norm_other, other, preferred_element_type=F32)
        return (total * factor).astype(BF).reshape(3, n_pair * n_chip, own_rows, part)

    partial = jnp.stack([product(grads, grads_other), product(grads_core, grads_other_core)])
    groups = [
        [(2 * z + y) * n_patch + 2 * x + c for z in range(n_pair) for x in range(n_chip)]
        for y in range(2)
        for c in range(2)
    ]
    pieces = lax.all_to_all(
        partial.transpose(2, 0, 1, 3, 4), both, 0, 0, axis_index_groups=groups, tiled=True
    )
    pieces = pieces.reshape(n_pair, n_chip, 2, 3, own_rows, part).astype(F32)
    summed = jnp.sum(pieces, axis=0)
    summed = jnp.where(core == 0, summed, summed[:, ::-1])
    grad_w_qkv = summed.transpose(3, 2, 0, 1, 4).reshape(own_rows, 3 * width)

    share = sum(
        lax.dot_general(grads[c], weights[c], COLS, preferred_element_type=F32) for c in range(3)
    )

    def split(values, axis, high):
        low_part = lax.index_in_dim(values, 0, axis, keepdims=False)
        high_part = lax.index_in_dim(values, 1, axis, keepdims=False)
        return jnp.where(high, high_part, low_part), jnp.where(high, low_part, high_part)

    bits = n_patch.bit_length() - 1
    share = share.reshape((n_tm,) + (2,) * bits + (t_dev * columns, width))
    for n in range(bits):
        stay, leave = split(share, bits - n, (patch & (1 << n)) != 0)
        share = stay + swap(leave.astype(BF), "patch", n_patch, 1 << n).astype(F32)
    bits = n_tm.bit_length() - 1
    share = share.astype(BF).reshape((2,) * bits + (1, t_dev * columns, width))
    for n in range(bits):
        high = (tm & (1 << n)) != 0
        stay, leave = split(share, bits - 1 - n, high)
        come = swap(leave, "tm", n_tm, 1 << n)
        share = jnp.concatenate([jnp.where(high, come, stay), jnp.where(high, stay, come)], bits - 1 - n)
    d_norm = share.reshape(n_tm, t_dev, columns, width).transpose(1, 0, 2, 3)
    d_norm = d_norm.reshape(-1, width).astype(F32)
    scaled = d_norm * ln_gain
    branch = inverse * (
        scaled
        - jnp.mean(scaled, axis=-1, keepdims=True)
        - normed * jnp.mean(scaled * normed, axis=-1, keepdims=True)
    )
    grad_x = (grad_rows.astype(F32) + branch).astype(BF).reshape(t_dev, patches, width)
    return (grad_x, grad_w_qkv)


def solution(mesh):
    return jax.shard_map(
        per_device,
        mesh=mesh,
        in_specs=(
            P(("tm", "patch"), None, None),
            P(),
            P(),
            P(),
            P(),
            P(None, "tm", "patch"),
            P(None, "tm", "patch"),
            P(None, "tm", "patch"),
            P(("tm", "patch"), None, None),
        ),
        out_specs=(P(("tm", "patch"), None, None), P(("tm", "patch"), None)),
        check_vma=False,
    )
```

```python
import functools
import math

import jax
import jax.numpy as jnp
from jax import lax
from jax.experimental import pallas as pl
from jax.experimental.pallas import tpu as pltpu
from jax.sharding import PartitionSpec as P

DH = 88
BF = jnp.bfloat16
F32 = jnp.float32
ROWS = (((0,), (0,)), ((), ()))
COLS = (((1,), (1,)), ((), ()))
ROOM = pltpu.CompilerParams(vmem_limit_bytes=48 * 1024 * 1024)


def attend_kernel(q_ref, k_ref, v_ref, d_ref, out_ref, *, columns, block):
    n_tok, width = q_ref.shape
    factor = 1.0 / math.sqrt(DH)
    source = lax.broadcasted_iota(jnp.int32, (n_tok, block), 0)
    target = lax.broadcasted_iota(jnp.int32, (n_tok, block), 1)
    same = ((source ^ target) & (columns - 1)) == 0
    for head in range(width // DH):
        lanes = slice(head * DH, (head + 1) * DH)
        k_head = k_ref[:, lanes]
        v_head = v_ref[:, lanes]
        key_sum = value_sum = None
        for start in range(0, n_tok, block):
            rows = slice(start, start + block)
            q_rows = q_ref[rows, lanes]
            d_rows = d_ref[rows, lanes]
            scores = lax.dot_general(k_head, q_rows, COLS, preferred_element_type=F32) * factor
            scores = jnp.where(same, scores, -jnp.inf)
            exponent = jnp.exp(scores - jnp.max(scores, axis=0, keepdims=True))
            probability = exponent * (1.0 / jnp.sum(exponent, axis=0, keepdims=True))
            prob_grad = lax.dot_general(v_head, d_rows, COLS, preferred_element_type=F32)
            row_dot = jnp.sum(probability * prob_grad, axis=0, keepdims=True)
            score_grad = (probability * (prob_grad - row_dot) * factor).astype(BF)
            prob_low = probability.astype(BF)
            query = lax.dot_general(score_grad, k_head, ROWS, preferred_element_type=F32)
            out_ref[0, rows, lanes] = query.astype(BF)
            key = jnp.dot(score_grad, q_rows, preferred_element_type=F32)
            value = jnp.dot(prob_low, d_rows, preferred_element_type=F32)
            key_sum = key if key_sum is None else key_sum + key
            value_sum = value if value_sum is None else value_sum + value
        out_ref[1, :, lanes] = key_sum.astype(BF)
        out_ref[2, :, lanes] = value_sum.astype(BF)
def attend(query,key,value,grad,columns,block=512):
    n_tok,width=query.shape
    return pl.pallas_call(functools.partial(attend_kernel,columns=columns,block=min(block,n_tok)),
        out_shape=jax.ShapeDtypeStruct((3,n_tok,width),BF),
        compiler_params=ROOM)(query,key,value,grad)

def first_kernel(
    x_ref, gain_ref, bias_ref, grad_ref, w_ref, out_ref, norm_ref, *, n_pair, columns, own_rows, t_dev
):
    step = pl.program_id(0)
    n_rows, width = x_ref.shape
    part = w_ref.shape[0]
    patches = n_rows // t_dev

    @pl.when(step == 0)
    def _():
        rows = x_ref[...].astype(F32)
        centered = rows - jnp.mean(rows, axis=-1, keepdims=True)
        variance = jnp.mean(centered * centered, axis=-1, keepdims=True)
        norm_ref[...] = centered * lax.rsqrt(variance + 1e-06) * gain_ref[...] + bias_ref[...]

    def pick(values, at):
        pieces = [values[t * patches + at : t * patches + at + columns] for t in range(t_dev)]
        return jnp.concatenate(pieces, axis=0).astype(BF)

    d_attn = lax.dot_general(grad_ref[...], w_ref[...], COLS, preferred_element_type=F32)
    for tm in range(2 * n_pair):
        out_ref[tm * 4 + step, 0] = pick(d_attn, tm * columns)
    for y in range(2):
        for c in range(2):

            @pl.when(step == 2 * y + c)
            def _(y=y, c=c):
                starts = [
                    (((2 * z + y) * 2 + x) * 2 + c) * own_rows for z in range(n_pair) for x in range(2)
                ]
                quarter = jnp.concatenate(
                    [norm_ref[:, start : start + own_rows] for start in starts], axis=1
                )
                for z in range(n_pair):
                    for x in range(2):
                        out_ref[((2 * z + y) * 2 + x) * 2 + c, 1] = pick(
                            quarter, (2 * z + (y ^ x)) * columns
                        )


def first_product(tokens, gain, bias, grads, w_out, n_pair, columns, own_rows, t_dev):
    n_rows, width = tokens.shape
    part = width // 4
    rows = pl.BlockSpec((n_rows, width), lambda j: (0, 0))
    line = pl.BlockSpec((1, width), lambda j: (0, 0))
    shape = (8 * n_pair, 2, t_dev * columns, part)
    return pl.pallas_call(
        functools.partial(
            first_kernel, n_pair=n_pair, columns=columns, own_rows=own_rows, t_dev=t_dev
        ),
        grid=(4,),
        in_specs=[rows, line, line, rows, pl.BlockSpec((part, width), lambda j: (j, 0))],
        out_specs=pl.BlockSpec(shape, lambda j: (0, 0, 0, 0)),
        out_shape=jax.ShapeDtypeStruct(shape, BF),
        scratch_shapes=[pltpu.VMEM((n_rows, width), F32)],
        compiler_params=ROOM,
    )(tokens, gain[None], bias[None], grads, w_out)


def share_kernel(where_ref, g_ref, w_ref, leave_ref, stay_ref, win_ref, pad_ref, sem, *, n_patch):
    kinds, n_tok, part = g_ref.shape
    window = win_ref.shape[2]
    width = win_ref.shape[1]
    patch = where_ref[0]
    core = patch % 2
    starts=[min(part * j // 128 * 128, width - window) for j in range(n_patch)]
    start = sum(jnp.where(patch == j, s, 0) for j, s in enumerate(starts))
    copies = [pltpu.make_async_copy(w_ref.at[:, pl.ds(pl.multiple_of(c * width + start, 128), window)], win_ref.at[c], sem.at[c]) for c in range(kinds)]
    for copy in copies:
        copy.start()
    for j in range(n_patch):
        @pl.when(patch == j)
        def _(j=j):
            before = part * j - starts[j]
            for c in range(kinds):
                pieces = [g_ref[c]]
                if before: pieces = [jnp.zeros((n_tok, before), BF)] + pieces
                after = window - before - part
                if after: pieces = pieces + [jnp.zeros((n_tok, after), BF)]
                pad_ref[c] = jnp.concatenate(pieces, axis=1).reshape(pad_ref.shape[1:])
    for copy in copies:
        copy.wait()
    shape = leave_ref.shape
    def product(which):
        total = None
        for c in range(kinds):
            one = lax.dot_general(pad_ref[c, :, which].reshape(n_tok // 2, window), win_ref[c], COLS, preferred_element_type=F32)
            total = one if total is None else total + one
        return total.reshape(shape)
    leave_ref[...] = product(1 - core).astype(BF)
    stay_ref[...] = product(core)
def share_send(grads, w_qkv, patch, n_patch, group):
    kinds,n_tok,part=grads.shape
    width=w_qkv.shape[0]
    window=-(-(part+96)//128)*128
    n=n_tok//(2*group)
    return pl.pallas_call(functools.partial(share_kernel,n_patch=n_patch),
        grid_spec=pltpu.PrefetchScalarGridSpec(num_scalar_prefetch=1,grid=(1,),
            in_specs=[pl.BlockSpec((kinds,n_tok,part),lambda i,s:(0,0,0)),pl.BlockSpec(memory_space=pl.ANY)],
            out_specs=[pl.BlockSpec((n,group,width),lambda i,s:(0,0,0))]*2,
            scratch_shapes=[pltpu.VMEM((kinds,width,window),BF),pltpu.VMEM((kinds,n,2,group,window),BF),pltpu.SemaphoreType.DMA((kinds,))]),
        out_shape=[jax.ShapeDtypeStruct((n,group,width),BF),jax.ShapeDtypeStruct((n,group,width),F32)],
        compiler_params=ROOM)(patch[None],grads,w_qkv)

def product_kernel(
    chip_ref, mine_ref, theirs_ref, own_ref, other_ref, own_core_ref, other_core_ref, out_ref, *, factor
):
    kinds, n_tok, part = own_ref.shape
    own_rows = out_ref.shape[1]
    mine = mine_ref[...].astype(F32).T.astype(BF)
    theirs = theirs_ref[...].astype(F32).T.astype(BF)
    first = chip_ref[0] == 0
    left = [jnp.where(first, mine, theirs), jnp.where(first, theirs, mine)]
    for r, pair in enumerate(((own_ref, other_ref), (own_core_ref, other_core_ref))):
        for c in range(kinds):
            total = jnp.dot(left[0], pair[0][c], preferred_element_type=F32)
            total += jnp.dot(left[1], pair[1][c], preferred_element_type=F32)
            total = total * factor
            at = (r * kinds + c) * part
            for k in range(out_ref.shape[0]):
                out_ref[k, :, at : at + part] = total[k * own_rows : (k + 1) * own_rows].astype(BF)


def product(chip, mine, theirs, grads, other, core, other_core, own_rows, factor):
    kinds, n_tok, part = grads.shape
    norm = pl.BlockSpec(mine.shape, lambda i, s: (0, 0))
    whole = pl.BlockSpec(grads.shape, lambda i, s: (0, 0, 0))
    shape = (part // own_rows, own_rows, 2 * kinds * part)
    return pl.pallas_call(
        functools.partial(product_kernel, factor=factor),
        grid_spec=pltpu.PrefetchScalarGridSpec(
            num_scalar_prefetch=1,
            grid=(1,),
            in_specs=[norm, norm, whole, whole, whole, whole],
            out_specs=pl.BlockSpec(shape, lambda i, s: (0, 0, 0)),
        ),
        out_shape=jax.ShapeDtypeStruct(shape, BF),
        compiler_params=ROOM,
    )(chip[None], mine, theirs, grads, other, core, other_core)


def final_kernel(core_ref, in_ref, out_ref, *, part, kinds):
    n_pair, n_chip, own_rows, _ = in_ref.shape
    for core in range(2):
        @pl.when(core_ref[0] == core)
        def _(core=core):
            for x in range(n_chip):
                total = in_ref[0, x].astype(F32)
                for z in range(1, n_pair):
                    total = total + in_ref[z, x].astype(F32)
                for r in range(2):
                    for c in range(kinds):
                        at = (c * n_chip * 2 + 2 * x + (r ^ core)) * part
                        src = (r * kinds + c) * part
                        out_ref[:, at : at + part] = total[:, src : src + part]
def final_sum(pieces, core, part, kinds):
    n_pair,n_chip,own_rows,_=pieces.shape
    return pl.pallas_call(functools.partial(final_kernel,part=part,kinds=kinds),
        grid_spec=pltpu.PrefetchScalarGridSpec(num_scalar_prefetch=1,grid=(1,),
            in_specs=[pl.BlockSpec(pieces.shape,lambda i,s:(0,0,0,0))],
            out_specs=pl.BlockSpec((own_rows,2*n_chip*kinds*part),lambda i,s:(0,0))),
        out_shape=jax.ShapeDtypeStruct((own_rows,2*n_chip*kinds*part),F32),compiler_params=ROOM)(core[None],pieces)


def per_device(tokens, ln_gain, ln_bias, w_qkv, w_out, q_time, k_time, v_time, grad_out):
    t_dev, patches, width = tokens.shape
    frames, columns, part = q_time.shape
    n_tm = lax.axis_size("tm")
    n_patch = lax.axis_size("patch")
    n_pair = n_tm // 2
    n_chip = n_patch // 2
    devices = n_tm * n_patch
    n_tok = frames * columns
    own_rows = width // devices
    tm = lax.axis_index("tm")
    patch = lax.axis_index("patch")
    side = tm % 2
    core = patch % 2
    both = ("tm", "patch")

    def swap(values, axis, size, bit):
        return lax.ppermute(values, axis, [(i, i ^ bit) for i in range(size)])

    grad_rows = grad_out.reshape(-1, width)
    token_rows = tokens.reshape(-1, width)
    sent = first_product(
        token_rows, ln_gain, ln_bias, grad_rows, w_out, n_pair, columns, own_rows, t_dev
    )
    got = lax.all_to_all(sent, both, 0, 0, tiled=True)

    saved = [values.reshape(n_tok, part) for values in (q_time, k_time, v_time)]
    saved_other = [swap(values, "tm", n_tm, 1) for values in saved]
    got, saved_other = lax.optimization_barrier((got, saved_other))
    d_time = got[:, 0].reshape(n_tok, part)
    mine = got[:, 1].reshape(n_tok, part)
    d_other = swap(d_time, "tm", n_tm, 1)
    theirs = swap(mine, "patch", n_patch, 2)
    d_other, theirs = lax.optimization_barrier((d_other, theirs))

    as_float = token_rows.astype(F32)
    centered = as_float - jnp.mean(as_float, axis=-1, keepdims=True)
    variance = jnp.mean(centered * centered, axis=-1, keepdims=True)
    inverse = lax.rsqrt(variance + 1e-06)
    normed = centered * inverse

    grads = attend(*saved, d_time, columns)
    grads_core = swap(grads, "patch", n_patch, 1)
    grads_other = attend(*saved_other, d_other, columns)
    leave, stay = share_send(grads, w_qkv, patch, n_patch, t_dev * columns)
    leave, stay, grads_other = lax.optimization_barrier((leave, stay, grads_other))
    grads_other_core = swap(grads_other, "patch", n_patch, 1)

    factor = 1.0 / math.sqrt(frames * patches)
    groups = [
        [(2 * z + y) * n_patch + 2 * x + c for z in range(n_pair) for x in range(n_chip)]
        for y in range(2)
        for c in range(2)
    ]
    pieces = lax.all_to_all(
        product(
            patch // 2, mine, theirs, grads, grads_other, grads_core, grads_other_core, own_rows, factor
        ),
        both,
        0,
        0,
        axis_index_groups=groups,
        tiled=True,
    )
    grad_w_qkv = final_sum(pieces.reshape(n_pair, n_chip, own_rows, 6 * part), core, part, 3)

    def split(values, axis, high):
        low_part = lax.index_in_dim(values, 0, axis, keepdims=False)
        high_part = lax.index_in_dim(values, 1, axis, keepdims=False)
        return jnp.where(high, high_part, low_part), jnp.where(high, low_part, high_part)

    share = stay + swap(leave, "patch", n_patch, 1).astype(F32)
    bits = n_patch.bit_length() - 1
    share = share.reshape((n_tm,) + (2,) * (bits - 1) + (t_dev * columns, width))
    for n in range(1, bits):
        stay, leave = split(share, bits - n, (patch & (1 << n)) != 0)
        share = stay + swap(leave.astype(BF), "patch", n_patch, 1 << n).astype(F32)
    bits = n_tm.bit_length() - 1
    share = share.astype(BF).reshape((2,) * bits + (1, t_dev * columns, width))
    for n in range(bits):
        high = (tm & (1 << n)) != 0
        stay, leave = split(share, bits - 1 - n, high)
        come = swap(leave, "tm", n_tm, 1 << n)
        share = jnp.concatenate([jnp.where(high, come, stay), jnp.where(high, stay, come)], bits - 1 - n)
    d_norm = share.reshape(n_tm, t_dev, columns, width).transpose(1, 0, 2, 3)
    d_norm = d_norm.reshape(-1, width).astype(F32)
    scaled = d_norm * ln_gain
    branch = inverse * (
        scaled
        - jnp.mean(scaled, axis=-1, keepdims=True)
        - normed * jnp.mean(scaled * normed, axis=-1, keepdims=True)
    )
    grad_x = (grad_rows.astype(F32) + branch).astype(BF).reshape(t_dev, patches, width)
    return (grad_x, grad_w_qkv)


def solution(mesh):
    return jax.shard_map(
        per_device,
        mesh=mesh,
        in_specs=(
            P(("tm", "patch"), None, None),
            P(),
            P(),
            P(),
            P(),
            P(None, "tm", "patch"),
            P(None, "tm", "patch"),
            P(None, "tm", "patch"),
            P(("tm", "patch"), None, None),
        ),
        out_specs=(P(("tm", "patch"), None, None), P(("tm", "patch"), None)),
        check_vma=False,
    )
```

```python
import functools
import math

import jax
import jax.numpy as jnp
from jax import lax
from jax.experimental import pallas as pl
from jax.experimental.pallas import tpu as pltpu
from jax.sharding import PartitionSpec as P

DH = 88
BF = jnp.bfloat16
F32 = jnp.float32
ROWS = (((0,), (0,)), ((), ()))
COLS = (((1,), (1,)), ((), ()))
CROSS = (((0,), (1,)), ((), ()))
ROOM = pltpu.CompilerParams(vmem_limit_bytes=48 * 1024 * 1024)


def attend_kernel(q_ref, k_ref, v_ref, d_ref, out_ref, *, columns):
    n_tok, width = q_ref.shape
    factor = 1.0 / math.sqrt(DH)
    source = lax.broadcasted_iota(jnp.int32, (n_tok, n_tok), 0)
    target = lax.broadcasted_iota(jnp.int32, (n_tok, n_tok), 1)
    same = ((source ^ target) & (columns - 1)) == 0
    for start in range(0, width, DH):
        lanes = slice(start, start + DH)
        query, key, value, grad = [ref[:, lanes] for ref in (q_ref, k_ref, v_ref, d_ref)]
        scores = lax.dot_general(key, query, COLS, preferred_element_type=F32) * factor
        scores = jnp.where(same, scores, -jnp.inf)
        exponent = jnp.exp(scores - jnp.max(scores, axis=0, keepdims=True))
        probability = exponent * (1.0 / jnp.sum(exponent, axis=0, keepdims=True))
        prob_grad = lax.dot_general(value, grad, COLS, preferred_element_type=F32)
        row_dot = jnp.sum(probability * prob_grad, axis=0, keepdims=True)
        score_grad = (probability * (prob_grad - row_dot) * factor).astype(BF)
        prob_low = probability.astype(BF)
        for kind, (left, right, dims) in enumerate(
            ((key, score_grad, ROWS), (query, score_grad, CROSS), (grad, prob_low, CROSS))
        ):
            total = lax.dot_general(left, right, dims, preferred_element_type=F32)
            out_ref[kind, lanes, :] = total.astype(BF)


def attend(query, key, value, grad, columns):
    n_tok, width = query.shape
    return pl.pallas_call(
        functools.partial(attend_kernel, columns=columns),
        out_shape=jax.ShapeDtypeStruct((3, width, n_tok), BF),
        compiler_params=ROOM,
    )(query, key, value, grad)


def norm_kernel(x_ref, gain_ref, bias_ref, out_ref, *, n_pair, n_chip, columns, own_rows, t_dev):
    width = x_ref.shape[1]
    rows = x_ref[...].astype(F32)
    centered = rows - jnp.mean(rows, axis=-1, keepdims=True)
    variance = jnp.mean(centered * centered, axis=-1, keepdims=True)
    norm = centered * lax.rsqrt(variance + 1e-06) * gain_ref[...] + bias_ref[...]
    patches = x_ref.shape[0] // t_dev
    for y in range(2):
        for c in range(2):
            starts = [((2 * z + y) * n_chip + x) * 2 * own_rows + c * own_rows for z in range(n_pair) for x in range(n_chip)]
            part = jnp.concatenate([norm[:, s : s + own_rows] for s in starts], axis=1)
            for z in range(n_pair):
                for slot in range(2):
                    at = (2 * z + (y ^ slot)) * columns
                    piece = jnp.concatenate([part[t * patches + at : t * patches + at + columns] for t in range(t_dev)], axis=0).astype(BF)
                    for x in range(n_chip):
                        out_ref[((2 * z + y) * n_chip + x) * 2 + c, slot] = piece
def norm_send(tokens, gain, bias, n_pair, n_chip, columns, own_rows, t_dev):
    devices = 4 * n_pair * n_chip
    return pl.pallas_call(functools.partial(norm_kernel,n_pair=n_pair,n_chip=n_chip,columns=columns,own_rows=own_rows,t_dev=t_dev),
        out_shape=jax.ShapeDtypeStruct((devices,2,t_dev*columns,tokens.shape[1]//4),BF),compiler_params=ROOM)(tokens,gain[None],bias[None])

def share_kernel(where_ref, g_ref, w_ref, leave_ref, stay_ref, win_ref, pad_ref, acc_ref, sem, *, n_patch):
    kinds, part, n_tok = g_ref.shape
    _, width, window = win_ref.shape
    patch = where_ref[0]
    starts = [min(part * j // 128 * 128, width - window) for j in range(n_patch)]
    start = sum(jnp.where(patch == j, at, 0) for j, at in enumerate(starts))
    copies = [
        pltpu.make_async_copy(
            w_ref.at[:, pl.ds(pl.multiple_of(c * width + start, 128), window)], win_ref.at[c], sem.at[c]
        )
        for c in range(kinds)
    ]
    for copy in copies:
        copy.start()
    pad_ref[...] = jnp.zeros_like(pad_ref)
    for j in range(n_patch):

        @pl.when(patch == j)
        def _(j=j):
            before = part * j - starts[j]
            for c in range(kinds):
                pad_ref[c, before : before + part, :] = g_ref[c]

    total = None
    for c, copy in enumerate(copies):
        copy.wait()
        one = lax.dot_general(pad_ref[c], win_ref[c], CROSS, preferred_element_type=F32)
        total = one if total is None else total + one
    acc_ref[...] = total.reshape(acc_ref.shape)
    leave_ref[...] = acc_ref[:, 1 - patch % 2].astype(BF)
    stay_ref[...] = acc_ref[:, patch % 2]


def share_send(grads, w_qkv, patch, n_patch, group):
    kinds, part, n_tok = grads.shape
    width = w_qkv.shape[0]
    window = -(-(part + 96) // 128) * 128
    n = n_tok // (2 * group)
    return pl.pallas_call(
        functools.partial(share_kernel, n_patch=n_patch),
        grid_spec=pltpu.PrefetchScalarGridSpec(
            num_scalar_prefetch=1,
            grid=(1,),
            in_specs=[
                pl.BlockSpec((kinds, part, n_tok), lambda i, s: (0, 0, 0)),
                pl.BlockSpec(memory_space=pl.ANY),
            ],
            out_specs=[pl.BlockSpec((n, group, width), lambda i, s: (0, 0, 0))] * 2,
            scratch_shapes=[
                pltpu.VMEM((kinds, width, window), BF),
                pltpu.VMEM((kinds, window, n_tok), BF),
                pltpu.VMEM((n, 2, group, width), F32),
                pltpu.SemaphoreType.DMA((kinds,)),
            ],
        ),
        out_shape=[
            jax.ShapeDtypeStruct((n, group, width), BF),
            jax.ShapeDtypeStruct((n, group, width), F32),
        ],
        compiler_params=ROOM,
    )(patch[None], grads, w_qkv)


def merge_kernel(chip_ref, stay_ref, come_ref, leave_ref, keep_ref):
    chip = chip_ref[0]
    leave_ref[...] = (stay_ref[:, 1 - chip] + come_ref[:, 1 - chip].astype(F32)).astype(BF)
    keep_ref[...] = stay_ref[:, chip] + come_ref[:, chip].astype(F32)


def merge(stay, come, chip):
    n, group, width = stay.shape
    both = pl.BlockSpec((n // 2, 2, group, width), lambda i, s: (0, 0, 0, 0))
    half = pl.BlockSpec((n // 2, group, width), lambda i, s: (0, 0, 0))
    return pl.pallas_call(
        merge_kernel,
        grid_spec=pltpu.PrefetchScalarGridSpec(
            num_scalar_prefetch=1, grid=(1,), in_specs=[both, both], out_specs=[half, half]
        ),
        out_shape=[
            jax.ShapeDtypeStruct((n // 2, group, width), BF),
            jax.ShapeDtypeStruct((n // 2, group, width), F32),
        ],
        compiler_params=ROOM,
    )(chip[None], stay.reshape(n // 2, 2, group, width), come.reshape(n // 2, 2, group, width))


def add_kernel(stay_ref, come_ref, out_ref):
    out_ref[...] = (stay_ref[...] + come_ref[...].astype(F32)).astype(BF)


def product_kernel(a_ref, own_ref, other_ref, own_core_ref, other_core_ref, out_ref, *, factor):
    n, _, group, quarter = a_ref.shape
    kinds, part, n_tok = own_ref.shape
    own_rows = out_ref.shape[1]
    left = [a_ref[:, slot].reshape(n_tok, quarter).astype(F32).T.astype(BF) for slot in range(2)]
    for r, pair in enumerate(((own_ref, other_ref), (own_core_ref, other_core_ref))):
        for c in range(kinds):
            total = lax.dot_general(left[0], pair[0][c], COLS, preferred_element_type=F32)
            total += lax.dot_general(left[1], pair[1][c], COLS, preferred_element_type=F32)
            total = total * factor
            at = (r * kinds + c) * part
            for k in range(out_ref.shape[0]):
                out_ref[k, :, at : at + part] = total[k * own_rows : (k + 1) * own_rows].astype(BF)
def product(got, grads, other, core, other_core, own_rows, factor):
    kinds, part, n_tok = grads.shape
    quarter = got.shape[-1]
    return pl.pallas_call(functools.partial(product_kernel,factor=factor),
        out_shape=jax.ShapeDtypeStruct((quarter//own_rows,own_rows,2*kinds*part),BF),compiler_params=ROOM)(got,grads,other,core,other_core)

def final_kernel(core_ref, in_ref, out_ref, *, part, kinds):
    n_pair, n_chip, own_rows, _ = in_ref.shape
    for core in range(2):
        @pl.when(core_ref[0] == core)
        def _(core=core):
            for x in range(n_chip):
                total = in_ref[0, x].astype(F32)
                for z in range(1, n_pair):
                    total = total + in_ref[z, x].astype(F32)
                for r in range(2):
                    for c in range(kinds):
                        at = (c * n_chip * 2 + 2 * x + (r ^ core)) * part
                        src = (r * kinds + c) * part
                        out_ref[:, at : at + part] = total[:, src : src + part]
def final_sum(pieces, core, part, kinds):
    n_pair,n_chip,own_rows,_=pieces.shape
    return pl.pallas_call(functools.partial(final_kernel,part=part,kinds=kinds),
        grid_spec=pltpu.PrefetchScalarGridSpec(num_scalar_prefetch=1,grid=(1,),
            in_specs=[pl.BlockSpec(pieces.shape,lambda i,s:(0,0,0,0))],
            out_specs=pl.BlockSpec((own_rows,2*n_chip*kinds*part),lambda i,s:(0,0))),
        out_shape=jax.ShapeDtypeStruct((own_rows,2*n_chip*kinds*part),F32),compiler_params=ROOM)(core[None],pieces)


def per_device(tokens, ln_gain, ln_bias, w_qkv, w_out, q_time, k_time, v_time, grad_out):
    t_dev, patches, width = tokens.shape
    frames, columns, part = q_time.shape
    n_tm = lax.axis_size("tm")
    n_patch = lax.axis_size("patch")
    n_pair = n_tm // 2
    n_chip = n_patch // 2
    devices = n_tm * n_patch
    n_tok = frames * columns
    own_rows = width // devices
    tm = lax.axis_index("tm")
    patch = lax.axis_index("patch")
    core = patch % 2
    both = ("tm", "patch")

    def swap(values, axis, size, bit):
        return lax.ppermute(values, axis, [(i, i ^ bit) for i in range(size)])

    grad_rows = grad_out.reshape(-1, width)
    d_attn = jnp.einsum(
        "to,jfo->jtf", grad_rows, w_out.reshape(n_patch, part, width), preferred_element_type=F32
    ).astype(BF)
    d_attn = d_attn.reshape(n_patch, t_dev, n_tm, columns, part).transpose(2, 0, 1, 3, 4)
    d_attn, tokens = lax.optimization_barrier((d_attn, tokens))
    d_time = lax.all_to_all(
        d_attn.reshape(devices, t_dev, columns, part), both, 0, 0, tiled=True
    ).reshape(n_tok, part)

    as_float = tokens.reshape(-1, width).astype(F32)
    centered = as_float - jnp.mean(as_float, axis=-1, keepdims=True)
    variance = jnp.mean(centered * centered, axis=-1, keepdims=True)
    inverse = lax.rsqrt(variance + 1e-06)
    normed = centered * inverse

    quarter = width // 4
    sent = norm_send(tokens.reshape(-1, width), ln_gain, ln_bias, n_pair, n_chip, columns, own_rows, t_dev)
    d_time, sent = lax.optimization_barrier((d_time, sent))
    got = lax.all_to_all(sent, both, 0, 0, tiled=True)

    saved = [values.reshape(n_tok, part) for values in (q_time, k_time, v_time)]
    grads = attend(*saved, d_time, columns)
    grads_other = swap(grads, "tm", n_tm, 1)
    leave, stay = share_send(grads, w_qkv, patch, n_patch, t_dev * columns)
    leave, stay = merge(stay, swap(leave, "patch", n_patch, 1), patch // 2)
    share = pl.pallas_call(
        add_kernel, out_shape=jax.ShapeDtypeStruct(leave.shape, BF), compiler_params=ROOM
    )(stay, swap(leave, "patch", n_patch, 2))
    grads_other, share = lax.optimization_barrier((grads_other, share))
    grads_core = swap(grads, "patch", n_patch, 1)
    grads_other_core = swap(grads_other, "patch", n_patch, 1)

    factor = 1.0 / math.sqrt(frames * patches)
    groups = [
        [(2 * z + y) * n_patch + 2 * x + c for z in range(n_pair) for x in range(n_chip)]
        for y in range(2)
        for c in range(2)
    ]
    pieces = lax.all_to_all(
        product(got, grads, grads_other, grads_core, grads_other_core, own_rows, factor),
        both,
        0,
        0,
        axis_index_groups=groups,
        tiled=True,
    )
    grad_w_qkv = final_sum(pieces.reshape(n_pair, n_chip, own_rows, 6 * part), core, part, 3)

    bits = n_tm.bit_length() - 1
    share = share.reshape((2,) * bits + (1, t_dev * columns, width))
    for n in range(bits):
        high = (tm & (1 << n)) != 0
        at = bits - 1 - n
        low_part, high_part = [lax.index_in_dim(share, i, at, keepdims=False) for i in range(2)]
        stay = jnp.where(high, high_part, low_part)
        come = swap(jnp.where(high, low_part, high_part), "tm", n_tm, 1 << n)
        share = jnp.concatenate([jnp.where(high, come, stay), jnp.where(high, stay, come)], at)
    d_norm = share
    d_norm = d_norm.reshape(n_tm, t_dev, columns, width).transpose(1, 0, 2, 3)
    d_norm = d_norm.reshape(-1, width).astype(F32)
    scaled = d_norm * ln_gain
    branch = inverse * (
        scaled
        - jnp.mean(scaled, axis=-1, keepdims=True)
        - normed * jnp.mean(scaled * normed, axis=-1, keepdims=True)
    )
    grad_x = (grad_rows.astype(F32) + branch).astype(BF).reshape(t_dev, patches, width)
    return (grad_x, grad_w_qkv)


def solution(mesh):
    return jax.shard_map(
        per_device,
        mesh=mesh,
        in_specs=(
            P(("tm", "patch"), None, None),
            P(),
            P(),
            P(),
            P(),
            P(None, "tm", "patch"),
            P(None, "tm", "patch"),
            P(None, "tm", "patch"),
            P(("tm", "patch"), None, None),
        ),
        out_specs=(P(("tm", "patch"), None, None), P(("tm", "patch"), None)),
        check_vma=False,
    )
```

```python
import functools
import math

import jax
import jax.numpy as jnp
from jax import lax
from jax.experimental import pallas as pl
from jax.experimental.pallas import tpu as pltpu
from jax.sharding import PartitionSpec as P

DH = 88
BF = jnp.bfloat16
F32 = jnp.float32
ROWS = (((0,), (0,)), ((), ()))
COLS = (((1,), (1,)), ((), ()))
CROSS = (((0,), (1,)), ((), ()))
ROOM = pltpu.CompilerParams(vmem_limit_bytes=48 * 1024 * 1024)


def attend_kernel(q_ref, k_ref, v_ref, d_ref, out_ref, *, columns):
    n_tok, width = q_ref.shape
    factor = 1.0 / math.sqrt(DH)
    source = lax.broadcasted_iota(jnp.int32, (n_tok, n_tok), 0)
    target = lax.broadcasted_iota(jnp.int32, (n_tok, n_tok), 1)
    same = ((source ^ target) & (columns - 1)) == 0
    for start in range(0, width, DH):
        lanes = slice(start, start + DH)
        query, key, value, grad = [ref[:, lanes] for ref in (q_ref, k_ref, v_ref, d_ref)]
        scores = lax.dot_general(key, query, COLS, preferred_element_type=F32) * factor
        scores = jnp.where(same, scores, -jnp.inf)
        exponent = jnp.exp(scores - jnp.max(scores, axis=0, keepdims=True))
        probability = exponent * (1.0 / jnp.sum(exponent, axis=0, keepdims=True))
        prob_grad = lax.dot_general(value, grad, COLS, preferred_element_type=F32)
        row_dot = jnp.sum(probability * prob_grad, axis=0, keepdims=True)
        score_grad = (probability * (prob_grad - row_dot) * factor).astype(BF)
        prob_low = probability.astype(BF)
        for kind, (left, right, dims) in enumerate(
            ((key, score_grad, ROWS), (query, score_grad, CROSS), (grad, prob_low, CROSS))
        ):
            total = lax.dot_general(left, right, dims, preferred_element_type=F32)
            out_ref[kind, lanes, :] = total.astype(BF)


def attend(query, key, value, grad, columns):
    n_tok, width = query.shape
    return pl.pallas_call(
        functools.partial(attend_kernel, columns=columns),
        out_shape=jax.ShapeDtypeStruct((3, width, n_tok), BF),
        compiler_params=ROOM,
    )(query, key, value, grad)


def norm_kernel(x_ref, gain_ref, bias_ref, out_ref, *, n_pair, n_chip, columns, own_rows, t_dev):
    width = x_ref.shape[1]
    rows = x_ref[...].astype(F32)
    centered = rows - jnp.mean(rows, axis=-1, keepdims=True)
    variance = jnp.mean(centered * centered, axis=-1, keepdims=True)
    norm = centered * lax.rsqrt(variance + 1e-06) * gain_ref[...] + bias_ref[...]
    patches = x_ref.shape[0] // t_dev
    for y in range(2):
        for c in range(2):
            starts = [((2 * z + y) * n_chip + x) * 2 * own_rows + c * own_rows for z in range(n_pair) for x in range(n_chip)]
            part = jnp.concatenate([norm[:, s : s + own_rows] for s in starts], axis=1)
            for z in range(n_pair):
                for slot in range(2):
                    at = (2 * z + (y ^ slot)) * columns
                    piece = jnp.concatenate([part[t * patches + at : t * patches + at + columns] for t in range(t_dev)], axis=0).astype(BF)
                    out_ref[((2 * z + y) * 2 + slot) * 2 + c] = piece
def norm_send(tokens, gain, bias, n_pair, n_chip, columns, own_rows, t_dev):
    devices = 4 * n_pair * n_chip
    return pl.pallas_call(functools.partial(norm_kernel,n_pair=n_pair,n_chip=n_chip,columns=columns,own_rows=own_rows,t_dev=t_dev),
        out_shape=jax.ShapeDtypeStruct((devices,t_dev*columns,tokens.shape[1]//4),BF),compiler_params=ROOM)(tokens,gain[None],bias[None])

def weights_kernel(where_ref, w_ref, out_ref, win_ref, sem, *, n_patch):
    kinds, width, part = out_ref.shape
    window = win_ref.shape[2]
    patch = where_ref[0]
    starts = [min(part * j // 128 * 128, width - window) for j in range(n_patch)]
    start = sum(jnp.where(patch == j, at, 0) for j, at in enumerate(starts))
    copies = [
        pltpu.make_async_copy(
            w_ref.at[:, pl.ds(pl.multiple_of(c * width + start, 128), window)], win_ref.at[c], sem.at[c]
        )
        for c in range(kinds)
    ]
    for copy in copies:
        copy.start()
    for copy in copies:
        copy.wait()
    for j in range(n_patch):

        @pl.when(patch == j)
        def _(j=j):
            before = part * j - starts[j]
            for c in range(kinds):
                out_ref[c] = win_ref[c, :, before : before + part]


def own_weights(w_qkv, patch, n_patch):
    width = w_qkv.shape[0]
    kinds, part = w_qkv.shape[1] // width, width // n_patch
    window = -(-(part + 96) // 128) * 128
    return pl.pallas_call(
        functools.partial(weights_kernel, n_patch=n_patch),
        grid_spec=pltpu.PrefetchScalarGridSpec(
            num_scalar_prefetch=1,
            grid=(1,),
            in_specs=[pl.BlockSpec(memory_space=pl.ANY)],
            out_specs=pl.BlockSpec((kinds, width, part), lambda i, s: (0, 0, 0)),
            scratch_shapes=[
                pltpu.VMEM((kinds, width, window), BF),
                pltpu.SemaphoreType.DMA((kinds,)),
            ],
        ),
        out_shape=jax.ShapeDtypeStruct((kinds, width, part), BF),
        compiler_params=ROOM,
    )(patch[None], w_qkv)


def share_kernel(where_ref, g_ref, w_ref, leave_ref, stay_ref, acc_ref):
    core = where_ref[0] % 2
    total = None
    for c in range(g_ref.shape[0]):
        one = lax.dot_general(g_ref[c], w_ref[c], CROSS, preferred_element_type=F32)
        total = one if total is None else total + one
    acc_ref[...] = total.reshape(acc_ref.shape)
    leave_ref[...] = acc_ref[:, 1 - core].astype(BF)
    stay_ref[...] = acc_ref[:, core]


def share_send(grads, weights, patch, group):
    kinds, part, n_tok = grads.shape
    width = weights.shape[1]
    n = n_tok // (2 * group)
    return pl.pallas_call(
        share_kernel,
        grid_spec=pltpu.PrefetchScalarGridSpec(
            num_scalar_prefetch=1,
            grid=(1,),
            in_specs=[
                pl.BlockSpec((kinds, part, n_tok), lambda i, s: (0, 0, 0)),
                pl.BlockSpec((kinds, width, part), lambda i, s: (0, 0, 0)),
            ],
            out_specs=[pl.BlockSpec((n, group, width), lambda i, s: (0, 0, 0))] * 2,
            scratch_shapes=[pltpu.VMEM((n, 2, group, width), F32)],
        ),
        out_shape=[
            jax.ShapeDtypeStruct((n, group, width), BF),
            jax.ShapeDtypeStruct((n, group, width), F32),
        ],
        compiler_params=ROOM,
    )(patch[None], grads, weights)


def merge_kernel(chip_ref, stay_ref, come_ref, leave_ref, keep_ref):
    chip = chip_ref[0]
    leave_ref[...] = (stay_ref[:, 1 - chip] + come_ref[:, 1 - chip].astype(F32)).astype(BF)
    keep_ref[...] = stay_ref[:, chip] + come_ref[:, chip].astype(F32)


def merge(stay, come, chip):
    n, group, width = stay.shape
    both = pl.BlockSpec((n // 2, 2, group, width), lambda i, s: (0, 0, 0, 0))
    half = pl.BlockSpec((n // 2, group, width), lambda i, s: (0, 0, 0))
    return pl.pallas_call(
        merge_kernel,
        grid_spec=pltpu.PrefetchScalarGridSpec(
            num_scalar_prefetch=1, grid=(1,), in_specs=[both, both], out_specs=[half, half]
        ),
        out_shape=[
            jax.ShapeDtypeStruct((n // 2, group, width), BF),
            jax.ShapeDtypeStruct((n // 2, group, width), F32),
        ],
        compiler_params=ROOM,
    )(chip[None], stay.reshape(n // 2, 2, group, width), come.reshape(n // 2, 2, group, width))


def add_kernel(stay_ref, come_ref, out_ref):
    out_ref[...] = (stay_ref[...] + come_ref[...].astype(F32)).astype(BF)


def product_kernel(
    chip_ref, mine_ref, theirs_ref, own_ref, other_ref, own_core_ref, other_core_ref, out_ref, *, factor
):
    kinds, part, n_tok = own_ref.shape
    own_rows = out_ref.shape[1]

    def write(norm_own, norm_other):
        for r, (own, other) in enumerate(((own_ref, other_ref), (own_core_ref, other_core_ref))):
            for c in range(kinds):
                total = jnp.dot(own[c], norm_own[...], preferred_element_type=F32)
                total += jnp.dot(other[c], norm_other[...], preferred_element_type=F32)
                total = (total * factor).T
                at = (r * kinds + c) * part
                for k in range(out_ref.shape[0]):
                    rows = total[k * own_rows : (k + 1) * own_rows]
                    out_ref[k, :, at : at + part] = rows.astype(BF)

    @pl.when(chip_ref[0] == 0)
    def _():
        write(mine_ref, theirs_ref)

    @pl.when(chip_ref[0] == 1)
    def _():
        write(theirs_ref, mine_ref)


def product(chip, mine, theirs, grads, other, core, other_core, own_rows, factor):
    kinds, part, n_tok = grads.shape
    norm = pl.BlockSpec(mine.shape, lambda i, s: (0, 0))
    whole = pl.BlockSpec(grads.shape, lambda i, s: (0, 0, 0))
    shape = (part // own_rows, own_rows, 2 * kinds * part)
    return pl.pallas_call(
        functools.partial(product_kernel, factor=factor),
        grid_spec=pltpu.PrefetchScalarGridSpec(
            num_scalar_prefetch=1,
            grid=(1,),
            in_specs=[norm, norm, whole, whole, whole, whole],
            out_specs=pl.BlockSpec(shape, lambda i, s: (0, 0, 0)),
        ),
        out_shape=jax.ShapeDtypeStruct(shape, BF),
        compiler_params=ROOM,
    )(chip[None], mine, theirs, grads, other, core, other_core)


def last_kernel(tm_ref, stay_ref, come_ref, x_ref, grad_ref, gain_ref, out_ref, *, columns, t_dev):
    n_pair, group, width = stay_ref.shape
    patches = x_ref.shape[0] // t_dev
    tm = tm_ref[0]
    first = tm % 2 == 0
    for z in range(n_pair):
        slot = (tm // 2) ^ z
        stay, come = stay_ref[slot].astype(F32), come_ref[slot].astype(F32)
        for y in range(2):
            d_norm = jnp.where(first == (y == 0), stay, come)
            for t in range(t_dev):
                at = t * patches + (2 * z + y) * columns
                rows = slice(at, at + columns)
                tokens = x_ref[rows, :].astype(F32)
                centered = tokens - jnp.mean(tokens, axis=-1, keepdims=True)
                variance = jnp.mean(centered * centered, axis=-1, keepdims=True)
                inverse = lax.rsqrt(variance + 1e-06)
                normed = centered * inverse
                scaled = d_norm[t * columns : (t + 1) * columns] * gain_ref[...]
                branch = inverse * (
                    scaled
                    - jnp.mean(scaled, axis=-1, keepdims=True)
                    - normed * jnp.mean(scaled * normed, axis=-1, keepdims=True)
                )
                out_ref[rows, :] = (grad_ref[rows, :].astype(F32) + branch).astype(BF)


def last(stay, come, tokens, grads, gain, tm, columns, t_dev):
    n_rows, width = tokens.shape
    part = pl.BlockSpec(stay.shape, lambda i, s: (0, 0, 0))
    rows = pl.BlockSpec((n_rows, width), lambda i, s: (0, 0))
    return pl.pallas_call(
        functools.partial(last_kernel, columns=columns, t_dev=t_dev),
        grid_spec=pltpu.PrefetchScalarGridSpec(
            num_scalar_prefetch=1,
            grid=(1,),
            in_specs=[part, part, rows, rows, pl.BlockSpec((1, width), lambda i, s: (0, 0))],
            out_specs=rows,
        ),
        out_shape=jax.ShapeDtypeStruct((n_rows, width), BF),
        compiler_params=ROOM,
    )(tm[None], stay, come, tokens, grads, gain[None])


def final_kernel(core_ref, in_ref, out_ref, *, part, kinds):
    n_pair, n_chip, own_rows, _ = in_ref.shape
    for core in range(2):
        @pl.when(core_ref[0] == core)
        def _(core=core):
            for x in range(n_chip):
                total = in_ref[0, x].astype(F32)
                for z in range(1, n_pair):
                    total = total + in_ref[z, x].astype(F32)
                for r in range(2):
                    for c in range(kinds):
                        at = (c * n_chip * 2 + 2 * x + (r ^ core)) * part
                        src = (r * kinds + c) * part
                        out_ref[:, at : at + part] = total[:, src : src + part]
def final_sum(pieces, core, part, kinds):
    n_pair,n_chip,own_rows,_=pieces.shape
    return pl.pallas_call(functools.partial(final_kernel,part=part,kinds=kinds),
        grid_spec=pltpu.PrefetchScalarGridSpec(num_scalar_prefetch=1,grid=(1,),
            in_specs=[pl.BlockSpec(pieces.shape,lambda i,s:(0,0,0,0))],
            out_specs=pl.BlockSpec((own_rows,2*n_chip*kinds*part),lambda i,s:(0,0))),
        out_shape=jax.ShapeDtypeStruct((own_rows,2*n_chip*kinds*part),F32),compiler_params=ROOM)(core[None],pieces)


def per_device(tokens, ln_gain, ln_bias, w_qkv, w_out, q_time, k_time, v_time, grad_out):
    t_dev, patches, width = tokens.shape
    frames, columns, part = q_time.shape
    n_tm = lax.axis_size("tm")
    n_patch = lax.axis_size("patch")
    n_pair = n_tm // 2
    n_chip = n_patch // 2
    devices = n_tm * n_patch
    n_tok = frames * columns
    own_rows = width // devices
    tm = lax.axis_index("tm")
    patch = lax.axis_index("patch")
    side = tm % 2
    core = patch % 2
    both = ("tm", "patch")

    def swap(values, axis, size, bit):
        return lax.ppermute(values, axis, [(i, i ^ bit) for i in range(size)])

    grad_rows = grad_out.reshape(-1, width)
    d_attn = jnp.einsum(
        "to,jfo->jtf", grad_rows, w_out.reshape(n_patch, part, width), preferred_element_type=F32
    ).astype(BF)
    d_attn = d_attn.reshape(n_patch, t_dev, n_tm, columns, part).transpose(2, 0, 1, 3, 4)
    d_attn, tokens = lax.optimization_barrier((d_attn, tokens))
    d_time = lax.all_to_all(
        d_attn.reshape(devices, t_dev, columns, part), both, 0, 0, tiled=True
    ).reshape(n_tok, part)

    quarter = width // 4
    sent = norm_send(tokens.reshape(-1, width), ln_gain, ln_bias, n_pair, n_chip, columns, own_rows, t_dev)
    weights = own_weights(w_qkv, patch, n_patch)
    d_time, sent, weights = lax.optimization_barrier((d_time, sent, weights))
    mine = lax.all_to_all(sent, both, 0, 0, tiled=True).reshape(n_tok, quarter)
    theirs = swap(mine, "patch", n_patch, 2)

    saved = [values.reshape(n_tok, part) for values in (q_time, k_time, v_time)]
    grads = attend(*saved, d_time, columns)
    grads_other = swap(grads, "tm", n_tm, 1)
    leave, stay = share_send(grads, weights, patch, t_dev * columns)
    leave, stay = merge(stay, swap(leave, "patch", n_patch, 1), patch // 2)
    share = pl.pallas_call(
        add_kernel, out_shape=jax.ShapeDtypeStruct(leave.shape, BF), compiler_params=ROOM
    )(stay, swap(leave, "patch", n_patch, 2))
    share = share.reshape((n_pair, 2) + share.shape[1:])
    spread = [
        swap(lax.dynamic_index_in_dim(share, (tm // 2) ^ n, 0, keepdims=False), "tm", n_tm, 2 * n)
        if n
        else lax.dynamic_index_in_dim(share, tm // 2, 0, keepdims=False)
        for n in range(n_pair)
    ]
    grads_other, spread, theirs = lax.optimization_barrier((grads_other, spread, theirs))
    grads_core = swap(grads, "patch", n_patch, 1)
    grads_other_core = swap(grads_other, "patch", n_patch, 1)

    factor = 1.0 / math.sqrt(frames * patches)
    groups = [
        [(2 * z + y) * n_patch + 2 * x + c for z in range(n_pair) for x in range(n_chip)]
        for y in range(2)
        for c in range(2)
    ]
    pieces = lax.all_to_all(
        product(
            patch // 2, mine, theirs, grads, grads_other, grads_core, grads_other_core, own_rows, factor
        ),
        both,
        0,
        0,
        axis_index_groups=groups,
        tiled=True,
    )
    grad_w_qkv = final_sum(pieces.reshape(n_pair, n_chip, own_rows, 6 * part), core, part, 3)

    spread = jnp.stack(spread)
    stay = lax.dynamic_index_in_dim(spread, side, 1, keepdims=False)
    come = swap(lax.dynamic_index_in_dim(spread, 1 - side, 1, keepdims=False), "tm", n_tm, 1)
    grad_x = last(stay, come, tokens.reshape(-1, width), grad_rows, ln_gain, tm, columns, t_dev)
    grad_x = grad_x.reshape(t_dev, patches, width)
    return (grad_x, grad_w_qkv)


def solution(mesh):
    return jax.shard_map(
        per_device,
        mesh=mesh,
        in_specs=(
            P(("tm", "patch"), None, None),
            P(),
            P(),
            P(),
            P(),
            P(None, "tm", "patch"),
            P(None, "tm", "patch"),
            P(None, "tm", "patch"),
            P(("tm", "patch"), None, None),
        ),
        out_specs=(P(("tm", "patch"), None, None), P(("tm", "patch"), None)),
        check_vma=False,
    )
```

```python
import functools
import math

import jax
import jax.numpy as jnp
from jax import lax
from jax.experimental import pallas as pl
from jax.experimental.pallas import tpu as pltpu
from jax.sharding import PartitionSpec as P

DH = 88
BF = jnp.bfloat16
F32 = jnp.float32
ROWS = (((0,), (0,)), ((), ()))
COLS = (((1,), (1,)), ((), ()))
CROSS = (((0,), (1,)), ((), ()))
ROOM = pltpu.CompilerParams(vmem_limit_bytes=48 * 1024 * 1024)


def attend_kernel(q_ref, k_ref, v_ref, d_ref, out_ref, *, columns):
    n_tok, width = q_ref.shape
    factor = 1.0 / math.sqrt(DH)
    source = lax.broadcasted_iota(jnp.int32, (n_tok, n_tok), 0)
    target = lax.broadcasted_iota(jnp.int32, (n_tok, n_tok), 1)
    same = ((source ^ target) & (columns - 1)) == 0
    for start in range(0, width, DH):
        lanes = slice(start, start + DH)
        query, key, value, grad = [ref[:, lanes] for ref in (q_ref, k_ref, v_ref, d_ref)]
        scores = lax.dot_general(key, query, COLS, preferred_element_type=F32) * factor
        scores = jnp.where(same, scores, -jnp.inf)
        exponent = jnp.exp(scores - jnp.max(scores, axis=0, keepdims=True))
        probability = exponent * (1.0 / jnp.sum(exponent, axis=0, keepdims=True))
        prob_grad = lax.dot_general(value, grad, COLS, preferred_element_type=F32)
        row_dot = jnp.sum(probability * prob_grad, axis=0, keepdims=True)
        score_grad = (probability * (prob_grad - row_dot) * factor).astype(BF)
        prob_low = probability.astype(BF)
        for kind, (left, right, dims) in enumerate(
            ((key, score_grad, ROWS), (query, score_grad, CROSS), (grad, prob_low, CROSS))
        ):
            total = lax.dot_general(left, right, dims, preferred_element_type=F32)
            out_ref[kind, lanes, :] = total.astype(BF)


def attend(query, key, value, grad, columns):
    n_tok, width = query.shape
    return pl.pallas_call(
        functools.partial(attend_kernel, columns=columns),
        out_shape=jax.ShapeDtypeStruct((3, width, n_tok), BF),
        compiler_params=ROOM,
    )(query, key, value, grad)


def first_kernel(
    gain_ref, bias_ref, x_ref, grad_ref, w_ref, out_ref, x_buf, grad_buf, w_buf, sem, *, n_pair, columns, own_rows, t_dev
):
    n_rows, width = x_buf.shape
    heads, part, _ = w_buf.shape
    patches = n_rows // t_dev
    copies = [
        pltpu.make_async_copy(x_ref, x_buf, sem.at[0]),
        pltpu.make_async_copy(grad_ref, grad_buf, sem.at[1]),
    ] + [
        pltpu.make_async_copy(w_ref.at[pl.ds(j * part, part), :], w_buf.at[j], sem.at[2 + j])
        for j in range(heads)
    ]
    for copy in copies:
        copy.start()

    def pick(values, at):
        pieces = [values[t * patches + at : t * patches + at + columns] for t in range(t_dev)]
        return jnp.concatenate(pieces, axis=0).astype(BF)

    copies[0].wait()
    rows = x_buf[...].astype(F32)
    centered = rows - jnp.mean(rows, axis=-1, keepdims=True)
    variance = jnp.mean(centered * centered, axis=-1, keepdims=True)
    norm = centered * lax.rsqrt(variance + 1e-06) * gain_ref[...] + bias_ref[...]
    for y in range(2):
        for c in range(2):
            starts = [
                (((2 * z + y) * 2 + x) * 2 + c) * own_rows for z in range(n_pair) for x in range(2)
            ]
            quarter = jnp.concatenate([norm[:, at : at + own_rows] for at in starts], axis=1)
            for z in range(n_pair):
                for x in range(2):
                    out_ref[((2 * z + y) * 2 + x) * 2 + c, 1] = pick(
                        quarter, (2 * z + (y ^ x)) * columns
                    )
    copies[1].wait()
    for j in range(heads):
        copies[2 + j].wait()
        d_attn = lax.dot_general(grad_buf[...], w_buf[j], COLS, preferred_element_type=F32)
        for tm in range(2 * n_pair):
            out_ref[tm * heads + j, 0] = pick(d_attn, tm * columns)


def first_product(tokens, gain, bias, grads, w_out, n_pair, columns, own_rows, t_dev):
    n_rows, width = tokens.shape
    heads = 4
    part = width // heads
    line = pl.BlockSpec((1, width), lambda i: (0, 0))
    shape = (2 * heads * n_pair, 2, t_dev * columns, part)
    return pl.pallas_call(
        functools.partial(
            first_kernel, n_pair=n_pair, columns=columns, own_rows=own_rows, t_dev=t_dev
        ),
        grid=(1,),
        in_specs=[line, line] + [pl.BlockSpec(memory_space=pl.ANY)] * 3,
        out_specs=pl.BlockSpec(shape, lambda i: (0, 0, 0, 0)),
        out_shape=jax.ShapeDtypeStruct(shape, BF),
        scratch_shapes=[
            pltpu.VMEM((n_rows, width), BF),
            pltpu.VMEM((n_rows, width), BF),
            pltpu.VMEM((heads, part, width), BF),
            pltpu.SemaphoreType.DMA((2 + heads,)),
        ],
        compiler_params=ROOM,
    )(gain[None], bias[None], tokens, grads, w_out)


def weights_kernel(chip_ref, w_ref, out_ref, win_ref, sem, *, n_chip):
    kinds, width, part = out_ref.shape
    window = win_ref.shape[2]
    chip = chip_ref[0]
    starts = [min(part * j // 128 * 128, width - window) for j in range(n_chip)]
    start = sum(jnp.where(chip == j, at, 0) for j, at in enumerate(starts))
    copies = [
        pltpu.make_async_copy(
            w_ref.at[:, pl.ds(pl.multiple_of(c * width + start, 128), window)], win_ref.at[c], sem.at[c]
        )
        for c in range(kinds)
    ]
    for copy in copies:
        copy.start()
    for copy in copies:
        copy.wait()
    for j in range(n_chip):

        @pl.when(chip == j)
        def _(j=j):
            before = part * j - starts[j]
            for c in range(kinds):
                out_ref[c] = win_ref[c, :, before : before + part]


def own_weights(w_qkv, chip, n_chip):
    width = w_qkv.shape[0]
    kinds, part = w_qkv.shape[1] // width, width // n_chip
    window = -(-(part + 64) // 128) * 128
    return pl.pallas_call(
        functools.partial(weights_kernel, n_chip=n_chip),
        grid_spec=pltpu.PrefetchScalarGridSpec(
            num_scalar_prefetch=1,
            grid=(1,),
            in_specs=[pl.BlockSpec(memory_space=pl.ANY)],
            out_specs=pl.BlockSpec((kinds, width, part), lambda i, s: (0, 0, 0)),
            scratch_shapes=[
                pltpu.VMEM((kinds, width, window), BF),
                pltpu.SemaphoreType.DMA((kinds,)),
            ],
        ),
        out_shape=jax.ShapeDtypeStruct((kinds, width, part), BF),
        compiler_params=ROOM,
    )(chip[None], w_qkv)


def share_kernel(where_ref, own_ref, core_ref, w_ref, leave_ref, stay_ref, turn_ref):
    patch = where_ref[0]
    chip, core = patch // 2, patch % 2
    kinds, part, _ = own_ref.shape
    n, group, _ = leave_ref.shape
    for side in range(2):

        @pl.when(core == side)
        def _(side=side):
            for c in range(kinds):
                for grads_ref, at in ((own_ref, side * part), (core_ref, (1 - side) * part)):
                    rows = grads_ref[c].astype(F32).T.astype(BF)
                    turn_ref[c, :, :, :, :, at : at + part] = rows.reshape(n, 2, 2, group, part)

    total = None
    for c in range(kinds):
        rows = jnp.concatenate(
            [turn_ref[c, :, which, core].reshape(n * group, 2 * part) for which in (1 - chip, chip)],
            axis=0,
        )
        one = lax.dot_general(rows, w_ref[c], COLS, preferred_element_type=F32)
        total = one if total is None else total + one
    leave_ref[...] = total[: n * group].reshape(leave_ref.shape).astype(BF)
    stay_ref[...] = total[n * group :].reshape(stay_ref.shape)


def share_send(grads, grads_core, weights, patch, group):
    kinds, part, n_tok = grads.shape
    width = weights.shape[1]
    n = n_tok // (4 * group)
    whole = pl.BlockSpec((kinds, part, n_tok), lambda i, s: (0, 0, 0))
    return pl.pallas_call(
        share_kernel,
        grid_spec=pltpu.PrefetchScalarGridSpec(
            num_scalar_prefetch=1,
            grid=(1,),
            in_specs=[whole, whole, pl.BlockSpec((kinds, width, 2 * part), lambda i, s: (0, 0, 0))],
            out_specs=[pl.BlockSpec((n, group, width), lambda i, s: (0, 0, 0))] * 2,
            scratch_shapes=[pltpu.VMEM((kinds, n, 2, 2, group, 2 * part), BF)],
        ),
        out_shape=[
            jax.ShapeDtypeStruct((n, group, width), BF),
            jax.ShapeDtypeStruct((n, group, width), F32),
        ],
        compiler_params=ROOM,
    )(patch[None], grads, grads_core, weights)


def add_kernel(stay_ref, come_ref, out_ref):
    out_ref[...] = (stay_ref[...] + come_ref[...].astype(F32)).astype(BF)


def product_kernel(
    chip_ref, mine_ref, theirs_ref, own_ref, other_ref, own_core_ref, other_core_ref, out_ref, *, factor
):
    kinds, part, n_tok = own_ref.shape
    own_rows = out_ref.shape[1]

    def write(norm_own, norm_other):
        for r, (own, other) in enumerate(((own_ref, other_ref), (own_core_ref, other_core_ref))):
            for c in range(kinds):
                total = jnp.dot(own[c], norm_own[...], preferred_element_type=F32)
                total += jnp.dot(other[c], norm_other[...], preferred_element_type=F32)
                total = (total * factor).T
                at = (r * kinds + c) * part
                for k in range(out_ref.shape[0]):
                    rows = total[k * own_rows : (k + 1) * own_rows]
                    out_ref[k, :, at : at + part] = rows.astype(BF)

    @pl.when(chip_ref[0] == 0)
    def _():
        write(mine_ref, theirs_ref)

    @pl.when(chip_ref[0] == 1)
    def _():
        write(theirs_ref, mine_ref)


def product(chip, mine, theirs, grads, other, core, other_core, own_rows, factor):
    kinds, part, n_tok = grads.shape
    norm = pl.BlockSpec(mine.shape, lambda i, s: (0, 0))
    whole = pl.BlockSpec(grads.shape, lambda i, s: (0, 0, 0))
    shape = (part // own_rows, own_rows, 2 * kinds * part)
    return pl.pallas_call(
        functools.partial(product_kernel, factor=factor),
        grid_spec=pltpu.PrefetchScalarGridSpec(
            num_scalar_prefetch=1,
            grid=(1,),
            in_specs=[norm, norm, whole, whole, whole, whole],
            out_specs=pl.BlockSpec(shape, lambda i, s: (0, 0, 0)),
        ),
        out_shape=jax.ShapeDtypeStruct(shape, BF),
        compiler_params=ROOM,
    )(chip[None], mine, theirs, grads, other, core, other_core)


def last_kernel(tm_ref, stay_ref, come_ref, x_ref, grad_ref, gain_ref, out_ref, *, columns, t_dev):
    n_pair, group, width = stay_ref.shape
    patches = x_ref.shape[0] // t_dev
    tm = tm_ref[0]
    first = tm % 2 == 0
    for z in range(n_pair):
        slot = (tm // 2) ^ z
        stay, come = stay_ref[slot].astype(F32), come_ref[slot].astype(F32)
        for y in range(2):
            d_norm = jnp.where(first == (y == 0), stay, come)
            for t in range(t_dev):
                at = t * patches + (2 * z + y) * columns
                rows = slice(at, at + columns)
                tokens = x_ref[rows, :].astype(F32)
                centered = tokens - jnp.mean(tokens, axis=-1, keepdims=True)
                variance = jnp.mean(centered * centered, axis=-1, keepdims=True)
                inverse = lax.rsqrt(variance + 1e-06)
                normed = centered * inverse
                scaled = d_norm[t * columns : (t + 1) * columns] * gain_ref[...]
                branch = inverse * (
                    scaled
                    - jnp.mean(scaled, axis=-1, keepdims=True)
                    - normed * jnp.mean(scaled * normed, axis=-1, keepdims=True)
                )
                out_ref[rows, :] = (grad_ref[rows, :].astype(F32) + branch).astype(BF)


def last(stay, come, tokens, grads, gain, tm, columns, t_dev):
    n_rows, width = tokens.shape
    part = pl.BlockSpec(stay.shape, lambda i, s: (0, 0, 0))
    rows = pl.BlockSpec((n_rows, width), lambda i, s: (0, 0))
    return pl.pallas_call(
        functools.partial(last_kernel, columns=columns, t_dev=t_dev),
        grid_spec=pltpu.PrefetchScalarGridSpec(
            num_scalar_prefetch=1,
            grid=(1,),
            in_specs=[part, part, rows, rows, pl.BlockSpec((1, width), lambda i, s: (0, 0))],
            out_specs=rows,
        ),
        out_shape=jax.ShapeDtypeStruct((n_rows, width), BF),
        compiler_params=ROOM,
    )(tm[None], stay, come, tokens, grads, gain[None])


def final_kernel(core_ref, in_ref, out_ref, *, part, kinds):
    n_pair, n_chip, own_rows, _ = in_ref.shape
    for core in range(2):
        @pl.when(core_ref[0] == core)
        def _(core=core):
            for x in range(n_chip):
                total = in_ref[0, x].astype(F32)
                for z in range(1, n_pair):
                    total = total + in_ref[z, x].astype(F32)
                for r in range(2):
                    for c in range(kinds):
                        at = (c * n_chip * 2 + 2 * x + (r ^ core)) * part
                        src = (r * kinds + c) * part
                        out_ref[:, at : at + part] = total[:, src : src + part]
def final_sum(pieces, core, part, kinds):
    n_pair,n_chip,own_rows,_=pieces.shape
    return pl.pallas_call(functools.partial(final_kernel,part=part,kinds=kinds),
        grid_spec=pltpu.PrefetchScalarGridSpec(num_scalar_prefetch=1,grid=(1,),
            in_specs=[pl.BlockSpec(pieces.shape,lambda i,s:(0,0,0,0))],
            out_specs=pl.BlockSpec((own_rows,2*n_chip*kinds*part),lambda i,s:(0,0))),
        out_shape=jax.ShapeDtypeStruct((own_rows,2*n_chip*kinds*part),F32),compiler_params=ROOM)(core[None],pieces)


def per_device(tokens, ln_gain, ln_bias, w_qkv, w_out, q_time, k_time, v_time, grad_out):
    t_dev, patches, width = tokens.shape
    frames, columns, part = q_time.shape
    n_tm = lax.axis_size("tm")
    n_patch = lax.axis_size("patch")
    n_pair = n_tm // 2
    n_chip = n_patch // 2
    devices = n_tm * n_patch
    n_tok = frames * columns
    own_rows = width // devices
    tm = lax.axis_index("tm")
    patch = lax.axis_index("patch")
    side = tm % 2
    core = patch % 2
    both = ("tm", "patch")

    def swap(values, axis, size, bit):
        return lax.ppermute(values, axis, [(i, i ^ bit) for i in range(size)])

    grad_rows = grad_out.reshape(-1, width)
    sent = first_product(
        tokens.reshape(-1, width), ln_gain, ln_bias, grad_rows, w_out, n_pair, columns, own_rows, t_dev
    )
    got = lax.all_to_all(sent, both, 0, 0, tiled=True)
    sent, w_late = lax.optimization_barrier((sent, w_qkv))
    weights = own_weights(w_late, patch // 2, n_chip)
    got, weights = lax.optimization_barrier((got, weights))
    d_time = got[:, 0].reshape(n_tok, part)
    mine = got[:, 1].reshape(n_tok, part)
    theirs = swap(mine, "patch", n_patch, 2)

    saved = [values.reshape(n_tok, part) for values in (q_time, k_time, v_time)]
    grads = attend(*saved, d_time, columns)
    grads_other = swap(grads, "tm", n_tm, 1)
    grads_core = swap(grads, "patch", n_patch, 1)

    leave, stay = share_send(grads, grads_core, weights, patch, t_dev * columns)
    share = pl.pallas_call(
        add_kernel, out_shape=jax.ShapeDtypeStruct(leave.shape, BF), compiler_params=ROOM
    )(stay, swap(leave, "patch", n_patch, 2))
    share = share.reshape((n_pair, 2) + share.shape[1:])
    spread = [lax.dynamic_index_in_dim(share, (tm // 2) ^ n, 0, keepdims=False) for n in range(n_pair)]
    spread = spread[:1] + [swap(spread[n], "tm", n_tm, 2 * n) for n in range(1, n_pair)]
    grads_other, theirs, spread = lax.optimization_barrier((grads_other, theirs, spread))
    grads_other_core = swap(grads_other, "patch", n_patch, 1)

    factor = 1.0 / math.sqrt(frames * patches)
    groups = [
        [(2 * z + y) * n_patch + 2 * x + c for z in range(n_pair) for x in range(n_chip)]
        for y in range(2)
        for c in range(2)
    ]
    partial = product(
        patch // 2, mine, theirs, grads, grads_other, grads_core, grads_other_core, own_rows, factor
    )
    partial, spread = lax.optimization_barrier((partial, spread))
    pieces = lax.all_to_all(partial, both, 0, 0, axis_index_groups=groups, tiled=True)
    grad_w_qkv = final_sum(pieces.reshape(n_pair, n_chip, own_rows, 6 * part), core, part, 3)

    spread = jnp.stack(spread)
    stay = lax.dynamic_index_in_dim(spread, side, 1, keepdims=False)
    come = swap(lax.dynamic_index_in_dim(spread, 1 - side, 1, keepdims=False), "tm", n_tm, 1)
    grad_x = last(stay, come, tokens.reshape(-1, width), grad_rows, ln_gain, tm, columns, t_dev)
    grad_x = grad_x.reshape(t_dev, patches, width)
    return (grad_x, grad_w_qkv)


def solution(mesh):
    return jax.shard_map(
        per_device,
        mesh=mesh,
        in_specs=(
            P(("tm", "patch"), None, None),
            P(),
            P(),
            P(),
            P(),
            P(None, "tm", "patch"),
            P(None, "tm", "patch"),
            P(None, "tm", "patch"),
            P(("tm", "patch"), None, None),
        ),
        out_specs=(P(("tm", "patch"), None, None), P(("tm", "patch"), None)),
        check_vma=False,
    )
```

```python
import functools
import math

import jax
import jax.numpy as jnp
from jax import lax
from jax.experimental import pallas as pl
from jax.experimental.pallas import tpu as pltpu
from jax.sharding import PartitionSpec as P

DH = 88
BF = jnp.bfloat16
F32 = jnp.float32
ROWS = (((0,), (0,)), ((), ()))
COLS = (((1,), (1,)), ((), ()))
CROSS = (((0,), (1,)), ((), ()))
ROOM = pltpu.CompilerParams(vmem_limit_bytes=48 * 1024 * 1024)


def attend_kernel(q_ref, k_ref, v_ref, d_ref, out_ref, *, columns):
    n_tok, width = q_ref.shape
    factor = 1.0 / math.sqrt(DH)
    source = lax.broadcasted_iota(jnp.int32, (n_tok, n_tok), 0)
    target = lax.broadcasted_iota(jnp.int32, (n_tok, n_tok), 1)
    same = ((source ^ target) & (columns - 1)) == 0
    for start in range(0, width, DH):
        lanes = slice(start, start + DH)
        query, key, value, grad = [ref[:, lanes] for ref in (q_ref, k_ref, v_ref, d_ref)]
        scores = lax.dot_general(key, query, COLS, preferred_element_type=F32) * factor
        scores = jnp.where(same, scores, -jnp.inf)
        exponent = jnp.exp(scores - jnp.max(scores, axis=0, keepdims=True))
        probability = exponent * (1.0 / jnp.sum(exponent, axis=0, keepdims=True))
        prob_grad = lax.dot_general(value, grad, COLS, preferred_element_type=F32)
        row_dot = jnp.sum(probability * prob_grad, axis=0, keepdims=True)
        score_grad = (probability * (prob_grad - row_dot) * factor).astype(BF)
        prob_low = probability.astype(BF)
        for kind, (left, right, dims) in enumerate(
            ((key, score_grad, ROWS), (query, score_grad, CROSS), (grad, prob_low, CROSS))
        ):
            total = lax.dot_general(left, right, dims, preferred_element_type=F32)
            out_ref[kind, lanes, :] = total.astype(BF)


def attend(query, key, value, grad, columns):
    n_tok, width = query.shape
    return pl.pallas_call(
        functools.partial(attend_kernel, columns=columns),
        out_shape=jax.ShapeDtypeStruct((3, width, n_tok), BF),
        compiler_params=ROOM,
    )(query, key, value, grad)


def norm_kernel(x_ref, gain_ref, bias_ref, out_ref, *, n_pair, n_chip, columns, own_rows, t_dev):
    width = x_ref.shape[1]
    rows = x_ref[...].astype(F32)
    centered = rows - jnp.mean(rows, axis=-1, keepdims=True)
    variance = jnp.mean(centered * centered, axis=-1, keepdims=True)
    norm = centered * lax.rsqrt(variance + 1e-06) * gain_ref[...] + bias_ref[...]
    patches = x_ref.shape[0] // t_dev
    for y in range(2):
        for c in range(2):
            starts = [((2 * z + y) * n_chip + x) * 2 * own_rows + c * own_rows for z in range(n_pair) for x in range(n_chip)]
            part = jnp.concatenate([norm[:, s : s + own_rows] for s in starts], axis=1)
            for z in range(n_pair):
                for slot in range(2):
                    at = (2 * z + (y ^ slot)) * columns
                    piece = jnp.concatenate([part[t * patches + at : t * patches + at + columns] for t in range(t_dev)], axis=0).astype(BF)
                    out_ref[((2 * z + y) * 2 + slot) * 2 + c] = piece
def norm_send(tokens, gain, bias, n_pair, n_chip, columns, own_rows, t_dev):
    devices = 4 * n_pair * n_chip
    return pl.pallas_call(functools.partial(norm_kernel,n_pair=n_pair,n_chip=n_chip,columns=columns,own_rows=own_rows,t_dev=t_dev),
        out_shape=jax.ShapeDtypeStruct((devices,t_dev*columns,tokens.shape[1]//4),BF),compiler_params=ROOM)(tokens,gain[None],bias[None])

def weights_kernel(chip_ref, w_ref, out_ref, win_ref, sem, *, n_chip):
    kinds, width, part = out_ref.shape
    window = win_ref.shape[2]
    chip = chip_ref[0]
    starts = [min(part * j // 128 * 128, width - window) for j in range(n_chip)]
    start = sum(jnp.where(chip == j, at, 0) for j, at in enumerate(starts))
    copies = [
        pltpu.make_async_copy(
            w_ref.at[:, pl.ds(pl.multiple_of(c * width + start, 128), window)], win_ref.at[c], sem.at[c]
        )
        for c in range(kinds)
    ]
    for copy in copies:
        copy.start()
    for copy in copies:
        copy.wait()
    for j in range(n_chip):

        @pl.when(chip == j)
        def _(j=j):
            before = part * j - starts[j]
            for c in range(kinds):
                out_ref[c] = win_ref[c, :, before : before + part]


def own_weights(w_qkv, chip, n_chip):
    width = w_qkv.shape[0]
    kinds, part = w_qkv.shape[1] // width, width // n_chip
    window = -(-(part + 64) // 128) * 128
    return pl.pallas_call(
        functools.partial(weights_kernel, n_chip=n_chip),
        grid_spec=pltpu.PrefetchScalarGridSpec(
            num_scalar_prefetch=1,
            grid=(1,),
            in_specs=[pl.BlockSpec(memory_space=pl.ANY)],
            out_specs=pl.BlockSpec((kinds, width, part), lambda i, s: (0, 0, 0)),
            scratch_shapes=[
                pltpu.VMEM((kinds, width, window), BF),
                pltpu.SemaphoreType.DMA((kinds,)),
            ],
        ),
        out_shape=jax.ShapeDtypeStruct((kinds, width, part), BF),
        compiler_params=ROOM,
    )(chip[None], w_qkv)


def share_kernel(where_ref, own_ref, core_ref, w_ref, leave_ref, stay_ref, turn_ref):
    patch = where_ref[0]
    chip, core = patch // 2, patch % 2
    kinds, part, _ = own_ref.shape
    n, group, _ = leave_ref.shape
    for side in range(2):

        @pl.when(core == side)
        def _(side=side):
            for c in range(kinds):
                for grads_ref, at in ((own_ref, side * part), (core_ref, (1 - side) * part)):
                    rows = grads_ref[c].astype(F32).T.astype(BF)
                    turn_ref[c, :, :, :, :, at : at + part] = rows.reshape(n, 2, 2, group, part)

    total = None
    for c in range(kinds):
        rows = jnp.concatenate(
            [turn_ref[c, :, which, core].reshape(n * group, 2 * part) for which in (1 - chip, chip)],
            axis=0,
        )
        one = lax.dot_general(rows, w_ref[c], COLS, preferred_element_type=F32)
        total = one if total is None else total + one
    leave_ref[...] = total[: n * group].reshape(leave_ref.shape).astype(BF)
    stay_ref[...] = total[n * group :].reshape(stay_ref.shape)


def share_send(grads, grads_core, weights, patch, group):
    kinds, part, n_tok = grads.shape
    width = weights.shape[1]
    n = n_tok // (4 * group)
    whole = pl.BlockSpec((kinds, part, n_tok), lambda i, s: (0, 0, 0))
    return pl.pallas_call(
        share_kernel,
        grid_spec=pltpu.PrefetchScalarGridSpec(
            num_scalar_prefetch=1,
            grid=(1,),
            in_specs=[whole, whole, pl.BlockSpec((kinds, width, 2 * part), lambda i, s: (0, 0, 0))],
            out_specs=[pl.BlockSpec((n, group, width), lambda i, s: (0, 0, 0))] * 2,
            scratch_shapes=[pltpu.VMEM((kinds, n, 2, 2, group, 2 * part), BF)],
        ),
        out_shape=[
            jax.ShapeDtypeStruct((n, group, width), BF),
            jax.ShapeDtypeStruct((n, group, width), F32),
        ],
        compiler_params=ROOM,
    )(patch[None], grads, grads_core, weights)


def add_kernel(stay_ref, come_ref, out_ref):
    out_ref[...] = (stay_ref[...] + come_ref[...].astype(F32)).astype(BF)


def product_kernel(
    chip_ref, mine_ref, theirs_ref, own_ref, core_ref, a_ref, b_ref, a_core_ref, b_core_ref, out_ref, *, factor
):
    kinds, part, _ = own_ref.shape
    own_rows = out_ref.shape[1]
    first = chip_ref[0] == 0
    mine, theirs = mine_ref[...], theirs_ref[...]
    norm_own = jnp.where(first, mine, theirs)
    norm_other = jnp.where(first, theirs, mine)
    for r, (own, other) in enumerate(
        ((own_ref, (a_ref, b_ref)), (core_ref, (a_core_ref, b_core_ref)))
    ):
        for c in range(kinds):
            second = other[0][c] if c < other[0].shape[0] else other[1][c - other[0].shape[0]]
            total = jnp.dot(own[c], norm_own, preferred_element_type=F32)
            total += jnp.dot(second, norm_other, preferred_element_type=F32)
            total = (total * factor).T
            at = (r * kinds + c) * part
            for k in range(out_ref.shape[0]):
                rows = total[k * own_rows : (k + 1) * own_rows]
                out_ref[k, :, at : at + part] = rows.astype(BF)


def product(chip, mine, theirs, grads, core, others, own_rows, factor):
    kinds, part, n_tok = grads.shape
    arrays = [mine, theirs, grads, core, *others]
    shape = (part // own_rows, own_rows, 2 * kinds * part)
    return pl.pallas_call(
        functools.partial(product_kernel, factor=factor),
        grid_spec=pltpu.PrefetchScalarGridSpec(
            num_scalar_prefetch=1,
            grid=(1,),
            in_specs=[
                pl.BlockSpec(array.shape, lambda i, s, n=array.ndim: (0,) * n) for array in arrays
            ],
            out_specs=pl.BlockSpec(shape, lambda i, s: (0, 0, 0)),
        ),
        out_shape=jax.ShapeDtypeStruct(shape, BF),
        compiler_params=ROOM,
    )(chip[None], *arrays)


def last_kernel(tm_ref, stay_ref, come_ref, x_ref, grad_ref, gain_ref, out_ref, *, columns, t_dev):
    n_pair, group, width = stay_ref.shape
    patches = x_ref.shape[0] // t_dev
    tm = tm_ref[0]
    first = tm % 2 == 0
    for z in range(n_pair):
        slot = (tm // 2) ^ z
        stay, come = stay_ref[slot].astype(F32), come_ref[slot].astype(F32)
        for y in range(2):
            d_norm = jnp.where(first == (y == 0), stay, come)
            for t in range(t_dev):
                at = t * patches + (2 * z + y) * columns
                rows = slice(at, at + columns)
                tokens = x_ref[rows, :].astype(F32)
                centered = tokens - jnp.mean(tokens, axis=-1, keepdims=True)
                variance = jnp.mean(centered * centered, axis=-1, keepdims=True)
                inverse = lax.rsqrt(variance + 1e-06)
                normed = centered * inverse
                scaled = d_norm[t * columns : (t + 1) * columns] * gain_ref[...]
                branch = inverse * (
                    scaled
                    - jnp.mean(scaled, axis=-1, keepdims=True)
                    - normed * jnp.mean(scaled * normed, axis=-1, keepdims=True)
                )
                out_ref[rows, :] = (grad_ref[rows, :].astype(F32) + branch).astype(BF)


def last(stay, come, tokens, grads, gain, tm, columns, t_dev):
    n_rows, width = tokens.shape
    part = pl.BlockSpec(stay.shape, lambda i, s: (0, 0, 0))
    rows = pl.BlockSpec((n_rows, width), lambda i, s: (0, 0))
    return pl.pallas_call(
        functools.partial(last_kernel, columns=columns, t_dev=t_dev),
        grid_spec=pltpu.PrefetchScalarGridSpec(
            num_scalar_prefetch=1,
            grid=(1,),
            in_specs=[part, part, rows, rows, pl.BlockSpec((1, width), lambda i, s: (0, 0))],
            out_specs=rows,
        ),
        out_shape=jax.ShapeDtypeStruct((n_rows, width), BF),
        compiler_params=ROOM,
    )(tm[None], stay, come, tokens, grads, gain[None])


def final_kernel(core_ref, in_ref, out_ref, *, part, kinds):
    n_pair, n_chip, own_rows, _ = in_ref.shape
    for core in range(2):
        @pl.when(core_ref[0] == core)
        def _(core=core):
            for x in range(n_chip):
                total = in_ref[0, x].astype(F32)
                for z in range(1, n_pair):
                    total = total + in_ref[z, x].astype(F32)
                for r in range(2):
                    for c in range(kinds):
                        at = (c * n_chip * 2 + 2 * x + (r ^ core)) * part
                        src = (r * kinds + c) * part
                        out_ref[:, at : at + part] = total[:, src : src + part]
def final_sum(pieces, core, part, kinds):
    n_pair,n_chip,own_rows,_=pieces.shape
    return pl.pallas_call(functools.partial(final_kernel,part=part,kinds=kinds),
        grid_spec=pltpu.PrefetchScalarGridSpec(num_scalar_prefetch=1,grid=(1,),
            in_specs=[pl.BlockSpec(pieces.shape,lambda i,s:(0,0,0,0))],
            out_specs=pl.BlockSpec((own_rows,2*n_chip*kinds*part),lambda i,s:(0,0))),
        out_shape=jax.ShapeDtypeStruct((own_rows,2*n_chip*kinds*part),F32),compiler_params=ROOM)(core[None],pieces)


def per_device(tokens, ln_gain, ln_bias, w_qkv, w_out, q_time, k_time, v_time, grad_out):
    t_dev, patches, width = tokens.shape
    frames, columns, part = q_time.shape
    n_tm = lax.axis_size("tm")
    n_patch = lax.axis_size("patch")
    n_pair = n_tm // 2
    n_chip = n_patch // 2
    devices = n_tm * n_patch
    n_tok = frames * columns
    own_rows = width // devices
    tm = lax.axis_index("tm")
    patch = lax.axis_index("patch")
    side = tm % 2
    core = patch % 2
    both = ("tm", "patch")

    def swap(values, axis, size, bit):
        return lax.ppermute(values, axis, [(i, i ^ bit) for i in range(size)])

    grad_rows = grad_out.reshape(-1, width)
    d_attn = jnp.einsum(
        "to,jfo->jtf", grad_rows, w_out.reshape(n_patch, part, width), preferred_element_type=F32
    ).astype(BF)
    d_attn = d_attn.reshape(n_patch, t_dev, n_tm, columns, part).transpose(2, 0, 1, 3, 4)
    d_attn, token_rows, w_late = lax.optimization_barrier((d_attn, tokens.reshape(-1, width), w_qkv))
    d_time = lax.all_to_all(
        d_attn.reshape(devices, t_dev, columns, part), both, 0, 0, tiled=True
    ).reshape(n_tok, part)

    sent = norm_send(token_rows, ln_gain, ln_bias, n_pair, n_chip, columns, own_rows, t_dev)
    weights = own_weights(w_late, patch // 2, n_chip)
    d_time, sent, weights = lax.optimization_barrier((d_time, sent, weights))
    mine = lax.all_to_all(sent, both, 0, 0, tiled=True).reshape(n_tok, width // 4)
    theirs = swap(mine, "patch", n_patch, 2)

    saved = [values.reshape(n_tok, part) for values in (q_time, k_time, v_time)]
    grads = attend(*saved, d_time, columns)
    grads_core = swap(grads, "patch", n_patch, 1)
    grads, grads_core = lax.optimization_barrier((grads, grads_core))
    grads_other = [swap(piece, "tm", n_tm, 1) for piece in (grads[:1], grads[1:])]

    leave, stay = share_send(grads, grads_core, weights, patch, t_dev * columns)
    share = pl.pallas_call(
        add_kernel, out_shape=jax.ShapeDtypeStruct(leave.shape, BF), compiler_params=ROOM
    )(stay, swap(leave, "patch", n_patch, 2))
    share = share.reshape((n_pair, 2) + share.shape[1:])
    spread = [lax.dynamic_index_in_dim(share, (tm // 2) ^ n, 0, keepdims=False) for n in range(n_pair)]
    spread = spread[:1] + [swap(spread[n], "tm", n_tm, 2 * n) for n in range(1, n_pair)]
    grads_other, theirs, spread = lax.optimization_barrier((grads_other, theirs, spread))
    grads_other += [swap(piece, "patch", n_patch, 1) for piece in grads_other]

    factor = 1.0 / math.sqrt(frames * patches)
    groups = [
        [(2 * z + y) * n_patch + 2 * x + c for z in range(n_pair) for x in range(n_chip)]
        for y in range(2)
        for c in range(2)
    ]
    partial = product(
        patch // 2, mine, theirs, grads, grads_core, grads_other, own_rows, factor
    )
    partial, spread = lax.optimization_barrier((partial, spread))
    pieces = lax.all_to_all(partial, both, 0, 0, axis_index_groups=groups, tiled=True)
    grad_w_qkv = final_sum(pieces.reshape(n_pair, n_chip, own_rows, 6 * part), core, part, 3)

    spread = jnp.stack(spread)
    stay = lax.dynamic_index_in_dim(spread, side, 1, keepdims=False)
    come = swap(lax.dynamic_index_in_dim(spread, 1 - side, 1, keepdims=False), "tm", n_tm, 1)
    grad_x = last(stay, come, tokens.reshape(-1, width), grad_rows, ln_gain, tm, columns, t_dev)
    grad_x = grad_x.reshape(t_dev, patches, width)
    return (grad_x, grad_w_qkv)


def solution(mesh):
    return jax.shard_map(
        per_device,
        mesh=mesh,
        in_specs=(
            P(("tm", "patch"), None, None),
            P(),
            P(),
            P(),
            P(),
            P(None, "tm", "patch"),
            P(None, "tm", "patch"),
            P(None, "tm", "patch"),
            P(("tm", "patch"), None, None),
        ),
        out_specs=(P(("tm", "patch"), None, None), P(("tm", "patch"), None)),
        check_vma=False,
    )
```

```python
import functools
import math

import jax
import jax.numpy as jnp
from jax import lax
from jax.experimental import pallas as pl
from jax.experimental.pallas import tpu as pltpu
from jax.sharding import PartitionSpec as P

DH = 88
BF = jnp.bfloat16
F32 = jnp.float32
ROWS = (((0,), (0,)), ((), ()))
COLS = (((1,), (1,)), ((), ()))
CROSS = (((0,), (1,)), ((), ()))
ROOM = pltpu.CompilerParams(vmem_limit_bytes=28 * 1024 * 1024)


def attend_kernel(q_ref, k_ref, v_ref, d_ref, all_ref, query_ref, rest_ref, *, columns):
    n_tok, width = q_ref.shape
    factor = 1.0 / math.sqrt(DH)
    source = lax.broadcasted_iota(jnp.int32, (n_tok, n_tok), 0)
    target = lax.broadcasted_iota(jnp.int32, (n_tok, n_tok), 1)
    same = ((source ^ target) & (columns - 1)) == 0
    for start in range(0, width, DH):
        lanes = slice(start, start + DH)
        query, key, value, grad = [ref[:, lanes] for ref in (q_ref, k_ref, v_ref, d_ref)]
        scores = lax.dot_general(key, query, COLS, preferred_element_type=F32) * factor
        scores = jnp.where(same, scores, -jnp.inf)
        exponent = jnp.exp(scores - jnp.max(scores, axis=0, keepdims=True))
        probability = exponent * (1.0 / jnp.sum(exponent, axis=0, keepdims=True))
        prob_grad = lax.dot_general(value, grad, COLS, preferred_element_type=F32)
        row_dot = jnp.sum(probability * prob_grad, axis=0, keepdims=True)
        score_grad = (probability * (prob_grad - row_dot) * factor).astype(BF)
        prob_low = probability.astype(BF)
        for kind, (left, right, dims, out_ref) in enumerate(
            (
                (key, score_grad, ROWS, query_ref.at[0]),
                (query, score_grad, CROSS, rest_ref.at[0]),
                (grad, prob_low, CROSS, rest_ref.at[1]),
            )
        ):
            total = lax.dot_general(left, right, dims, preferred_element_type=F32).astype(BF)
            out_ref[lanes, :] = total
            all_ref[kind, lanes, :] = total


def attend(query, key, value, grad, columns):
    n_tok, width = query.shape
    return pl.pallas_call(
        functools.partial(attend_kernel, columns=columns),
        out_shape=[jax.ShapeDtypeStruct((kinds, width, n_tok), BF) for kinds in (3, 1, 2)],
        compiler_params=ROOM,
    )(query, key, value, grad)


def norm_kernel(x_ref, gain_ref, bias_ref, out_ref, *, n_pair, n_chip, columns, own_rows, t_dev):
    width = x_ref.shape[1]
    rows = x_ref[...].astype(F32)
    centered = rows - jnp.mean(rows, axis=-1, keepdims=True)
    variance = jnp.mean(centered * centered, axis=-1, keepdims=True)
    norm = centered * lax.rsqrt(variance + 1e-06) * gain_ref[...] + bias_ref[...]
    patches = x_ref.shape[0] // t_dev
    for y in range(2):
        for c in range(2):
            starts = [((2 * z + y) * n_chip + x) * 2 * own_rows + c * own_rows for z in range(n_pair) for x in range(n_chip)]
            part = jnp.concatenate([norm[:, s : s + own_rows] for s in starts], axis=1)
            for z in range(n_pair):
                for slot in range(2):
                    at = (2 * z + (y ^ slot)) * columns
                    piece = jnp.concatenate([part[t * patches + at : t * patches + at + columns] for t in range(t_dev)], axis=0).astype(BF)
                    out_ref[((2 * z + y) * 2 + slot) * 2 + c] = piece
def norm_send(tokens, gain, bias, n_pair, n_chip, columns, own_rows, t_dev):
    devices = 4 * n_pair * n_chip
    return pl.pallas_call(functools.partial(norm_kernel,n_pair=n_pair,n_chip=n_chip,columns=columns,own_rows=own_rows,t_dev=t_dev),
        out_shape=jax.ShapeDtypeStruct((devices,t_dev*columns,tokens.shape[1]//4),BF),compiler_params=ROOM)(tokens,gain[None],bias[None])

def weights_kernel(chip_ref, w_ref, out_ref, win_ref, sem, *, n_chip):
    kinds, width, part = out_ref.shape
    window = win_ref.shape[2]
    chip = chip_ref[0]
    starts = [min(part * j // 128 * 128, width - window) for j in range(n_chip)]
    start = sum(jnp.where(chip == j, at, 0) for j, at in enumerate(starts))
    copies = [
        pltpu.make_async_copy(
            w_ref.at[:, pl.ds(pl.multiple_of(c * width + start, 128), window)], win_ref.at[c], sem.at[c]
        )
        for c in range(kinds)
    ]
    for copy in copies:
        copy.start()
    for copy in copies:
        copy.wait()
    for j in range(n_chip):

        @pl.when(chip == j)
        def _(j=j):
            before = part * j - starts[j]
            for c in range(kinds):
                out_ref[c] = win_ref[c, :, before : before + part]


def own_weights(w_qkv, chip, n_chip):
    width = w_qkv.shape[0]
    kinds, part = w_qkv.shape[1] // width, width // n_chip
    window = -(-(part + 64) // 128) * 128
    return pl.pallas_call(
        functools.partial(weights_kernel, n_chip=n_chip),
        grid_spec=pltpu.PrefetchScalarGridSpec(
            num_scalar_prefetch=1,
            grid=(1,),
            in_specs=[pl.BlockSpec(memory_space=pl.ANY)],
            out_specs=pl.BlockSpec((kinds, width, part), lambda i, s: (0, 0, 0)),
            scratch_shapes=[
                pltpu.VMEM((kinds, width, window), BF),
                pltpu.SemaphoreType.DMA((kinds,)),
            ],
        ),
        out_shape=jax.ShapeDtypeStruct((kinds, width, part), BF),
        compiler_params=ROOM,
    )(chip[None], w_qkv)


def share_kernel(where_ref, *refs):
    grads_refs, (w_ref, leave_ref, stay_ref, turn_ref) = refs[:2], refs[2:]
    patch = where_ref[0]
    chip, core = patch // 2, patch % 2
    kinds = w_ref.shape[0]
    part = w_ref.shape[2] // 2
    n, group, _ = leave_ref.shape
    for side in range(2):

        @pl.when(core == side)
        def _(side=side):
            for pieces, at in ((grads_refs[:1], side * part), (grads_refs[1:], (1 - side) * part)):
                for c, grads in enumerate(kinds_of(pieces)):
                    rows = grads.astype(F32).T.astype(BF)
                    turn_ref[c, :, :, :, :, at : at + part] = rows.reshape(n, 2, 2, group, part)

    total = None
    for c in range(kinds):
        rows = jnp.concatenate(
            [turn_ref[c, :, which, core].reshape(n * group, 2 * part) for which in (1 - chip, chip)],
            axis=0,
        )
        one = lax.dot_general(rows, w_ref[c], COLS, preferred_element_type=F32)
        total = one if total is None else total + one
    leave_ref[...] = total[: n * group].reshape(leave_ref.shape).astype(BF)
    stay_ref[...] = total[n * group :].reshape(stay_ref.shape)


def kinds_of(refs):
    return [ref[i] for ref in refs for i in range(ref.shape[0])]


def whole_spec(array):
    return pl.BlockSpec(array.shape, lambda i, s: (0,) * array.ndim)


def share_send(pieces, weights, patch, group):
    kinds, width, double = weights.shape
    n = pieces[0].shape[-1] // (4 * group)
    return pl.pallas_call(
        share_kernel,
        grid_spec=pltpu.PrefetchScalarGridSpec(
            num_scalar_prefetch=1,
            grid=(1,),
            in_specs=[whole_spec(array) for array in (*pieces, weights)],
            out_specs=[pl.BlockSpec((n, group, width), lambda i, s: (0, 0, 0))] * 2,
            scratch_shapes=[pltpu.VMEM((kinds, n, 2, 2, group, double), BF)],
        ),
        out_shape=[
            jax.ShapeDtypeStruct((n, group, width), BF),
            jax.ShapeDtypeStruct((n, group, width), F32),
        ],
        compiler_params=ROOM,
    )(patch[None], *pieces, weights)


def add_kernel(stay_ref, come_ref, out_ref):
    out_ref[...] = (stay_ref[...] + come_ref[...].astype(F32)).astype(BF)


def own_kernel(chip_ref, mine_ref, theirs_ref, *refs):
    norm = jnp.where(chip_ref[0] == 0, mine_ref[...], theirs_ref[...])
    part = refs[0].shape[1]
    for i, grads in enumerate(kinds_of(refs[:-1])):
        refs[-1][i * part : (i + 1) * part, :] = jnp.dot(grads, norm, preferred_element_type=F32)


def own_product(chip, mine, theirs, pieces):
    part = mine.shape[1]
    rows = part * sum(piece.shape[0] for piece in pieces)
    arrays = (mine, theirs, *pieces)
    return pl.pallas_call(
        own_kernel,
        grid_spec=pltpu.PrefetchScalarGridSpec(
            num_scalar_prefetch=1,
            grid=(1,),
            in_specs=[whole_spec(array) for array in arrays],
            out_specs=pl.BlockSpec((rows, part), lambda i, s: (0, 0)),
        ),
        out_shape=jax.ShapeDtypeStruct((rows, part), F32),
        compiler_params=ROOM,
    )(chip[None], *arrays)


def other_kernel(chip_ref, mine_ref, theirs_ref, acc_ref, *refs, factor, own_rows):
    pieces, (out_ref, sum_ref) = refs[:-2], refs[-2:]
    norm = jnp.where(chip_ref[0] == 0, theirs_ref[...], mine_ref[...])
    part = pieces[0].shape[1]
    for i, grads in enumerate(kinds_of(pieces)):
        rows = slice(i * part, (i + 1) * part)
        total = acc_ref[rows, :] + jnp.dot(grads, norm, preferred_element_type=F32)
        sum_ref[rows, :] = total * factor
    full, left = divmod(sum_ref.shape[0], 128)
    packed = len(out_ref.shape) == 3 and out_ref.shape[2] == 128
    for n in range(full + (left > 0)):
        block = sum_ref[n * 128 : (n + 1) * 128, :].T if n < full else sum_ref[n * 128 :, :].T
        for k in range(out_ref.shape[0]):
            rows = block[k * own_rows : (k + 1) * own_rows].astype(BF)
            if not packed:
                out_ref[k, :, n * 128 : n * 128 + rows.shape[1]] = rows
            elif n < full:
                out_ref[k, n * own_rows : (n + 1) * own_rows, :] = rows
            else:
                rows = block[k * own_rows : (k + 1) * own_rows]
                both = jnp.concatenate([rows[: own_rows // 2], rows[own_rows // 2 :]], axis=1)
                out_ref[k, n * own_rows :, :] = both.astype(BF)


def packable(own_rows, lanes):
    return own_rows % 4 == 0 and lanes % 128 == 64


def other_product(chip, mine, theirs, acc, pieces, own_rows, factor):
    lanes, part = acc.shape
    chunk = (own_rows * lanes // 128, 128) if packable(own_rows, lanes) else (own_rows, lanes)
    shape = (part // own_rows,) + chunk
    arrays = (mine, theirs, acc, *pieces)
    return pl.pallas_call(
        functools.partial(other_kernel, factor=factor, own_rows=own_rows),
        grid_spec=pltpu.PrefetchScalarGridSpec(
            num_scalar_prefetch=1,
            grid=(1,),
            in_specs=[whole_spec(array) for array in arrays],
            out_specs=pl.BlockSpec(shape, lambda i, s: (0, 0, 0)),
            scratch_shapes=[pltpu.VMEM((lanes, part), F32)],
        ),
        out_shape=jax.ShapeDtypeStruct(shape, BF),
        compiler_params=ROOM,
    )(chip[None], *arrays)


def last_kernel(tm_ref, stay_ref, come_ref, x_ref, grad_ref, gain_ref, out_ref, *, columns, t_dev):
    n_pair, group, width = stay_ref.shape
    patches = x_ref.shape[0] // t_dev
    tm = tm_ref[0]
    first = tm % 2 == 0
    for z in range(n_pair):
        slot = (tm // 2) ^ z
        stay, come = stay_ref[slot].astype(F32), come_ref[slot].astype(F32)
        for y in range(2):
            d_norm = jnp.where(first == (y == 0), stay, come)
            for t in range(t_dev):
                at = t * patches + (2 * z + y) * columns
                rows = slice(at, at + columns)
                tokens = x_ref[rows, :].astype(F32)
                centered = tokens - jnp.mean(tokens, axis=-1, keepdims=True)
                variance = jnp.mean(centered * centered, axis=-1, keepdims=True)
                inverse = lax.rsqrt(variance + 1e-06)
                normed = centered * inverse
                scaled = d_norm[t * columns : (t + 1) * columns] * gain_ref[...]
                branch = inverse * (
                    scaled
                    - jnp.mean(scaled, axis=-1, keepdims=True)
                    - normed * jnp.mean(scaled * normed, axis=-1, keepdims=True)
                )
                out_ref[rows, :] = (grad_ref[rows, :].astype(F32) + branch).astype(BF)


def last(stay, come, tokens, grads, gain, tm, columns, t_dev):
    n_rows, width = tokens.shape
    part = pl.BlockSpec(stay.shape, lambda i, s: (0, 0, 0))
    rows = pl.BlockSpec((n_rows, width), lambda i, s: (0, 0))
    return pl.pallas_call(
        functools.partial(last_kernel, columns=columns, t_dev=t_dev),
        grid_spec=pltpu.PrefetchScalarGridSpec(
            num_scalar_prefetch=1,
            grid=(1,),
            in_specs=[part, part, rows, rows, pl.BlockSpec((1, width), lambda i, s: (0, 0))],
            out_specs=rows,
        ),
        out_shape=jax.ShapeDtypeStruct((n_rows, width), BF),
        compiler_params=ROOM,
    )(tm[None], stay, come, tokens, grads, gain[None])


def final_kernel(core_ref, in_ref, out_ref, *, part, kinds):
    n_pair, n_chip = in_ref.shape[:2]
    own_rows = out_ref.shape[0]
    lanes = 2 * kinds * part
    for x in range(n_chip):
        total = in_ref[0, x].astype(F32)
        for z in range(1, n_pair):
            total = total + in_ref[z, x].astype(F32)
        if packable(own_rows, lanes):
            full = lanes // 128
            blocks = [total[n * own_rows : (n + 1) * own_rows] for n in range(full)]
            both, half = total[full * own_rows :], own_rows // 2
            blocks.append(jnp.concatenate([both[:half, :64], both[:half, 64:]], axis=0))
            total = jnp.concatenate(blocks, axis=1)
        for core in range(2):

            @pl.when(core_ref[0] == core)
            def _(core=core, total=total, x=x):
                for r in range(2):
                    for c in range(kinds):
                        at = (c * n_chip * 2 + 2 * x + (r ^ core)) * part
                        src = (r * kinds + c) * part
                        out_ref[:, at : at + part] = total[:, src : src + part]


def final_sum(pieces, core, own_rows, part, kinds):
    n_chip = pieces.shape[1]
    shape = (own_rows, 2 * n_chip * kinds * part)
    return pl.pallas_call(
        functools.partial(final_kernel, part=part, kinds=kinds),
        grid_spec=pltpu.PrefetchScalarGridSpec(
            num_scalar_prefetch=1,
            grid=(1,),
            in_specs=[whole_spec(pieces)],
            out_specs=pl.BlockSpec(shape, lambda i, s: (0, 0)),
        ),
        out_shape=jax.ShapeDtypeStruct(shape, F32),
        compiler_params=ROOM,
    )(core[None], pieces)


def per_device(tokens, ln_gain, ln_bias, w_qkv, w_out, q_time, k_time, v_time, grad_out):
    t_dev, patches, width = tokens.shape
    frames, columns, part = q_time.shape
    n_tm = lax.axis_size("tm")
    n_patch = lax.axis_size("patch")
    n_pair = n_tm // 2
    n_chip = n_patch // 2
    devices = n_tm * n_patch
    n_tok = frames * columns
    own_rows = width // devices
    tm = lax.axis_index("tm")
    patch = lax.axis_index("patch")
    side = tm % 2
    core = patch % 2
    both = ("tm", "patch")

    def swap(values, axis, size, bit):
        return lax.ppermute(values, axis, [(i, i ^ bit) for i in range(size)])

    grad_rows = grad_out.reshape(-1, width)
    d_attn = jnp.einsum(
        "to,jfo->jtf", grad_rows, w_out.reshape(n_patch, part, width), preferred_element_type=F32
    ).astype(BF)
    d_attn = d_attn.reshape(n_patch, t_dev, n_tm, columns, part).transpose(2, 0, 1, 3, 4)
    d_attn, token_rows, w_late = lax.optimization_barrier((d_attn, tokens.reshape(-1, width), w_qkv))
    d_time = lax.all_to_all(
        d_attn.reshape(devices, t_dev, columns, part), both, 0, 0, tiled=True
    ).reshape(n_tok, part)

    sent = norm_send(token_rows, ln_gain, ln_bias, n_pair, n_chip, columns, own_rows, t_dev)
    weights = own_weights(w_late, patch // 2, n_chip)
    d_time, sent, weights = lax.optimization_barrier((d_time, sent, weights))
    mine = lax.all_to_all(sent, both, 0, 0, tiled=True).reshape(n_tok, width // 4)
    theirs = swap(mine, "patch", n_patch, 2)

    saved = [values.reshape(n_tok, part) for values in (q_time, k_time, v_time)]
    grads, *others = attend(*saved, d_time, columns)
    grads_core, others = lax.optimization_barrier((swap(grads, "patch", n_patch, 1), others))
    pieces = [grads, grads_core]
    others = [swap(piece, "tm", n_tm, 1) for piece in others]

    leave, stay = share_send(pieces, weights, patch, t_dev * columns)
    come = swap(leave, "patch", n_patch, 2)
    share = pl.pallas_call(
        add_kernel, out_shape=jax.ShapeDtypeStruct(leave.shape, BF), compiler_params=ROOM
    )(stay, come)
    share = share.reshape((n_pair, 2) + share.shape[1:])
    spread = [lax.dynamic_index_in_dim(share, (tm // 2) ^ n, 0, keepdims=False) for n in range(n_pair)]
    spread = spread[:1] + [swap(spread[n], "tm", n_tm, 2 * n) for n in range(1, n_pair)]
    own = own_product(patch // 2, mine, theirs, pieces)
    others, theirs, own, early = lax.optimization_barrier((others, theirs, own, spread[:-1]))
    others = list(others)
    spread = early + spread[-1:]
    others += [swap(piece, "patch", n_patch, 1) for piece in others]

    factor = 1.0 / math.sqrt(frames * patches)
    groups = [
        [(2 * z + y) * n_patch + 2 * x + c for z in range(n_pair) for x in range(n_chip)]
        for y in range(2)
        for c in range(2)
    ]
    partial = other_product(patch // 2, mine, theirs, own, others, own_rows, factor)
    partial, spread = lax.optimization_barrier((partial, spread))
    summands = lax.all_to_all(partial, both, 0, 0, axis_index_groups=groups, tiled=True)
    summands = summands.reshape((n_pair, n_chip) + summands.shape[1:])
    grad_w_qkv = final_sum(summands, core, own_rows, part, 3)

    spread = jnp.stack(spread)
    stay = lax.dynamic_index_in_dim(spread, side, 1, keepdims=False)
    come = swap(lax.dynamic_index_in_dim(spread, 1 - side, 1, keepdims=False), "tm", n_tm, 1)
    grad_x = last(stay, come, tokens.reshape(-1, width), grad_rows, ln_gain, tm, columns, t_dev)
    grad_x = grad_x.reshape(t_dev, patches, width)
    return (grad_x, grad_w_qkv)


def solution(mesh):
    return jax.shard_map(
        per_device,
        mesh=mesh,
        in_specs=(
            P(("tm", "patch"), None, None),
            P(),
            P(),
            P(),
            P(),
            P(None, "tm", "patch"),
            P(None, "tm", "patch"),
            P(None, "tm", "patch"),
            P(("tm", "patch"), None, None),
        ),
        out_specs=(P(("tm", "patch"), None, None), P(("tm", "patch"), None)),
        check_vma=False,
    )
```

```python
import functools
import math

import jax
import jax.numpy as jnp
from jax import lax
from jax.experimental import pallas as pl
from jax.experimental.pallas import tpu as pltpu
from jax.sharding import PartitionSpec as P

DH = 88
BF = jnp.bfloat16
F32 = jnp.float32
ROWS = (((0,), (0,)), ((), ()))
COLS = (((1,), (1,)), ((), ()))
CROSS = (((0,), (1,)), ((), ()))
ROOM = pltpu.CompilerParams(vmem_limit_bytes=28 * 1024 * 1024)


def attend_kernel(q_ref, k_ref, v_ref, d_ref, all_ref, query_ref, rest_ref, sem, *, columns):
    n_tok, width = q_ref.shape
    factor = 1.0 / math.sqrt(DH)
    source = lax.broadcasted_iota(jnp.int32, (n_tok, n_tok), 0)
    target = lax.broadcasted_iota(jnp.int32, (n_tok, n_tok), 1)
    same = ((source ^ target) & (columns - 1)) == 0
    for start in range(0, width, DH):
        lanes = slice(start, start + DH)
        query, key, value, grad = [ref[:, lanes] for ref in (q_ref, k_ref, v_ref, d_ref)]
        scores = lax.dot_general(key, query, COLS, preferred_element_type=F32) * factor
        scores = jnp.where(same, scores, -jnp.inf)
        exponent = jnp.exp(scores - jnp.max(scores, axis=0, keepdims=True))
        probability = exponent * (1.0 / jnp.sum(exponent, axis=0, keepdims=True))
        prob_grad = lax.dot_general(value, grad, COLS, preferred_element_type=F32)
        row_dot = jnp.sum(probability * prob_grad, axis=0, keepdims=True)
        score_grad = (probability * (prob_grad - row_dot) * factor).astype(BF)
        prob_low = probability.astype(BF)
        for kind, (left, right, dims) in enumerate(
            ((key, score_grad, ROWS), (query, score_grad, CROSS), (grad, prob_low, CROSS))
        ):
            total = lax.dot_general(left, right, dims, preferred_element_type=F32)
            all_ref[kind, lanes, :] = total.astype(BF)
    copies = [
        pltpu.make_async_copy(all_ref.at[pl.ds(at, ref.shape[0])], ref, sem.at[at])
        for at, ref in ((0, query_ref), (1, rest_ref))
    ]
    for copy in copies:
        copy.start()
    for copy in copies:
        copy.wait()


def attend(query, key, value, grad, columns):
    n_tok, width = query.shape
    return pl.pallas_call(
        functools.partial(attend_kernel, columns=columns),
        out_specs=[pl.BlockSpec(memory_space=pltpu.VMEM)] + [pl.BlockSpec(memory_space=pltpu.HBM)] * 2,
        scratch_shapes=[pltpu.SemaphoreType.DMA((2,))],
        out_shape=[jax.ShapeDtypeStruct((3, width, n_tok), BF)]
        + [pltpu.HBM((kinds, width, n_tok), BF) for kinds in (1, 2)],
        compiler_params=ROOM,
    )(query, key, value, grad)


def norm_kernel(x_ref, gain_ref, bias_ref, out_ref, *, n_pair, n_chip, columns, own_rows, t_dev):
    width = x_ref.shape[1]
    rows = x_ref[...].astype(F32)
    centered = rows - jnp.mean(rows, axis=-1, keepdims=True)
    variance = jnp.mean(centered * centered, axis=-1, keepdims=True)
    norm = centered * lax.rsqrt(variance + 1e-06) * gain_ref[...] + bias_ref[...]
    patches = x_ref.shape[0] // t_dev
    for y in range(2):
        for c in range(2):
            starts = [((2 * z + y) * n_chip + x) * 2 * own_rows + c * own_rows for z in range(n_pair) for x in range(n_chip)]
            part = jnp.concatenate([norm[:, s : s + own_rows] for s in starts], axis=1)
            for z in range(n_pair):
                for slot in range(2):
                    at = (2 * z + (y ^ slot)) * columns
                    piece = jnp.concatenate([part[t * patches + at : t * patches + at + columns] for t in range(t_dev)], axis=0).astype(BF)
                    out_ref[((2 * z + y) * 2 + slot) * 2 + c] = piece
def norm_send(tokens, gain, bias, n_pair, n_chip, columns, own_rows, t_dev):
    devices = 4 * n_pair * n_chip
    return pl.pallas_call(functools.partial(norm_kernel,n_pair=n_pair,n_chip=n_chip,columns=columns,own_rows=own_rows,t_dev=t_dev),
        out_shape=jax.ShapeDtypeStruct((devices,t_dev*columns,tokens.shape[1]//4),BF),compiler_params=ROOM)(tokens,gain[None],bias[None])

def weights_kernel(chip_ref, w_ref, out_ref, win_ref, sem, *, n_chip):
    kinds, width, part = out_ref.shape
    window = win_ref.shape[2]
    chip = chip_ref[0]
    starts = [min(part * j // 128 * 128, width - window) for j in range(n_chip)]
    start = sum(jnp.where(chip == j, at, 0) for j, at in enumerate(starts))
    copies = [
        pltpu.make_async_copy(
            w_ref.at[:, pl.ds(pl.multiple_of(c * width + start, 128), window)], win_ref.at[c], sem.at[c]
        )
        for c in range(kinds)
    ]
    for copy in copies:
        copy.start()
    for copy in copies:
        copy.wait()
    for j in range(n_chip):

        @pl.when(chip == j)
        def _(j=j):
            before = part * j - starts[j]
            for c in range(kinds):
                out_ref[c] = win_ref[c, :, before : before + part]


def own_weights(w_qkv, chip, n_chip):
    width = w_qkv.shape[0]
    kinds, part = w_qkv.shape[1] // width, width // n_chip
    window = -(-(part + 64) // 128) * 128
    return pl.pallas_call(
        functools.partial(weights_kernel, n_chip=n_chip),
        grid_spec=pltpu.PrefetchScalarGridSpec(
            num_scalar_prefetch=1,
            grid=(1,),
            in_specs=[pl.BlockSpec(memory_space=pl.ANY)],
            out_specs=pl.BlockSpec((kinds, width, part), lambda i, s: (0, 0, 0)),
            scratch_shapes=[
                pltpu.VMEM((kinds, width, window), BF),
                pltpu.SemaphoreType.DMA((kinds,)),
            ],
        ),
        out_shape=pltpu.HBM((kinds, width, part), BF),
        compiler_params=ROOM,
    )(chip[None], pltpu.with_memory_space_constraint(w_qkv, pltpu.HBM))


def share_kernel(where_ref, *refs):
    grads_refs, (w_hbm, leave_ref, stay_hbm, turn_ref, w_ref, stay_ref, sem) = refs[:2], refs[2:]
    copies = [
        pltpu.make_async_copy(w_hbm.at[c], w_ref.at[c], sem.at[c]) for c in range(w_ref.shape[0])
    ]
    for copy in copies:
        copy.start()
    patch = where_ref[0]
    chip, core = patch // 2, patch % 2
    kinds = w_ref.shape[0]
    part = w_ref.shape[2] // 2
    n, group, _ = leave_ref.shape
    for side in range(2):

        @pl.when(core == side)
        def _(side=side):
            for pieces, at in ((grads_refs[:1], side * part), (grads_refs[1:], (1 - side) * part)):
                for c, grads in enumerate(kinds_of(pieces)):
                    rows = grads.astype(F32).T.astype(BF)
                    turn_ref[c, :, :, :, :, at : at + part] = rows.reshape(n, 2, 2, group, part)

    total = None
    for c in range(kinds):
        copies[c].wait()
        rows = jnp.concatenate(
            [turn_ref[c, :, which, core].reshape(n * group, 2 * part) for which in (1 - chip, chip)],
            axis=0,
        )
        one = lax.dot_general(rows, w_ref[c], COLS, preferred_element_type=F32)
        total = one if total is None else total + one
    stay_ref[...] = total[n * group :].reshape(stay_ref.shape)
    copy = pltpu.make_async_copy(stay_ref, stay_hbm, sem.at[kinds])
    copy.start()
    leave_ref[...] = total[: n * group].reshape(leave_ref.shape).astype(BF)
    copy.wait()


def kinds_of(refs):
    return [ref[i] for ref in refs for i in range(ref.shape[0])]


def whole_spec(array):
    return pl.BlockSpec(array.shape, lambda i, s: (0,) * array.ndim)


def share_send(pieces, weights, patch, group):
    kinds, width, double = weights.shape
    n = pieces[0].shape[-1] // (4 * group)
    return pl.pallas_call(
        share_kernel,
        grid_spec=pltpu.PrefetchScalarGridSpec(
            num_scalar_prefetch=1,
            grid=(1,),
            in_specs=[whole_spec(array) for array in pieces] + [pl.BlockSpec(memory_space=pltpu.HBM)],
            out_specs=[
                pl.BlockSpec((n, group, width), lambda i, s: (0, 0, 0)),
                pl.BlockSpec(memory_space=pltpu.HBM),
            ],
            scratch_shapes=[
                pltpu.VMEM((kinds, n, 2, 2, group, double), BF),
                pltpu.VMEM((kinds, width, double), BF),
                pltpu.VMEM((n, group, width), F32),
                pltpu.SemaphoreType.DMA((kinds + 1,)),
            ],
        ),
        out_shape=[
            jax.ShapeDtypeStruct((n, group, width), BF),
            pltpu.HBM((n, group, width), F32),
        ],
        compiler_params=ROOM,
    )(patch[None], *pieces, pltpu.with_memory_space_constraint(weights, pltpu.HBM))


def add_kernel(stay_hbm, come_ref, out_ref, stay_ref, sem):
    copy = pltpu.make_async_copy(stay_hbm, stay_ref, sem)
    copy.start()
    copy.wait()
    out_ref[...] = (stay_ref[...] + come_ref[...].astype(F32)).astype(BF)


def own_kernel(chip_ref, mine_ref, theirs_ref, *refs):
    norm = jnp.where(chip_ref[0] == 0, mine_ref[...], theirs_ref[...])
    part = refs[0].shape[1]
    for i, grads in enumerate(kinds_of(refs[:-1])):
        refs[-1][i * part : (i + 1) * part, :] = jnp.dot(grads, norm, preferred_element_type=F32)


def own_product(chip, mine, theirs, pieces):
    part = mine.shape[1]
    rows = part * sum(piece.shape[0] for piece in pieces)
    arrays = (mine, theirs, *pieces)
    return pl.pallas_call(
        own_kernel,
        grid_spec=pltpu.PrefetchScalarGridSpec(
            num_scalar_prefetch=1,
            grid=(1,),
            in_specs=[whole_spec(array) for array in arrays],
            out_specs=pl.BlockSpec((rows, part), lambda i, s: (0, 0)),
        ),
        out_shape=jax.ShapeDtypeStruct((rows, part), F32),
        compiler_params=ROOM,
    )(chip[None], *arrays)


def other_kernel(chip_ref, mine_ref, theirs_ref, acc_ref, *refs, factor, own_rows):
    pieces, (out_ref, sum_ref) = refs[:-2], refs[-2:]
    norm = jnp.where(chip_ref[0] == 0, theirs_ref[...], mine_ref[...])
    part = pieces[0].shape[1]
    for i, grads in enumerate(kinds_of(pieces)):
        rows = slice(i * part, (i + 1) * part)
        total = acc_ref[rows, :] + jnp.dot(grads, norm, preferred_element_type=F32)
        sum_ref[rows, :] = total * factor
    full, left = divmod(sum_ref.shape[0], 128)
    packed = len(out_ref.shape) == 3 and out_ref.shape[2] == 128
    for n in range(full + (left > 0)):
        block = sum_ref[n * 128 : (n + 1) * 128, :].T if n < full else sum_ref[n * 128 :, :].T
        for k in range(out_ref.shape[0]):
            rows = block[k * own_rows : (k + 1) * own_rows].astype(BF)
            if not packed:
                out_ref[k, :, n * 128 : n * 128 + rows.shape[1]] = rows
            elif n < full:
                out_ref[k, n * own_rows : (n + 1) * own_rows, :] = rows
            else:
                rows = block[k * own_rows : (k + 1) * own_rows]
                both = jnp.concatenate([rows[: own_rows // 2], rows[own_rows // 2 :]], axis=1)
                out_ref[k, n * own_rows :, :] = both.astype(BF)


def packable(own_rows, lanes):
    return own_rows % 4 == 0 and lanes % 128 == 64


def other_product(chip, mine, theirs, acc, pieces, own_rows, factor):
    lanes, part = acc.shape
    chunk = (own_rows * lanes // 128, 128) if packable(own_rows, lanes) else (own_rows, lanes)
    shape = (part // own_rows,) + chunk
    arrays = (mine, theirs, acc, *pieces)
    return pl.pallas_call(
        functools.partial(other_kernel, factor=factor, own_rows=own_rows),
        grid_spec=pltpu.PrefetchScalarGridSpec(
            num_scalar_prefetch=1,
            grid=(1,),
            in_specs=[whole_spec(array) for array in arrays],
            out_specs=pl.BlockSpec(shape, lambda i, s: (0, 0, 0)),
            scratch_shapes=[pltpu.VMEM((lanes, part), F32)],
        ),
        out_shape=jax.ShapeDtypeStruct(shape, BF),
        compiler_params=ROOM,
    )(chip[None], *arrays)


def last_kernel(tm_ref, stay_ref, come_ref, x_ref, grad_ref, gain_ref, out_ref, *, columns, t_dev):
    n_pair, group, width = stay_ref.shape
    patches = x_ref.shape[0] // t_dev
    tm = tm_ref[0]
    first = tm % 2 == 0
    for z in range(n_pair):
        slot = (tm // 2) ^ z
        stay, come = stay_ref[slot].astype(F32), come_ref[slot].astype(F32)
        for y in range(2):
            d_norm = jnp.where(first == (y == 0), stay, come)
            for t in range(t_dev):
                at = t * patches + (2 * z + y) * columns
                rows = slice(at, at + columns)
                tokens = x_ref[rows, :].astype(F32)
                centered = tokens - jnp.mean(tokens, axis=-1, keepdims=True)
                variance = jnp.mean(centered * centered, axis=-1, keepdims=True)
                inverse = lax.rsqrt(variance + 1e-06)
                normed = centered * inverse
                scaled = d_norm[t * columns : (t + 1) * columns] * gain_ref[...]
                branch = inverse * (
                    scaled
                    - jnp.mean(scaled, axis=-1, keepdims=True)
                    - normed * jnp.mean(scaled * normed, axis=-1, keepdims=True)
                )
                out_ref[rows, :] = (grad_ref[rows, :].astype(F32) + branch).astype(BF)


def last(stay, come, tokens, grads, gain, tm, columns, t_dev):
    n_rows, width = tokens.shape
    part = pl.BlockSpec(stay.shape, lambda i, s: (0, 0, 0))
    rows = pl.BlockSpec((n_rows, width), lambda i, s: (0, 0))
    return pl.pallas_call(
        functools.partial(last_kernel, columns=columns, t_dev=t_dev),
        grid_spec=pltpu.PrefetchScalarGridSpec(
            num_scalar_prefetch=1,
            grid=(1,),
            in_specs=[part, part, rows, rows, pl.BlockSpec((1, width), lambda i, s: (0, 0))],
            out_specs=rows,
        ),
        out_shape=jax.ShapeDtypeStruct((n_rows, width), BF),
        compiler_params=ROOM,
    )(tm[None], stay, come, tokens, grads, gain[None])


def final_kernel(core_ref, in_ref, out_ref, *, part, kinds):
    n_pair, n_chip = in_ref.shape[:2]
    own_rows = out_ref.shape[0]
    lanes = 2 * kinds * part
    for x in range(n_chip):
        total = in_ref[0, x].astype(F32)
        for z in range(1, n_pair):
            total = total + in_ref[z, x].astype(F32)
        if packable(own_rows, lanes):
            full = lanes // 128
            blocks = [total[n * own_rows : (n + 1) * own_rows] for n in range(full)]
            both, half = total[full * own_rows :], own_rows // 2
            blocks.append(jnp.concatenate([both[:half, :64], both[:half, 64:]], axis=0))
            total = jnp.concatenate(blocks, axis=1)
        for core in range(2):

            @pl.when(core_ref[0] == core)
            def _(core=core, total=total, x=x):
                for r in range(2):
                    for c in range(kinds):
                        at = (c * n_chip * 2 + 2 * x + (r ^ core)) * part
                        src = (r * kinds + c) * part
                        out_ref[:, at : at + part] = total[:, src : src + part]


def final_sum(pieces, core, own_rows, part, kinds):
    n_chip = pieces.shape[1]
    shape = (own_rows, 2 * n_chip * kinds * part)
    return pl.pallas_call(
        functools.partial(final_kernel, part=part, kinds=kinds),
        grid_spec=pltpu.PrefetchScalarGridSpec(
            num_scalar_prefetch=1,
            grid=(1,),
            in_specs=[whole_spec(pieces)],
            out_specs=pl.BlockSpec(shape, lambda i, s: (0, 0)),
        ),
        out_shape=jax.ShapeDtypeStruct(shape, F32),
        compiler_params=ROOM,
    )(core[None], pieces)


def per_device(tokens, ln_gain, ln_bias, w_qkv, w_out, q_time, k_time, v_time, grad_out):
    t_dev, patches, width = tokens.shape
    frames, columns, part = q_time.shape
    n_tm = lax.axis_size("tm")
    n_patch = lax.axis_size("patch")
    n_pair = n_tm // 2
    n_chip = n_patch // 2
    devices = n_tm * n_patch
    n_tok = frames * columns
    own_rows = width // devices
    tm = lax.axis_index("tm")
    patch = lax.axis_index("patch")
    side = tm % 2
    core = patch % 2
    both = ("tm", "patch")

    def swap(values, axis, size, bit):
        return lax.ppermute(values, axis, [(i, i ^ bit) for i in range(size)])

    grad_rows = grad_out.reshape(-1, width)
    d_attn = jnp.einsum(
        "to,jfo->jtf", grad_rows, w_out.reshape(n_patch, part, width), preferred_element_type=F32
    ).astype(BF)
    d_attn = d_attn.reshape(n_patch, t_dev, n_tm, columns, part).transpose(2, 0, 1, 3, 4)
    d_attn, token_rows, w_late = lax.optimization_barrier((d_attn, tokens.reshape(-1, width), w_qkv))
    d_time = lax.all_to_all(
        d_attn.reshape(devices, t_dev, columns, part), both, 0, 0, tiled=True
    ).reshape(n_tok, part)

    sent = norm_send(token_rows, ln_gain, ln_bias, n_pair, n_chip, columns, own_rows, t_dev)
    weights = own_weights(w_late, patch // 2, n_chip)
    d_time, sent, weights = lax.optimization_barrier((d_time, sent, weights))
    mine = lax.all_to_all(sent, both, 0, 0, tiled=True).reshape(n_tok, width // 4)
    theirs = swap(mine, "patch", n_patch, 2)

    saved = [values.reshape(n_tok, part) for values in (q_time, k_time, v_time)]
    grads, *others = attend(*saved, d_time, columns)
    grads_core, others = lax.optimization_barrier((swap(grads, "patch", n_patch, 1), others))
    pieces = [grads, grads_core]
    others = [swap(piece, "tm", n_tm, 1) for piece in others]

    leave, stay = share_send(pieces, weights, patch, t_dev * columns)
    come = swap(leave, "patch", n_patch, 2)
    share = pl.pallas_call(
        add_kernel,
        in_specs=[pl.BlockSpec(memory_space=space) for space in (pltpu.HBM, pltpu.VMEM)],
        out_shape=jax.ShapeDtypeStruct(leave.shape, BF),
        scratch_shapes=[pltpu.VMEM(stay.shape, F32), pltpu.SemaphoreType.DMA(())],
        compiler_params=ROOM,
    )(pltpu.with_memory_space_constraint(stay, pltpu.HBM), come)
    share = share.reshape((n_pair, 2) + share.shape[1:])
    spread = [lax.dynamic_index_in_dim(share, (tm // 2) ^ n, 0, keepdims=False) for n in range(n_pair)]
    spread = spread[:1] + [swap(spread[n], "tm", n_tm, 2 * n) for n in range(1, n_pair)]
    own = own_product(patch // 2, mine, theirs, pieces)
    others, theirs, own, early = lax.optimization_barrier((others, theirs, own, spread[:-1]))
    others = list(others)
    spread = early + spread[-1:]
    others += [swap(piece, "patch", n_patch, 1) for piece in others]

    factor = 1.0 / math.sqrt(frames * patches)
    groups = [
        [(2 * z + y) * n_patch + 2 * x + c for z in range(n_pair) for x in range(n_chip)]
        for y in range(2)
        for c in range(2)
    ]
    partial = other_product(patch // 2, mine, theirs, own, others, own_rows, factor)
    partial, spread = lax.optimization_barrier((partial, spread))
    summands = lax.all_to_all(partial, both, 0, 0, axis_index_groups=groups, tiled=True)
    summands = summands.reshape((n_pair, n_chip) + summands.shape[1:])
    grad_w_qkv = final_sum(summands, core, own_rows, part, 3)

    spread = jnp.stack(spread)
    stay = lax.dynamic_index_in_dim(spread, side, 1, keepdims=False)
    come = swap(lax.dynamic_index_in_dim(spread, 1 - side, 1, keepdims=False), "tm", n_tm, 1)
    grad_x = last(stay, come, tokens.reshape(-1, width), grad_rows, ln_gain, tm, columns, t_dev)
    grad_x = grad_x.reshape(t_dev, patches, width)
    return (grad_x, grad_w_qkv)


def solution(mesh):
    return jax.shard_map(
        per_device,
        mesh=mesh,
        in_specs=(
            P(("tm", "patch"), None, None),
            P(),
            P(),
            P(),
            P(),
            P(None, "tm", "patch"),
            P(None, "tm", "patch"),
            P(None, "tm", "patch"),
            P(("tm", "patch"), None, None),
        ),
        out_specs=(P(("tm", "patch"), None, None), P(("tm", "patch"), None)),
        check_vma=False,
    )
```

```python
import functools
import math

import jax
import jax.numpy as jnp
from jax import lax
from jax.experimental import pallas as pl
from jax.experimental.pallas import tpu as pltpu
from jax.sharding import PartitionSpec as P

DH = 88
BF = jnp.bfloat16
F32 = jnp.float32
ROWS = (((0,), (0,)), ((), ()))
COLS = (((1,), (1,)), ((), ()))
CROSS = (((0,), (1,)), ((), ()))
ROOM = pltpu.CompilerParams(vmem_limit_bytes=28 * 1024 * 1024)


def attend_kernel(q_ref, k_ref, v_ref, d_ref, all_ref, query_ref, rest_ref, sem, *, columns):
    n_tok, width = q_ref.shape
    factor = 1.0 / math.sqrt(DH)
    key_row = lax.broadcasted_iota(jnp.int32, (n_tok, n_tok), 0)
    query_row = lax.broadcasted_iota(jnp.int32, (n_tok, n_tok), 1)
    same = ((key_row ^ query_row) & (columns - 1)) == 0
    copies = []
    for head, start in enumerate(range(0, width, DH)):
        lanes = slice(start, start + DH)
        query, key, value, grad = [ref[:, lanes] for ref in (q_ref, k_ref, v_ref, d_ref)]
        scores = lax.dot_general(key, query, COLS, preferred_element_type=F32) * factor
        scores = jnp.where(same, scores, -jnp.inf)
        exponent = jnp.exp(scores - jnp.max(scores, axis=0, keepdims=True))
        probability = exponent * (1.0 / jnp.sum(exponent, axis=0, keepdims=True))
        prob_grad = lax.dot_general(value, grad, COLS, preferred_element_type=F32)
        row_dot = jnp.sum(probability * prob_grad, axis=0, keepdims=True)
        score_grad = (probability * (prob_grad - row_dot) * factor).astype(BF)
        prob_low = probability.astype(BF)
        for kind, (left, right, dims) in enumerate(
            ((key, score_grad, ROWS), (query, score_grad, CROSS), (grad, prob_low, CROSS))
        ):
            total = lax.dot_general(left, right, dims, preferred_element_type=F32)
            all_ref[kind, lanes, :] = total.astype(BF)
        for at, ref in ((0, query_ref), (1, rest_ref)):
            source = all_ref.at[pl.ds(at, ref.shape[0]), pl.ds(start, DH)]
            copy = pltpu.make_async_copy(source, ref.at[:, pl.ds(start, DH)], sem.at[head, at])
            copy.start()
            copies.append(copy)
    for copy in copies:
        copy.wait()


def attend(query, key, value, grad, columns):
    n_tok, width = query.shape
    return pl.pallas_call(
        functools.partial(attend_kernel, columns=columns),
        out_specs=[pl.BlockSpec(memory_space=pltpu.VMEM)] + [pl.BlockSpec(memory_space=pltpu.HBM)] * 2,
        scratch_shapes=[pltpu.SemaphoreType.DMA((width // DH, 2))],
        out_shape=[jax.ShapeDtypeStruct((3, width, n_tok), BF)]
        + [pltpu.HBM((kinds, width, n_tok), BF) for kinds in (1, 2)],
        compiler_params=ROOM,
    )(query, key, value, grad)


def norm_kernel(x_ref, gain_ref, bias_ref, out_ref, *, n_pair, n_chip, columns, own_rows, t_dev):
    width = x_ref.shape[1]
    rows = x_ref[...].astype(F32)
    centered = rows - jnp.mean(rows, axis=-1, keepdims=True)
    variance = jnp.mean(centered * centered, axis=-1, keepdims=True)
    norm = centered * lax.rsqrt(variance + 1e-06) * gain_ref[...] + bias_ref[...]
    patches = x_ref.shape[0] // t_dev
    for y in range(2):
        for c in range(2):
            starts = [((2 * z + y) * n_chip + x) * 2 * own_rows + c * own_rows for z in range(n_pair) for x in range(n_chip)]
            part = jnp.concatenate([norm[:, s : s + own_rows] for s in starts], axis=1)
            for z in range(n_pair):
                for slot in range(2):
                    at = (2 * z + (y ^ slot)) * columns
                    piece = jnp.concatenate([part[t * patches + at : t * patches + at + columns] for t in range(t_dev)], axis=0).astype(BF)
                    out_ref[((2 * z + y) * 2 + slot) * 2 + c] = piece
def norm_send(tokens, gain, bias, n_pair, n_chip, columns, own_rows, t_dev):
    devices = 4 * n_pair * n_chip
    return pl.pallas_call(functools.partial(norm_kernel,n_pair=n_pair,n_chip=n_chip,columns=columns,own_rows=own_rows,t_dev=t_dev),
        out_shape=jax.ShapeDtypeStruct((devices,t_dev*columns,tokens.shape[1]//4),BF),compiler_params=ROOM)(tokens,gain[None],bias[None])

def weights_kernel(chip_ref, w_ref, out_ref, win_ref, sem, *, n_chip):
    kinds, width, part = out_ref.shape
    window = win_ref.shape[2]
    chip = chip_ref[0]
    starts = [min(part * j // 128 * 128, width - window) for j in range(n_chip)]
    start = sum(jnp.where(chip == j, at, 0) for j, at in enumerate(starts))
    copies = [
        pltpu.make_async_copy(
            w_ref.at[:, pl.ds(pl.multiple_of(c * width + start, 128), window)], win_ref.at[c], sem.at[c]
        )
        for c in range(kinds)
    ]
    for copy in copies:
        copy.start()
    for copy in copies:
        copy.wait()
    for j in range(n_chip):

        @pl.when(chip == j)
        def _(j=j):
            before = part * j - starts[j]
            for c in range(kinds):
                out_ref[c] = win_ref[c, :, before : before + part]


def own_weights(w_qkv, chip, n_chip):
    width = w_qkv.shape[0]
    kinds, part = w_qkv.shape[1] // width, width // n_chip
    window = -(-(part + 64) // 128) * 128
    return pl.pallas_call(
        functools.partial(weights_kernel, n_chip=n_chip),
        grid_spec=pltpu.PrefetchScalarGridSpec(
            num_scalar_prefetch=1,
            grid=(1,),
            in_specs=[pl.BlockSpec(memory_space=pl.ANY)],
            out_specs=pl.BlockSpec((kinds, width, part), lambda i, s: (0, 0, 0)),
            scratch_shapes=[
                pltpu.VMEM((kinds, width, window), BF),
                pltpu.SemaphoreType.DMA((kinds,)),
            ],
        ),
        out_shape=pltpu.HBM((kinds, width, part), BF),
        compiler_params=ROOM,
    )(chip[None], pltpu.with_memory_space_constraint(w_qkv, pltpu.HBM))


def share_kernel(where_ref, *refs):
    grads_refs, (w_hbm, leave_ref, stay_hbm, turn_ref, w_ref, stay_ref, sem) = refs[:2], refs[2:]
    copies = [
        pltpu.make_async_copy(w_hbm.at[c], w_ref.at[c], sem.at[c]) for c in range(w_ref.shape[0])
    ]
    for copy in copies:
        copy.start()
    patch = where_ref[0]
    chip, core = patch // 2, patch % 2
    kinds = w_ref.shape[0]
    part = w_ref.shape[2] // 2
    n, group, _ = leave_ref.shape
    for side in range(2):

        @pl.when(core == side)
        def _(side=side):
            for pieces, at in ((grads_refs[:1], side * part), (grads_refs[1:], (1 - side) * part)):
                for c, grads in enumerate(kinds_of(pieces)):
                    rows = grads.astype(F32).T.astype(BF)
                    turn_ref[c, :, :, :, :, at : at + part] = rows.reshape(n, 2, 2, group, part)

    total = None
    for c in range(kinds):
        copies[c].wait()
        rows = jnp.concatenate(
            [turn_ref[c, :, which, core].reshape(n * group, 2 * part) for which in (1 - chip, chip)],
            axis=0,
        )
        one = lax.dot_general(rows, w_ref[c], COLS, preferred_element_type=F32)
        total = one if total is None else total + one
    stay_ref[...] = total[n * group :].reshape(stay_ref.shape)
    copy = pltpu.make_async_copy(stay_ref, stay_hbm, sem.at[kinds])
    copy.start()
    leave_ref[...] = total[: n * group].reshape(leave_ref.shape).astype(BF)
    copy.wait()


def kinds_of(refs):
    return [ref[i] for ref in refs for i in range(ref.shape[0])]


def whole_spec(array):
    return pl.BlockSpec(array.shape, lambda i, s: (0,) * array.ndim)


def share_send(pieces, weights, patch, group):
    kinds, width, double = weights.shape
    n = pieces[0].shape[-1] // (4 * group)
    return pl.pallas_call(
        share_kernel,
        grid_spec=pltpu.PrefetchScalarGridSpec(
            num_scalar_prefetch=1,
            grid=(1,),
            in_specs=[whole_spec(array) for array in pieces] + [pl.BlockSpec(memory_space=pltpu.HBM)],
            out_specs=[
                pl.BlockSpec((n, group, width), lambda i, s: (0, 0, 0)),
                pl.BlockSpec(memory_space=pltpu.HBM),
            ],
            scratch_shapes=[
                pltpu.VMEM((kinds, n, 2, 2, group, double), BF),
                pltpu.VMEM((kinds, width, double), BF),
                pltpu.VMEM((n, group, width), F32),
                pltpu.SemaphoreType.DMA((kinds + 1,)),
            ],
        ),
        out_shape=[
            jax.ShapeDtypeStruct((n, group, width), BF),
            pltpu.HBM((n, group, width), F32),
        ],
        compiler_params=ROOM,
    )(patch[None], *pieces, pltpu.with_memory_space_constraint(weights, pltpu.HBM))


def add_kernel(stay_hbm, come_ref, out_ref, stay_ref, sem):
    copy = pltpu.make_async_copy(stay_hbm, stay_ref, sem)
    copy.start()
    copy.wait()
    out_ref[...] = (stay_ref[...] + come_ref[...].astype(F32)).astype(BF)


def own_kernel(chip_ref, mine_ref, theirs_ref, *refs):
    norm = jnp.where(chip_ref[0] == 0, mine_ref[...], theirs_ref[...])
    part = refs[0].shape[1]
    for i, grads in enumerate(kinds_of(refs[:-1])):
        refs[-1][i * part : (i + 1) * part, :] = jnp.dot(grads, norm, preferred_element_type=F32)


def own_product(chip, mine, theirs, pieces):
    part = mine.shape[1]
    rows = part * sum(piece.shape[0] for piece in pieces)
    arrays = (mine, theirs, *pieces)
    return pl.pallas_call(
        own_kernel,
        grid_spec=pltpu.PrefetchScalarGridSpec(
            num_scalar_prefetch=1,
            grid=(1,),
            in_specs=[whole_spec(array) for array in arrays],
            out_specs=pl.BlockSpec((rows, part), lambda i, s: (0, 0)),
        ),
        out_shape=jax.ShapeDtypeStruct((rows, part), F32),
        compiler_params=ROOM,
    )(chip[None], *arrays)


def other_kernel(chip_ref, mine_ref, theirs_ref, acc_ref, *refs, factor, own_rows):
    pieces, (out_ref, sum_ref) = refs[:-2], refs[-2:]
    norm = jnp.where(chip_ref[0] == 0, theirs_ref[...], mine_ref[...])
    part = pieces[0].shape[1]
    for i, grads in enumerate(kinds_of(pieces)):
        rows = slice(i * part, (i + 1) * part)
        total = acc_ref[rows, :] + jnp.dot(grads, norm, preferred_element_type=F32)
        sum_ref[rows, :] = total * factor
    full, left = divmod(sum_ref.shape[0], 128)
    packed = len(out_ref.shape) == 3 and out_ref.shape[2] == 128
    for n in range(full + (left > 0)):
        block = sum_ref[n * 128 : (n + 1) * 128, :].T if n < full else sum_ref[n * 128 :, :].T
        for k in range(out_ref.shape[0]):
            rows = block[k * own_rows : (k + 1) * own_rows].astype(BF)
            if not packed:
                out_ref[k, :, n * 128 : n * 128 + rows.shape[1]] = rows
            elif n < full:
                out_ref[k, n * own_rows : (n + 1) * own_rows, :] = rows
            else:
                rows = block[k * own_rows : (k + 1) * own_rows]
                both = jnp.concatenate([rows[: own_rows // 2], rows[own_rows // 2 :]], axis=1)
                out_ref[k, n * own_rows :, :] = both.astype(BF)


def packable(own_rows, lanes):
    return own_rows % 4 == 0 and lanes % 128 == 64


def other_product(chip, mine, theirs, acc, pieces, own_rows, factor):
    lanes, part = acc.shape
    chunk = (own_rows * lanes // 128, 128) if packable(own_rows, lanes) else (own_rows, lanes)
    shape = (part // own_rows,) + chunk
    arrays = (mine, theirs, acc, *pieces)
    return pl.pallas_call(
        functools.partial(other_kernel, factor=factor, own_rows=own_rows),
        grid_spec=pltpu.PrefetchScalarGridSpec(
            num_scalar_prefetch=1,
            grid=(1,),
            in_specs=[whole_spec(array) for array in arrays],
            out_specs=pl.BlockSpec(shape, lambda i, s: (0, 0, 0)),
            scratch_shapes=[pltpu.VMEM((lanes, part), F32)],
        ),
        out_shape=jax.ShapeDtypeStruct(shape, BF),
        compiler_params=ROOM,
    )(chip[None], *arrays)


def last_kernel(tm_ref, stay_ref, come_ref, x_ref, grad_ref, gain_ref, out_ref, *, columns, t_dev):
    n_pair, group, width = stay_ref.shape
    patches = x_ref.shape[0] // t_dev
    tm = tm_ref[0]
    first = tm % 2 == 0
    for z in range(n_pair):
        slot = (tm // 2) ^ z
        stay, come = stay_ref[slot].astype(F32), come_ref[slot].astype(F32)
        for y in range(2):
            d_norm = jnp.where(first == (y == 0), stay, come)
            for t in range(t_dev):
                at = t * patches + (2 * z + y) * columns
                rows = slice(at, at + columns)
                tokens = x_ref[rows, :].astype(F32)
                centered = tokens - jnp.mean(tokens, axis=-1, keepdims=True)
                variance = jnp.mean(centered * centered, axis=-1, keepdims=True)
                inverse = lax.rsqrt(variance + 1e-06)
                normed = centered * inverse
                scaled = d_norm[t * columns : (t + 1) * columns] * gain_ref[...]
                branch = inverse * (
                    scaled
                    - jnp.mean(scaled, axis=-1, keepdims=True)
                    - normed * jnp.mean(scaled * normed, axis=-1, keepdims=True)
                )
                out_ref[rows, :] = (grad_ref[rows, :].astype(F32) + branch).astype(BF)


def last(stay, come, tokens, grads, gain, tm, columns, t_dev):
    n_rows, width = tokens.shape
    part = pl.BlockSpec(stay.shape, lambda i, s: (0, 0, 0))
    rows = pl.BlockSpec((n_rows, width), lambda i, s: (0, 0))
    return pl.pallas_call(
        functools.partial(last_kernel, columns=columns, t_dev=t_dev),
        grid_spec=pltpu.PrefetchScalarGridSpec(
            num_scalar_prefetch=1,
            grid=(1,),
            in_specs=[part, part, rows, rows, pl.BlockSpec((1, width), lambda i, s: (0, 0))],
            out_specs=rows,
        ),
        out_shape=jax.ShapeDtypeStruct((n_rows, width), BF),
        compiler_params=ROOM,
    )(tm[None], stay, come, tokens, grads, gain[None])


def final_kernel(core_ref, in_ref, out_ref, *, part, kinds):
    n_pair, n_chip = in_ref.shape[:2]
    own_rows = out_ref.shape[0]
    lanes = 2 * kinds * part
    for x in range(n_chip):
        total = in_ref[0, x].astype(F32)
        for z in range(1, n_pair):
            total = total + in_ref[z, x].astype(F32)
        if packable(own_rows, lanes):
            full = lanes // 128
            blocks = [total[n * own_rows : (n + 1) * own_rows] for n in range(full)]
            both, half = total[full * own_rows :], own_rows // 2
            blocks.append(jnp.concatenate([both[:half, :64], both[:half, 64:]], axis=0))
            total = jnp.concatenate(blocks, axis=1)
        for core in range(2):

            @pl.when(core_ref[0] == core)
            def _(core=core, total=total, x=x):
                for r in range(2):
                    for c in range(kinds):
                        at = (c * n_chip * 2 + 2 * x + (r ^ core)) * part
                        src = (r * kinds + c) * part
                        out_ref[:, at : at + part] = total[:, src : src + part]


def final_sum(pieces, core, own_rows, part, kinds):
    n_chip = pieces.shape[1]
    shape = (own_rows, 2 * n_chip * kinds * part)
    return pl.pallas_call(
        functools.partial(final_kernel, part=part, kinds=kinds),
        grid_spec=pltpu.PrefetchScalarGridSpec(
            num_scalar_prefetch=1,
            grid=(1,),
            in_specs=[whole_spec(pieces)],
            out_specs=pl.BlockSpec(shape, lambda i, s: (0, 0)),
        ),
        out_shape=jax.ShapeDtypeStruct(shape, F32),
        compiler_params=ROOM,
    )(core[None], pieces)


def per_device(tokens, ln_gain, ln_bias, w_qkv, w_out, q_time, k_time, v_time, grad_out):
    t_dev, patches, width = tokens.shape
    frames, columns, part = q_time.shape
    n_tm = lax.axis_size("tm")
    n_patch = lax.axis_size("patch")
    n_pair = n_tm // 2
    n_chip = n_patch // 2
    devices = n_tm * n_patch
    n_tok = frames * columns
    own_rows = width // devices
    tm = lax.axis_index("tm")
    patch = lax.axis_index("patch")
    side = tm % 2
    core = patch % 2
    both = ("tm", "patch")

    def swap(values, axis, size, bit):
        return lax.ppermute(values, axis, [(i, i ^ bit) for i in range(size)])

    grad_rows = grad_out.reshape(-1, width)
    d_attn = jnp.einsum(
        "to,jfo->jtf", grad_rows, w_out.reshape(n_patch, part, width), preferred_element_type=F32
    ).astype(BF)
    d_attn = d_attn.reshape(n_patch, t_dev, n_tm, columns, part).transpose(2, 0, 1, 3, 4)
    d_attn, token_rows, w_late = lax.optimization_barrier((d_attn, tokens.reshape(-1, width), w_qkv))
    d_time = lax.all_to_all(
        d_attn.reshape(devices, t_dev, columns, part), both, 0, 0, tiled=True
    ).reshape(n_tok, part)

    sent = norm_send(token_rows, ln_gain, ln_bias, n_pair, n_chip, columns, own_rows, t_dev)
    weights = own_weights(w_late, patch // 2, n_chip)
    d_time, sent, weights = lax.optimization_barrier((d_time, sent, weights))
    mine = lax.all_to_all(sent, both, 0, 0, tiled=True).reshape(n_tok, width // 4)
    theirs = swap(mine, "patch", n_patch, 2)

    saved = [values.reshape(n_tok, part) for values in (q_time, k_time, v_time)]
    grads, *others = attend(*saved, d_time, columns)
    grads_core = swap(grads, "patch", n_patch, 1)
    pieces = [grads, grads_core]
    others = [swap(piece, "tm", n_tm, 1) for piece in others]

    leave, stay = share_send(pieces, weights, patch, t_dev * columns)
    come = swap(leave, "patch", n_patch, 2)
    share = pl.pallas_call(
        add_kernel,
        in_specs=[pl.BlockSpec(memory_space=space) for space in (pltpu.HBM, pltpu.VMEM)],
        out_shape=jax.ShapeDtypeStruct(leave.shape, BF),
        scratch_shapes=[pltpu.VMEM(stay.shape, F32), pltpu.SemaphoreType.DMA(())],
        compiler_params=ROOM,
    )(pltpu.with_memory_space_constraint(stay, pltpu.HBM), come)
    share = share.reshape((n_pair, 2) + share.shape[1:])
    spread = [lax.dynamic_index_in_dim(share, (tm // 2) ^ n, 0, keepdims=False) for n in range(n_pair)]
    spread = spread[:1] + [swap(spread[n], "tm", n_tm, 2 * n) for n in range(1, n_pair)]
    own = own_product(patch // 2, mine, theirs, pieces)
    others, theirs, own, early = lax.optimization_barrier((others, theirs, own, spread[2:]))
    others = list(others)
    spread = spread[:2] + early
    others += [swap(piece, "patch", n_patch, 1) for piece in others]

    factor = 1.0 / math.sqrt(frames * patches)
    groups = [
        [(2 * z + y) * n_patch + 2 * x + c for z in range(n_pair) for x in range(n_chip)]
        for y in range(2)
        for c in range(2)
    ]
    partial = other_product(patch // 2, mine, theirs, own, others, own_rows, factor)
    partial, spread = lax.optimization_barrier((partial, spread))
    summands = lax.all_to_all(partial, both, 0, 0, axis_index_groups=groups, tiled=True)
    summands = summands.reshape((n_pair, n_chip) + summands.shape[1:])
    grad_w_qkv = final_sum(summands, core, own_rows, part, 3)

    spread = jnp.stack(spread)
    stay = lax.dynamic_index_in_dim(spread, side, 1, keepdims=False)
    come = swap(lax.dynamic_index_in_dim(spread, 1 - side, 1, keepdims=False), "tm", n_tm, 1)
    grad_x = last(stay, come, tokens.reshape(-1, width), grad_rows, ln_gain, tm, columns, t_dev)
    grad_x = grad_x.reshape(t_dev, patches, width)
    return (grad_x, grad_w_qkv)


def solution(mesh):
    return jax.shard_map(
        per_device,
        mesh=mesh,
        in_specs=(
            P(("tm", "patch"), None, None),
            P(),
            P(),
            P(),
            P(),
            P(None, "tm", "patch"),
            P(None, "tm", "patch"),
            P(None, "tm", "patch"),
            P(("tm", "patch"), None, None),
        ),
        out_specs=(P(("tm", "patch"), None, None), P(("tm", "patch"), None)),
        check_vma=False,
    )
```

```python
import functools
import math

import jax
import jax.numpy as jnp
from jax import lax
from jax.experimental import pallas as pl
from jax.experimental.pallas import tpu as pltpu
from jax.sharding import PartitionSpec as P

DH = 88
BF = jnp.bfloat16
F32 = jnp.float32
ROWS = (((0,), (0,)), ((), ()))
COLS = (((1,), (1,)), ((), ()))
CROSS = (((0,), (1,)), ((), ()))
ROOM = pltpu.CompilerParams(vmem_limit_bytes=28 * 1024 * 1024)


def attend_kernel(q_ref, k_ref, v_ref, d_ref, all_ref, query_ref, rest_ref, sem, *, columns):
    n_tok, width = q_ref.shape
    factor = 1.0 / math.sqrt(DH)
    key_row = lax.broadcasted_iota(jnp.int32, (n_tok, n_tok), 0)
    query_row = lax.broadcasted_iota(jnp.int32, (n_tok, n_tok), 1)
    same = ((key_row ^ query_row) & (columns - 1)) == 0
    copies = []
    for head, start in enumerate(range(0, width, DH)):
        lanes = slice(start, start + DH)
        query, key, value, grad = [ref[:, lanes] for ref in (q_ref, k_ref, v_ref, d_ref)]
        scores = lax.dot_general(key, query, COLS, preferred_element_type=F32) * factor
        scores = jnp.where(same, scores, -jnp.inf)
        exponent = jnp.exp(scores - jnp.max(scores, axis=0, keepdims=True))
        probability = exponent * (1.0 / jnp.sum(exponent, axis=0, keepdims=True))
        prob_grad = lax.dot_general(value, grad, COLS, preferred_element_type=F32)
        row_dot = jnp.sum(probability * prob_grad, axis=0, keepdims=True)
        score_grad = (probability * (prob_grad - row_dot) * factor).astype(BF)
        prob_low = probability.astype(BF)
        for kind, (left, right, dims) in enumerate(
            ((key, score_grad, ROWS), (query, score_grad, CROSS), (grad, prob_low, CROSS))
        ):
            total = lax.dot_general(left, right, dims, preferred_element_type=F32)
            all_ref[kind, lanes, :] = total.astype(BF)
        for at, ref in ((0, query_ref), (1, rest_ref)):
            source = all_ref.at[pl.ds(at, ref.shape[0]), pl.ds(start, DH)]
            copy = pltpu.make_async_copy(source, ref.at[:, pl.ds(start, DH)], sem.at[head, at])
            copy.start()
            copies.append(copy)
    for copy in copies:
        copy.wait()


def attend(query, key, value, grad, columns):
    n_tok, width = query.shape
    return pl.pallas_call(
        functools.partial(attend_kernel, columns=columns),
        out_specs=[pl.BlockSpec(memory_space=pltpu.VMEM)] + [pl.BlockSpec(memory_space=pltpu.HBM)] * 2,
        scratch_shapes=[pltpu.SemaphoreType.DMA((width // DH, 2))],
        out_shape=[jax.ShapeDtypeStruct((3, width, n_tok), BF)]
        + [pltpu.HBM((kinds, width, n_tok), BF) for kinds in (1, 2)],
        compiler_params=ROOM,
    )(query, key, value, grad)


def norm_kernel(x_ref, gain_ref, bias_ref, out_ref, *, n_pair, n_chip, columns, own_rows, t_dev):
    width = x_ref.shape[1]
    rows = x_ref[...].astype(F32)
    centered = rows - jnp.mean(rows, axis=-1, keepdims=True)
    variance = jnp.mean(centered * centered, axis=-1, keepdims=True)
    norm = centered * lax.rsqrt(variance + 1e-06) * gain_ref[...] + bias_ref[...]
    patches = x_ref.shape[0] // t_dev
    for y in range(2):
        for c in range(2):
            starts = [((2 * z + y) * n_chip + x) * 2 * own_rows + c * own_rows for z in range(n_pair) for x in range(n_chip)]
            part = jnp.concatenate([norm[:, s : s + own_rows] for s in starts], axis=1)
            for z in range(n_pair):
                for slot in range(2):
                    at = (2 * z + (y ^ slot)) * columns
                    piece = jnp.concatenate([part[t * patches + at : t * patches + at + columns] for t in range(t_dev)], axis=0).astype(BF)
                    out_ref[((2 * z + y) * 2 + slot) * 2 + c] = piece
def norm_send(tokens, gain, bias, n_pair, n_chip, columns, own_rows, t_dev):
    devices = 4 * n_pair * n_chip
    return pl.pallas_call(functools.partial(norm_kernel,n_pair=n_pair,n_chip=n_chip,columns=columns,own_rows=own_rows,t_dev=t_dev),
        out_shape=jax.ShapeDtypeStruct((devices,t_dev*columns,tokens.shape[1]//4),BF),compiler_params=ROOM)(tokens,gain[None],bias[None])

def weights_kernel(chip_ref, w_ref, out_ref, win_ref, sem, *, n_chip):
    kinds, width, part = out_ref.shape
    window = win_ref.shape[2]
    chip = chip_ref[0]
    starts = [min(part * j // 128 * 128, width - window) for j in range(n_chip)]
    start = sum(jnp.where(chip == j, at, 0) for j, at in enumerate(starts))
    copies = [
        pltpu.make_async_copy(
            w_ref.at[:, pl.ds(pl.multiple_of(c * width + start, 128), window)], win_ref.at[c], sem.at[c]
        )
        for c in range(kinds)
    ]
    for copy in copies:
        copy.start()
    for copy in copies:
        copy.wait()
    for j in range(n_chip):

        @pl.when(chip == j)
        def _(j=j):
            before = part * j - starts[j]
            for c in range(kinds):
                out_ref[c] = win_ref[c, :, before : before + part]


def own_weights(w_qkv, chip, n_chip):
    width = w_qkv.shape[0]
    kinds, part = w_qkv.shape[1] // width, width // n_chip
    window = -(-(part + 64) // 128) * 128
    return pl.pallas_call(
        functools.partial(weights_kernel, n_chip=n_chip),
        grid_spec=pltpu.PrefetchScalarGridSpec(
            num_scalar_prefetch=1,
            grid=(1,),
            in_specs=[pl.BlockSpec(memory_space=pl.ANY)],
            out_specs=pl.BlockSpec((kinds, width, part), lambda i, s: (0, 0, 0)),
            scratch_shapes=[
                pltpu.VMEM((kinds, width, window), BF),
                pltpu.SemaphoreType.DMA((kinds,)),
            ],
        ),
        out_shape=pltpu.HBM((kinds, width, part), BF),
        compiler_params=ROOM,
    )(chip[None], pltpu.with_memory_space_constraint(w_qkv, pltpu.HBM))


def share_kernel(where_ref, *refs):
    grads_refs, (w_hbm, leave_ref, stay_hbm, turn_ref, w_ref, stay_ref, sem) = refs[:2], refs[2:]
    copies = [
        pltpu.make_async_copy(w_hbm.at[c], w_ref.at[c], sem.at[c]) for c in range(w_ref.shape[0])
    ]
    for copy in copies:
        copy.start()
    patch = where_ref[0]
    chip, core = patch // 2, patch % 2
    kinds = w_ref.shape[0]
    part = w_ref.shape[2] // 2
    n, group, _ = leave_ref.shape
    for side in range(2):

        @pl.when(core == side)
        def _(side=side):
            for pieces, at in ((grads_refs[:1], side * part), (grads_refs[1:], (1 - side) * part)):
                for c, grads in enumerate(kinds_of(pieces)):
                    rows = grads.astype(F32).T.astype(BF)
                    turn_ref[c, :, :, :, :, at : at + part] = rows.reshape(n, 2, 2, group, part)

    total = None
    for c in range(kinds):
        copies[c].wait()
        rows = jnp.concatenate(
            [turn_ref[c, :, which, core].reshape(n * group, 2 * part) for which in (1 - chip, chip)],
            axis=0,
        )
        one = lax.dot_general(rows, w_ref[c], COLS, preferred_element_type=F32)
        total = one if total is None else total + one
    stay_ref[...] = total[n * group :].reshape(stay_ref.shape)
    copy = pltpu.make_async_copy(stay_ref, stay_hbm, sem.at[kinds])
    copy.start()
    leave_ref[...] = total[: n * group].reshape(leave_ref.shape).astype(BF)
    copy.wait()


def kinds_of(refs):
    return [ref[i] for ref in refs for i in range(ref.shape[0])]


def whole_spec(array):
    return pl.BlockSpec(array.shape, lambda i, s: (0,) * array.ndim)


def share_send(pieces, weights, patch, group):
    kinds, width, double = weights.shape
    n = pieces[0].shape[-1] // (4 * group)
    return pl.pallas_call(
        share_kernel,
        grid_spec=pltpu.PrefetchScalarGridSpec(
            num_scalar_prefetch=1,
            grid=(1,),
            in_specs=[whole_spec(array) for array in pieces] + [pl.BlockSpec(memory_space=pltpu.HBM)],
            out_specs=[
                pl.BlockSpec((n, group, width), lambda i, s: (0, 0, 0)),
                pl.BlockSpec(memory_space=pltpu.HBM),
            ],
            scratch_shapes=[
                pltpu.VMEM((kinds, n, 2, 2, group, double), BF),
                pltpu.VMEM((kinds, width, double), BF),
                pltpu.VMEM((n, group, width), F32),
                pltpu.SemaphoreType.DMA((kinds + 1,)),
            ],
        ),
        out_shape=[
            jax.ShapeDtypeStruct((n, group, width), BF),
            pltpu.HBM((n, group, width), F32),
        ],
        compiler_params=ROOM,
    )(patch[None], *pieces, pltpu.with_memory_space_constraint(weights, pltpu.HBM))


def add_kernel(stay_hbm, come_ref, out_ref, stay_ref, sem):
    copy = pltpu.make_async_copy(stay_hbm, stay_ref, sem)
    copy.start()
    copy.wait()
    out_ref[...] = (stay_ref[...] + come_ref[...].astype(F32)).astype(BF)


def own_kernel(chip_ref, mine_ref, theirs_ref, *refs):
    norm = jnp.where(chip_ref[0] == 0, mine_ref[...], theirs_ref[...])
    part = refs[0].shape[1]
    for i, grads in enumerate(kinds_of(refs[:-1])):
        refs[-1][i * part : (i + 1) * part, :] = jnp.dot(grads, norm, preferred_element_type=F32)


def own_product(chip, mine, theirs, pieces):
    part = mine.shape[1]
    rows = part * sum(piece.shape[0] for piece in pieces)
    arrays = (mine, theirs, *pieces)
    return pl.pallas_call(
        own_kernel,
        grid_spec=pltpu.PrefetchScalarGridSpec(
            num_scalar_prefetch=1,
            grid=(1,),
            in_specs=[whole_spec(array) for array in arrays],
            out_specs=pl.BlockSpec((rows, part), lambda i, s: (0, 0)),
        ),
        out_shape=jax.ShapeDtypeStruct((rows, part), F32),
        compiler_params=ROOM,
    )(chip[None], *arrays)


def other_kernel(chip_ref, mine_ref, theirs_ref, acc_ref, *refs, factor, own_rows, relative):
    pieces, (out_ref, sum_ref) = refs[:-2], refs[-2:]
    norm = jnp.where(chip_ref[0] == 0, theirs_ref[...], mine_ref[...])
    part = pieces[0].shape[1]
    for i, grads in enumerate(kinds_of(pieces)):
        rows = slice(i * part, (i + 1) * part)
        total = acc_ref[rows, :] + jnp.dot(grads, norm, preferred_element_type=F32)
        sum_ref[rows, :] = total * factor
    full, left = divmod(sum_ref.shape[0], 128)
    packed = len(out_ref.shape) == 3 and out_ref.shape[2] == 128
    for n in range(full + (left > 0)):
        block = sum_ref[n * 128 : (n + 1) * 128, :].T if n < full else sum_ref[n * 128 :, :].T
        for k in range(out_ref.shape[0]):
            rows = block[k * own_rows : (k + 1) * own_rows].astype(BF)
            to = ((k // 2) ^ chip_ref[1]) * 2 + ((k % 2) ^ chip_ref[0]) if relative else k
            if not packed:
                out_ref[to, :, n * 128 : n * 128 + rows.shape[1]] = rows
            elif n < full:
                out_ref[to, n * own_rows : (n + 1) * own_rows, :] = rows
            else:
                rows = block[k * own_rows : (k + 1) * own_rows]
                both = jnp.concatenate([rows[: own_rows // 2], rows[own_rows // 2 :]], axis=1)
                out_ref[to, n * own_rows :, :] = both.astype(BF)


def packable(own_rows, lanes):
    return own_rows % 4 == 0 and lanes % 128 == 64


def other_product(place, mine, theirs, acc, pieces, own_rows, factor, relative):
    lanes, part = acc.shape
    chunk = (own_rows * lanes // 128, 128) if packable(own_rows, lanes) else (own_rows, lanes)
    shape = (part // own_rows,) + chunk
    arrays = (mine, theirs, acc, *pieces)
    return pl.pallas_call(
        functools.partial(other_kernel, factor=factor, own_rows=own_rows, relative=relative),
        grid_spec=pltpu.PrefetchScalarGridSpec(
            num_scalar_prefetch=1,
            grid=(1,),
            in_specs=[whole_spec(array) for array in arrays],
            out_specs=pl.BlockSpec(shape, lambda i, s: (0, 0, 0)),
            scratch_shapes=[pltpu.VMEM((lanes, part), F32)],
        ),
        out_shape=jax.ShapeDtypeStruct(shape, BF),
        compiler_params=ROOM,
    )(place, *arrays)


def last_kernel(tm_ref, stay_ref, come_ref, x_ref, grad_ref, gain_ref, out_ref, *, columns, t_dev):
    n_pair, group, width = stay_ref.shape
    patches = x_ref.shape[0] // t_dev
    tm = tm_ref[0]
    first = tm % 2 == 0
    for z in range(n_pair):
        slot = (tm // 2) ^ z
        stay, come = stay_ref[slot].astype(F32), come_ref[slot].astype(F32)
        for y in range(2):
            d_norm = jnp.where(first == (y == 0), stay, come)
            for t in range(t_dev):
                at = t * patches + (2 * z + y) * columns
                rows = slice(at, at + columns)
                tokens = x_ref[rows, :].astype(F32)
                centered = tokens - jnp.mean(tokens, axis=-1, keepdims=True)
                variance = jnp.mean(centered * centered, axis=-1, keepdims=True)
                inverse = lax.rsqrt(variance + 1e-06)
                normed = centered * inverse
                scaled = d_norm[t * columns : (t + 1) * columns] * gain_ref[...]
                branch = inverse * (
                    scaled
                    - jnp.mean(scaled, axis=-1, keepdims=True)
                    - normed * jnp.mean(scaled * normed, axis=-1, keepdims=True)
                )
                out_ref[rows, :] = (grad_ref[rows, :].astype(F32) + branch).astype(BF)


def last(stay, come, tokens, grads, gain, tm, columns, t_dev):
    n_rows, width = tokens.shape
    part = pl.BlockSpec(stay.shape, lambda i, s: (0, 0, 0))
    rows = pl.BlockSpec((n_rows, width), lambda i, s: (0, 0))
    return pl.pallas_call(
        functools.partial(last_kernel, columns=columns, t_dev=t_dev),
        grid_spec=pltpu.PrefetchScalarGridSpec(
            num_scalar_prefetch=1,
            grid=(1,),
            in_specs=[part, part, rows, rows, pl.BlockSpec((1, width), lambda i, s: (0, 0))],
            out_specs=rows,
        ),
        out_shape=jax.ShapeDtypeStruct((n_rows, width), BF),
        compiler_params=ROOM,
    )(tm[None], stay, come, tokens, grads, gain[None])


def final_kernel(place_ref, *refs, part, kinds, n_chip):
    out_ref = refs[-1]
    own_rows = out_ref.shape[0]
    lanes = 2 * kinds * part
    count = (len(refs) - 1) // n_chip
    for x in range(n_chip):
        total = None
        for ref in refs[x * count : (x + 1) * count]:
            values = ref[...].astype(F32)
            total = values if total is None else total + values
        if packable(own_rows, lanes):
            full = lanes // 128
            blocks = [total[n * own_rows : (n + 1) * own_rows] for n in range(full)]
            both, half = total[full * own_rows :], own_rows // 2
            blocks.append(jnp.concatenate([both[:half, :64], both[:half, 64:]], axis=0))
            total = jnp.concatenate(blocks, axis=1)
        for core in range(2):
            for first in range(2):

                @pl.when((place_ref[0] == core) & (place_ref[1] == first))
                def _(core=core, first=first, total=total, x=x):
                    for r in range(2):
                        for c in range(kinds):
                            at = (c * n_chip * 2 + 2 * (x ^ first) + (r ^ core)) * part
                            src = (r * kinds + c) * part
                            out_ref[:, at : at + part] = total[:, src : src + part]


def final_sum(arrays, core, first, own_rows, part, kinds, n_chip):
    shape = (own_rows, 2 * n_chip * kinds * part)
    return pl.pallas_call(
        functools.partial(final_kernel, part=part, kinds=kinds, n_chip=n_chip),
        grid_spec=pltpu.PrefetchScalarGridSpec(
            num_scalar_prefetch=1,
            grid=(1,),
            in_specs=[whole_spec(array) for array in arrays],
            out_specs=pl.BlockSpec(shape, lambda i, s: (0, 0)),
        ),
        out_shape=jax.ShapeDtypeStruct(shape, F32),
        compiler_params=ROOM,
    )(jnp.stack([core, first]), *arrays)


def per_device(tokens, ln_gain, ln_bias, w_qkv, w_out, q_time, k_time, v_time, grad_out):
    t_dev, patches, width = tokens.shape
    frames, columns, part = q_time.shape
    n_tm = lax.axis_size("tm")
    n_patch = lax.axis_size("patch")
    n_pair = n_tm // 2
    n_chip = n_patch // 2
    devices = n_tm * n_patch
    n_tok = frames * columns
    own_rows = width // devices
    tm = lax.axis_index("tm")
    patch = lax.axis_index("patch")
    side = tm % 2
    core = patch % 2
    both = ("tm", "patch")

    def swap(values, axis, size, bit):
        return lax.ppermute(values, axis, [(i, i ^ bit) for i in range(size)])

    grad_rows = grad_out.reshape(-1, width)
    d_attn = jnp.einsum(
        "to,jfo->jtf", grad_rows, w_out.reshape(n_patch, part, width), preferred_element_type=F32
    ).astype(BF)
    d_attn = d_attn.reshape(n_patch, t_dev, n_tm, columns, part).transpose(2, 0, 1, 3, 4)
    d_attn, token_rows, w_late = lax.optimization_barrier((d_attn, tokens.reshape(-1, width), w_qkv))
    d_time = lax.all_to_all(
        d_attn.reshape(devices, t_dev, columns, part), both, 0, 0, tiled=True
    ).reshape(n_tok, part)

    sent = norm_send(token_rows, ln_gain, ln_bias, n_pair, n_chip, columns, own_rows, t_dev)
    weights = own_weights(w_late, patch // 2, n_chip)
    d_time, sent, weights = lax.optimization_barrier((d_time, sent, weights))
    mine = lax.all_to_all(sent, both, 0, 0, tiled=True).reshape(n_tok, width // 4)
    theirs = swap(mine, "patch", n_patch, 2)

    saved = [values.reshape(n_tok, part) for values in (q_time, k_time, v_time)]
    grads, *others = attend(*saved, d_time, columns)
    grads_core = swap(grads, "patch", n_patch, 1)
    pieces = [grads, grads_core]
    others = [swap(piece, "tm", n_tm, 1) for piece in others]

    leave, stay = share_send(pieces, weights, patch, t_dev * columns)
    come = swap(leave, "patch", n_patch, 2)
    share = pl.pallas_call(
        add_kernel,
        in_specs=[pl.BlockSpec(memory_space=space) for space in (pltpu.HBM, pltpu.VMEM)],
        out_shape=jax.ShapeDtypeStruct(leave.shape, BF),
        scratch_shapes=[pltpu.VMEM(stay.shape, F32), pltpu.SemaphoreType.DMA(())],
        compiler_params=ROOM,
    )(pltpu.with_memory_space_constraint(stay, pltpu.HBM), come)
    share = share.reshape((n_pair, 2) + share.shape[1:])
    spread = [lax.dynamic_index_in_dim(share, (tm // 2) ^ n, 0, keepdims=False) for n in range(n_pair)]
    spread = spread[:1] + [swap(spread[n], "tm", n_tm, 2 * n) for n in range(1, n_pair)]
    own = own_product(patch // 2, mine, theirs, pieces)
    others, theirs, own, early = lax.optimization_barrier((others, theirs, own, spread[2:]))
    others = list(others)
    spread = spread[:2] + early
    others += [swap(piece, "patch", n_patch, 1) for piece in others]

    factor = 1.0 / math.sqrt(frames * patches)
    across = n_pair == 4 and n_chip == 2
    place = jnp.stack([patch // 2, tm // 2])
    partial = other_product(place, mine, theirs, own, others, own_rows, factor, across)
    partial, spread = lax.optimization_barrier((partial, spread))
    if across:
        def send(values, dz, dx):
            flip = 2 * dz * n_patch + 2 * dx
            return lax.ppermute(values, both, [(i, i ^ flip) for i in range(devices)])

        passed = send(partial[6:8], 1, 0)
        summed = (partial[4:6].astype(F32) + passed.astype(F32)).astype(BF)
        own_chip = [partial[0], send(partial[2], 1, 0), send(summed[0], 2, 0)]
        other_chip = [send(partial[1], 0, 1), send(partial[3], 1, 1), send(summed[1], 2, 1)]
        summands, first = own_chip + other_chip, patch // 2
    else:
        groups = [
            [(2 * z + y) * n_patch + 2 * x + c for z in range(n_pair) for x in range(n_chip)]
            for y in range(2)
            for c in range(2)
        ]
        pieces = lax.all_to_all(partial, both, 0, 0, axis_index_groups=groups, tiled=True)
        summands = [pieces[z * n_chip + x] for x in range(n_chip) for z in range(n_pair)]
        first = 0 * core
    grad_w_qkv = final_sum(summands, core, first, own_rows, part, 3, n_chip)

    spread = jnp.stack(spread)
    stay = lax.dynamic_index_in_dim(spread, side, 1, keepdims=False)
    come = swap(lax.dynamic_index_in_dim(spread, 1 - side, 1, keepdims=False), "tm", n_tm, 1)
    grad_x = last(stay, come, tokens.reshape(-1, width), grad_rows, ln_gain, tm, columns, t_dev)
    grad_x = grad_x.reshape(t_dev, patches, width)
    return (grad_x, grad_w_qkv)


def solution(mesh):
    return jax.shard_map(
        per_device,
        mesh=mesh,
        in_specs=(
            P(("tm", "patch"), None, None),
            P(),
            P(),
            P(),
            P(),
            P(None, "tm", "patch"),
            P(None, "tm", "patch"),
            P(None, "tm", "patch"),
            P(("tm", "patch"), None, None),
        ),
        out_specs=(P(("tm", "patch"), None, None), P(("tm", "patch"), None)),
        check_vma=False,
    )
```

```python
import functools
import math

import jax
import jax.numpy as jnp
from jax import lax
from jax.experimental import pallas as pl
from jax.experimental.pallas import tpu as pltpu
from jax.sharding import PartitionSpec as P

DH = 88
BF = jnp.bfloat16
F32 = jnp.float32
ROWS = (((0,), (0,)), ((), ()))
COLS = (((1,), (1,)), ((), ()))
CROSS = (((0,), (1,)), ((), ()))
ROOM = pltpu.CompilerParams(vmem_limit_bytes=28 * 1024 * 1024)


def attend_kernel(q_ref, k_ref, v_ref, d_ref, all_ref, query_ref, rest_ref, sem, *, columns):
    n_tok, width = q_ref.shape
    factor = 1.0 / math.sqrt(DH)
    key_row = lax.broadcasted_iota(jnp.int32, (n_tok, n_tok), 0)
    query_row = lax.broadcasted_iota(jnp.int32, (n_tok, n_tok), 1)
    same = ((key_row ^ query_row) & (columns - 1)) == 0
    copies = []
    for head, start in enumerate(range(0, width, DH)):
        lanes = slice(start, start + DH)
        query, key, value, grad = [ref[:, lanes] for ref in (q_ref, k_ref, v_ref, d_ref)]
        scores = lax.dot_general(key, query, COLS, preferred_element_type=F32) * factor
        scores = jnp.where(same, scores, -jnp.inf)
        exponent = jnp.exp(scores - jnp.max(scores, axis=0, keepdims=True))
        probability = exponent * (1.0 / jnp.sum(exponent, axis=0, keepdims=True))
        prob_grad = lax.dot_general(value, grad, COLS, preferred_element_type=F32)
        row_dot = jnp.sum(probability * prob_grad, axis=0, keepdims=True)
        score_grad = (probability * (prob_grad - row_dot) * factor).astype(BF)
        prob_low = probability.astype(BF)
        for kind, (left, right, dims) in enumerate(
            ((key, score_grad, ROWS), (query, score_grad, CROSS), (grad, prob_low, CROSS))
        ):
            total = lax.dot_general(left, right, dims, preferred_element_type=F32)
            all_ref[kind, lanes, :] = total.astype(BF)
        for at, ref in ((0, query_ref), (1, rest_ref)):
            source = all_ref.at[pl.ds(at, ref.shape[0]), pl.ds(start, DH)]
            copy = pltpu.make_async_copy(source, ref.at[:, pl.ds(start, DH)], sem.at[head, at])
            copy.start()
            copies.append(copy)
    for copy in copies:
        copy.wait()


def attend(query, key, value, grad, columns):
    n_tok, width = query.shape
    return pl.pallas_call(
        functools.partial(attend_kernel, columns=columns),
        out_specs=[pl.BlockSpec(memory_space=pltpu.VMEM)] + [pl.BlockSpec(memory_space=pltpu.HBM)] * 2,
        scratch_shapes=[pltpu.SemaphoreType.DMA((width // DH, 2))],
        out_shape=[jax.ShapeDtypeStruct((3, width, n_tok), BF)]
        + [pltpu.HBM((kinds, width, n_tok), BF) for kinds in (1, 2)],
        compiler_params=ROOM,
    )(query, key, value, grad)


def norm_kernel(x_ref, gain_ref, bias_ref, out_ref, *, n_pair, n_chip, columns, own_rows, t_dev):
    width = x_ref.shape[1]
    rows = x_ref[...].astype(F32)
    centered = rows - jnp.mean(rows, axis=-1, keepdims=True)
    variance = jnp.mean(centered * centered, axis=-1, keepdims=True)
    norm = centered * lax.rsqrt(variance + 1e-06) * gain_ref[...] + bias_ref[...]
    patches = x_ref.shape[0] // t_dev
    for y in range(2):
        for c in range(2):
            starts = [((2 * z + y) * n_chip + x) * 2 * own_rows + c * own_rows for z in range(n_pair) for x in range(n_chip)]
            part = jnp.concatenate([norm[:, s : s + own_rows] for s in starts], axis=1)
            for z in range(n_pair):
                for slot in range(2):
                    at = (2 * z + (y ^ slot)) * columns
                    piece = jnp.concatenate([part[t * patches + at : t * patches + at + columns] for t in range(t_dev)], axis=0).astype(BF)
                    out_ref[((2 * z + y) * 2 + slot) * 2 + c] = piece
def norm_send(tokens, gain, bias, n_pair, n_chip, columns, own_rows, t_dev):
    devices = 4 * n_pair * n_chip
    return pl.pallas_call(functools.partial(norm_kernel,n_pair=n_pair,n_chip=n_chip,columns=columns,own_rows=own_rows,t_dev=t_dev),
        out_shape=jax.ShapeDtypeStruct((devices,t_dev*columns,tokens.shape[1]//4),BF),compiler_params=ROOM)(tokens,gain[None],bias[None])

def weights_kernel(chip_ref, w_ref, out_ref, win_ref, sem, *, n_chip):
    kinds, width, part = out_ref.shape
    window = win_ref.shape[2]
    chip = chip_ref[0]
    starts = [min(part * j // 128 * 128, width - window) for j in range(n_chip)]
    start = sum(jnp.where(chip == j, at, 0) for j, at in enumerate(starts))
    copies = [
        pltpu.make_async_copy(
            w_ref.at[:, pl.ds(pl.multiple_of(c * width + start, 128), window)], win_ref.at[c], sem.at[c]
        )
        for c in range(kinds)
    ]
    for copy in copies:
        copy.start()
    for copy in copies:
        copy.wait()
    for j in range(n_chip):

        @pl.when(chip == j)
        def _(j=j):
            before = part * j - starts[j]
            for c in range(kinds):
                out_ref[c] = win_ref[c, :, before : before + part]


def own_weights(w_qkv, chip, n_chip):
    width = w_qkv.shape[0]
    kinds, part = w_qkv.shape[1] // width, width // n_chip
    window = -(-(part + 64) // 128) * 128
    return pl.pallas_call(
        functools.partial(weights_kernel, n_chip=n_chip),
        grid_spec=pltpu.PrefetchScalarGridSpec(
            num_scalar_prefetch=1,
            grid=(1,),
            in_specs=[pl.BlockSpec(memory_space=pl.ANY)],
            out_specs=pl.BlockSpec((kinds, width, part), lambda i, s: (0, 0, 0)),
            scratch_shapes=[
                pltpu.VMEM((kinds, width, window), BF),
                pltpu.SemaphoreType.DMA((kinds,)),
            ],
        ),
        out_shape=pltpu.HBM((kinds, width, part), BF),
        compiler_params=ROOM,
    )(chip[None], pltpu.with_memory_space_constraint(w_qkv, pltpu.HBM))


def share_kernel(where_ref, *refs):
    grads_refs, (w_hbm, leave_ref, stay_hbm, turn_ref, w_ref, stay_ref, sem) = refs[:2], refs[2:]
    copies = [
        pltpu.make_async_copy(w_hbm.at[c], w_ref.at[c], sem.at[c]) for c in range(w_ref.shape[0])
    ]
    for copy in copies:
        copy.start()
    patch = where_ref[0]
    chip, core = patch // 2, patch % 2
    kinds = w_ref.shape[0]
    part = w_ref.shape[2] // 2
    n, group, _ = leave_ref.shape
    for side in range(2):

        @pl.when(core == side)
        def _(side=side):
            for pieces, at in ((grads_refs[:1], side * part), (grads_refs[1:], (1 - side) * part)):
                for c, grads in enumerate(kinds_of(pieces)):
                    rows = grads.astype(F32).T.astype(BF)
                    turn_ref[c, :, :, :, :, at : at + part] = rows.reshape(n, 2, 2, group, part)

    total = None
    for c in range(kinds):
        copies[c].wait()
        rows = jnp.concatenate(
            [turn_ref[c, :, which, core].reshape(n * group, 2 * part) for which in (1 - chip, chip)],
            axis=0,
        )
        one = lax.dot_general(rows, w_ref[c], COLS, preferred_element_type=F32)
        total = one if total is None else total + one
    stay_ref[...] = total[n * group :].reshape(stay_ref.shape)
    copy = pltpu.make_async_copy(stay_ref, stay_hbm, sem.at[kinds])
    copy.start()
    leave_ref[...] = total[: n * group].reshape(leave_ref.shape).astype(BF)
    copy.wait()


def kinds_of(refs):
    return [ref[i] for ref in refs for i in range(ref.shape[0])]


def whole_spec(array):
    return pl.BlockSpec(array.shape, lambda i, s: (0,) * array.ndim)


def share_send(pieces, weights, patch, group):
    kinds, width, double = weights.shape
    n = pieces[0].shape[-1] // (4 * group)
    return pl.pallas_call(
        share_kernel,
        grid_spec=pltpu.PrefetchScalarGridSpec(
            num_scalar_prefetch=1,
            grid=(1,),
            in_specs=[whole_spec(array) for array in pieces] + [pl.BlockSpec(memory_space=pltpu.HBM)],
            out_specs=[
                pl.BlockSpec((n, group, width), lambda i, s: (0, 0, 0)),
                pl.BlockSpec(memory_space=pltpu.HBM),
            ],
            scratch_shapes=[
                pltpu.VMEM((kinds, n, 2, 2, group, double), BF),
                pltpu.VMEM((kinds, width, double), BF),
                pltpu.VMEM((n, group, width), F32),
                pltpu.SemaphoreType.DMA((kinds + 1,)),
            ],
        ),
        out_shape=[
            jax.ShapeDtypeStruct((n, group, width), BF),
            pltpu.HBM((n, group, width), F32),
        ],
        compiler_params=ROOM,
    )(patch[None], *pieces, pltpu.with_memory_space_constraint(weights, pltpu.HBM))


def add_kernel(stay_hbm, come_ref, out_ref, stay_ref, sem):
    copy = pltpu.make_async_copy(stay_hbm, stay_ref, sem)
    copy.start()
    copy.wait()
    out_ref[...] = (stay_ref[...] + come_ref[...].astype(F32)).astype(BF)


def own_kernel(chip_ref, mine_ref, theirs_ref, *refs):
    norm = jnp.where(chip_ref[0] == 0, mine_ref[...], theirs_ref[...])
    part = refs[0].shape[1]
    for i, grads in enumerate(kinds_of(refs[:-1])):
        refs[-1][i * part : (i + 1) * part, :] = jnp.dot(grads, norm, preferred_element_type=F32)


def own_product(chip, mine, theirs, pieces):
    part = mine.shape[1]
    rows = part * sum(piece.shape[0] for piece in pieces)
    arrays = [pltpu.with_memory_space_constraint(x, pltpu.HBM) for x in (mine, theirs, *pieces)]
    return pl.pallas_call(
        own_kernel,
        grid_spec=pltpu.PrefetchScalarGridSpec(
            num_scalar_prefetch=1,
            grid=(1,),
            in_specs=[whole_spec(array) for array in arrays],
            out_specs=pl.BlockSpec((rows, part), lambda i, s: (0, 0)),
        ),
        out_shape=jax.ShapeDtypeStruct((rows, part), F32),
        compiler_params=ROOM,
    )(chip[None], *arrays)


def other_kernel(chip_ref, mine_ref, theirs_ref, acc_ref, *refs, factor, own_rows, relative):
    pieces, (out_ref, sum_ref) = refs[:-2], refs[-2:]
    norm = jnp.where(chip_ref[0] == 0, theirs_ref[...], mine_ref[...])
    part = pieces[0].shape[1]
    for i, grads in enumerate(kinds_of(pieces)):
        rows = slice(i * part, (i + 1) * part)
        total = acc_ref[rows, :] + jnp.dot(grads, norm, preferred_element_type=F32)
        sum_ref[rows, :] = total * factor
    full, left = divmod(sum_ref.shape[0], 128)
    packed = len(out_ref.shape) == 3 and out_ref.shape[2] == 128
    for n in range(full + (left > 0)):
        block = sum_ref[n * 128 : (n + 1) * 128, :].T if n < full else sum_ref[n * 128 :, :].T
        for k in range(out_ref.shape[0]):
            rows = block[k * own_rows : (k + 1) * own_rows].astype(BF)
            to = ((k // 2) ^ chip_ref[1]) * 2 + ((k % 2) ^ chip_ref[0]) if relative else k
            if not packed:
                out_ref[to, :, n * 128 : n * 128 + rows.shape[1]] = rows
            elif n < full:
                out_ref[to, n * own_rows : (n + 1) * own_rows, :] = rows
            else:
                rows = block[k * own_rows : (k + 1) * own_rows]
                both = jnp.concatenate([rows[: own_rows // 2], rows[own_rows // 2 :]], axis=1)
                out_ref[to, n * own_rows :, :] = both.astype(BF)


def packable(own_rows, lanes):
    return own_rows % 4 == 0 and lanes % 128 == 64


def other_product(place, mine, theirs, acc, pieces, own_rows, factor, relative):
    lanes, part = acc.shape
    chunk = (own_rows * lanes // 128, 128) if packable(own_rows, lanes) else (own_rows, lanes)
    shape = (part // own_rows,) + chunk
    mine, theirs = [pltpu.with_memory_space_constraint(x, pltpu.HBM) for x in (mine, theirs)]
    arrays = (mine, theirs, acc, *pieces)
    return pl.pallas_call(
        functools.partial(other_kernel, factor=factor, own_rows=own_rows, relative=relative),
        grid_spec=pltpu.PrefetchScalarGridSpec(
            num_scalar_prefetch=1,
            grid=(1,),
            in_specs=[whole_spec(array) for array in arrays],
            out_specs=pl.BlockSpec(shape, lambda i, s: (0, 0, 0)),
            scratch_shapes=[pltpu.VMEM((lanes, part), F32)],
        ),
        out_shape=jax.ShapeDtypeStruct(shape, BF),
        compiler_params=ROOM,
    )(place, *arrays)


def last_kernel(tm_ref, stay_ref, come_ref, x_ref, grad_ref, gain_ref, out_ref, *, columns, t_dev):
    n_pair, group, width = stay_ref.shape
    patches = x_ref.shape[0] // t_dev
    tm = tm_ref[0]
    first = tm % 2 == 0
    for z in range(n_pair):
        slot = (tm // 2) ^ z
        stay, come = stay_ref[slot].astype(F32), come_ref[slot].astype(F32)
        for y in range(2):
            d_norm = jnp.where(first == (y == 0), stay, come)
            for t in range(t_dev):
                at = t * patches + (2 * z + y) * columns
                rows = slice(at, at + columns)
                tokens = x_ref[rows, :].astype(F32)
                centered = tokens - jnp.mean(tokens, axis=-1, keepdims=True)
                variance = jnp.mean(centered * centered, axis=-1, keepdims=True)
                inverse = lax.rsqrt(variance + 1e-06)
                normed = centered * inverse
                scaled = d_norm[t * columns : (t + 1) * columns] * gain_ref[...]
                branch = inverse * (
                    scaled
                    - jnp.mean(scaled, axis=-1, keepdims=True)
                    - normed * jnp.mean(scaled * normed, axis=-1, keepdims=True)
                )
                out_ref[rows, :] = (grad_ref[rows, :].astype(F32) + branch).astype(BF)


def last(stay, come, tokens, grads, gain, tm, columns, t_dev):
    n_rows, width = tokens.shape
    part = pl.BlockSpec(stay.shape, lambda i, s: (0, 0, 0))
    rows = pl.BlockSpec((n_rows, width), lambda i, s: (0, 0))
    return pl.pallas_call(
        functools.partial(last_kernel, columns=columns, t_dev=t_dev),
        grid_spec=pltpu.PrefetchScalarGridSpec(
            num_scalar_prefetch=1,
            grid=(1,),
            in_specs=[part, part, rows, rows, pl.BlockSpec((1, width), lambda i, s: (0, 0))],
            out_specs=rows,
        ),
        out_shape=jax.ShapeDtypeStruct((n_rows, width), BF),
        compiler_params=ROOM,
    )(tm[None], stay, come, tokens, grads, gain[None])


def final_kernel(place_ref, *refs, part, kinds, n_chip):
    out_ref = refs[-1]
    own_rows = out_ref.shape[0]
    lanes = 2 * kinds * part
    count = (len(refs) - 1) // n_chip
    for x in range(n_chip):
        total = None
        for ref in refs[x * count : (x + 1) * count]:
            values = ref[...].astype(F32)
            total = values if total is None else total + values
        if packable(own_rows, lanes):
            full = lanes // 128
            blocks = [total[n * own_rows : (n + 1) * own_rows] for n in range(full)]
            both, half = total[full * own_rows :], own_rows // 2
            blocks.append(jnp.concatenate([both[:half, :64], both[:half, 64:]], axis=0))
            total = jnp.concatenate(blocks, axis=1)
        for core in range(2):
            for first in range(2):

                @pl.when((place_ref[0] == core) & (place_ref[1] == first))
                def _(core=core, first=first, total=total, x=x):
                    for r in range(2):
                        for c in range(kinds):
                            at = (c * n_chip * 2 + 2 * (x ^ first) + (r ^ core)) * part
                            src = (r * kinds + c) * part
                            out_ref[:, at : at + part] = total[:, src : src + part]


def final_sum(arrays, core, first, own_rows, part, kinds, n_chip):
    shape = (own_rows, 2 * n_chip * kinds * part)
    return pl.pallas_call(
        functools.partial(final_kernel, part=part, kinds=kinds, n_chip=n_chip),
        grid_spec=pltpu.PrefetchScalarGridSpec(
            num_scalar_prefetch=1,
            grid=(1,),
            in_specs=[whole_spec(array) for array in arrays],
            out_specs=pl.BlockSpec(shape, lambda i, s: (0, 0)),
        ),
        out_shape=jax.ShapeDtypeStruct(shape, F32),
        compiler_params=ROOM,
    )(jnp.stack([core, first]), *arrays)


def per_device(tokens, ln_gain, ln_bias, w_qkv, w_out, q_time, k_time, v_time, grad_out):
    t_dev, patches, width = tokens.shape
    frames, columns, part = q_time.shape
    n_tm = lax.axis_size("tm")
    n_patch = lax.axis_size("patch")
    n_pair = n_tm // 2
    n_chip = n_patch // 2
    devices = n_tm * n_patch
    n_tok = frames * columns
    own_rows = width // devices
    tm = lax.axis_index("tm")
    patch = lax.axis_index("patch")
    side = tm % 2
    core = patch % 2
    both = ("tm", "patch")

    def swap(values, axis, size, bit):
        return lax.ppermute(values, axis, [(i, i ^ bit) for i in range(size)])

    grad_rows = grad_out.reshape(-1, width)
    d_attn = jnp.einsum(
        "to,jfo->jtf", grad_rows, w_out.reshape(n_patch, part, width), preferred_element_type=F32
    ).astype(BF)
    d_attn = d_attn.reshape(n_patch, t_dev, n_tm, columns, part).transpose(2, 0, 1, 3, 4)
    d_attn, token_rows, w_late = lax.optimization_barrier((d_attn, tokens.reshape(-1, width), w_qkv))
    d_time = lax.all_to_all(
        d_attn.reshape(devices, t_dev, columns, part), both, 0, 0, tiled=True
    ).reshape(n_tok, part)

    sent = norm_send(token_rows, ln_gain, ln_bias, n_pair, n_chip, columns, own_rows, t_dev)
    weights = own_weights(w_late, patch // 2, n_chip)
    d_time, sent, weights = lax.optimization_barrier((d_time, sent, weights))
    mine = lax.all_to_all(sent, both, 0, 0, tiled=True).reshape(n_tok, width // 4)
    theirs = swap(mine, "patch", n_patch, 2)

    saved = [values.reshape(n_tok, part) for values in (q_time, k_time, v_time)]
    grads, *others = attend(*saved, d_time, columns)
    grads_core = swap(grads, "patch", n_patch, 1)
    pieces = [grads, grads_core]
    others = [swap(piece, "tm", n_tm, 1) for piece in others]

    leave, stay = share_send(pieces, weights, patch, t_dev * columns)
    come = swap(leave, "patch", n_patch, 2)
    share = pl.pallas_call(
        add_kernel,
        in_specs=[pl.BlockSpec(memory_space=space) for space in (pltpu.HBM, pltpu.VMEM)],
        out_shape=jax.ShapeDtypeStruct(leave.shape, BF),
        scratch_shapes=[pltpu.VMEM(stay.shape, F32), pltpu.SemaphoreType.DMA(())],
        compiler_params=ROOM,
    )(pltpu.with_memory_space_constraint(stay, pltpu.HBM), come)
    share = share.reshape((n_pair, 2) + share.shape[1:])
    spread = [lax.dynamic_index_in_dim(share, (tm // 2) ^ n, 0, keepdims=False) for n in range(n_pair)]
    spread = spread[:1] + [swap(spread[n], "tm", n_tm, 2 * n) for n in range(1, n_pair)]
    own = own_product(patch // 2, mine, theirs, pieces)
    others, theirs, own, early = lax.optimization_barrier((others, theirs, own, spread[2:]))
    others = list(others)
    spread = spread[:2] + early
    others += [swap(piece, "patch", n_patch, 1) for piece in others]

    factor = 1.0 / math.sqrt(frames * patches)
    across = n_pair == 4 and n_chip == 2
    place = jnp.stack([patch // 2, tm // 2])
    partial = other_product(place, mine, theirs, own, others, own_rows, factor, across)
    partial, spread = lax.optimization_barrier((partial, spread))
    if across:
        def send(values, dz, dx):
            flip = 2 * dz * n_patch + 2 * dx
            return lax.ppermute(values, both, [(i, i ^ flip) for i in range(devices)])

        passed = send(partial[6:8], 1, 0)
        summed = (partial[4:6].astype(F32) + passed.astype(F32)).astype(BF)
        own_chip = [partial[0], send(partial[2], 1, 0), send(summed[0], 2, 0)]
        other_chip = [send(partial[1], 0, 1), send(partial[3], 1, 1), send(summed[1], 2, 1)]
        summands, first = own_chip + other_chip, patch // 2
    else:
        groups = [
            [(2 * z + y) * n_patch + 2 * x + c for z in range(n_pair) for x in range(n_chip)]
            for y in range(2)
            for c in range(2)
        ]
        pieces = lax.all_to_all(partial, both, 0, 0, axis_index_groups=groups, tiled=True)
        summands = [pieces[z * n_chip + x] for x in range(n_chip) for z in range(n_pair)]
        first = 0 * core
    grad_w_qkv = final_sum(summands, core, first, own_rows, part, 3, n_chip)

    spread = jnp.stack(spread)
    stay = lax.dynamic_index_in_dim(spread, side, 1, keepdims=False)
    come = swap(lax.dynamic_index_in_dim(spread, 1 - side, 1, keepdims=False), "tm", n_tm, 1)
    grad_x = last(stay, come, tokens.reshape(-1, width), grad_rows, ln_gain, tm, columns, t_dev)
    grad_x = grad_x.reshape(t_dev, patches, width)
    return (grad_x, grad_w_qkv)


def solution(mesh):
    return jax.shard_map(
        per_device,
        mesh=mesh,
        in_specs=(
            P(("tm", "patch"), None, None),
            P(),
            P(),
            P(),
            P(),
            P(None, "tm", "patch"),
            P(None, "tm", "patch"),
            P(None, "tm", "patch"),
            P(("tm", "patch"), None, None),
        ),
        out_specs=(P(("tm", "patch"), None, None), P(("tm", "patch"), None)),
        check_vma=False,
    )
```

```python
import functools
import math

import jax
import jax.numpy as jnp
from jax import lax
from jax.experimental import pallas as pl
from jax.experimental.pallas import tpu as pltpu
from jax.sharding import PartitionSpec as P

DH = 88
BF = jnp.bfloat16
F32 = jnp.float32
ROWS = (((0,), (0,)), ((), ()))
COLS = (((1,), (1,)), ((), ()))
CROSS = (((0,), (1,)), ((), ()))
ROOM = pltpu.CompilerParams(vmem_limit_bytes=28 * 1024 * 1024)


def attend_kernel(q_ref, k_ref, v_ref, d_ref, all_ref, query_ref, rest_ref, sem, *, columns):
    n_tok, width = q_ref.shape
    factor = 1.0 / math.sqrt(DH)
    key_row = lax.broadcasted_iota(jnp.int32, (n_tok, n_tok), 0)
    query_row = lax.broadcasted_iota(jnp.int32, (n_tok, n_tok), 1)
    same = ((key_row ^ query_row) & (columns - 1)) == 0
    copies = []
    for head, start in enumerate(range(0, width, DH)):
        lanes = slice(start, start + DH)
        query, key, value, grad = [ref[:, lanes] for ref in (q_ref, k_ref, v_ref, d_ref)]
        scores = lax.dot_general(key, query, COLS, preferred_element_type=F32) * factor
        scores = jnp.where(same, scores, -jnp.inf)
        exponent = jnp.exp(scores - jnp.max(scores, axis=0, keepdims=True))
        probability = exponent * (1.0 / jnp.sum(exponent, axis=0, keepdims=True))
        prob_grad = lax.dot_general(value, grad, COLS, preferred_element_type=F32)
        row_dot = jnp.sum(probability * prob_grad, axis=0, keepdims=True)
        score_grad = (probability * (prob_grad - row_dot) * factor).astype(BF)
        prob_low = probability.astype(BF)
        for kind, (left, right, dims) in enumerate(
            ((key, score_grad, ROWS), (query, score_grad, CROSS), (grad, prob_low, CROSS))
        ):
            total = lax.dot_general(left, right, dims, preferred_element_type=F32)
            all_ref[kind, lanes, :] = total.astype(BF)
        for at, ref in ((0, query_ref), (1, rest_ref)):
            source = all_ref.at[pl.ds(at, ref.shape[0]), pl.ds(start, DH)]
            copy = pltpu.make_async_copy(source, ref.at[:, pl.ds(start, DH)], sem.at[head, at])
            copy.start()
            copies.append(copy)
    for copy in copies:
        copy.wait()


def attend(query, key, value, grad, columns):
    n_tok, width = query.shape
    return pl.pallas_call(
        functools.partial(attend_kernel, columns=columns),
        out_specs=[pl.BlockSpec(memory_space=pltpu.VMEM)] + [pl.BlockSpec(memory_space=pltpu.HBM)] * 2,
        scratch_shapes=[pltpu.SemaphoreType.DMA((width // DH, 2))],
        out_shape=[jax.ShapeDtypeStruct((3, width, n_tok), BF)]
        + [pltpu.HBM((kinds, width, n_tok), BF) for kinds in (1, 2)],
        compiler_params=ROOM,
    )(query, key, value, grad)


def norm_kernel(x_ref, gain_ref, bias_ref, out_ref, *, n_pair, n_chip, columns, own_rows, t_dev):
    width = x_ref.shape[1]
    rows = x_ref[...].astype(F32)
    centered = rows - jnp.mean(rows, axis=-1, keepdims=True)
    variance = jnp.mean(centered * centered, axis=-1, keepdims=True)
    norm = centered * lax.rsqrt(variance + 1e-06) * gain_ref[...] + bias_ref[...]
    patches = x_ref.shape[0] // t_dev
    for y in range(2):
        for c in range(2):
            starts = [((2 * z + y) * n_chip + x) * 2 * own_rows + c * own_rows for z in range(n_pair) for x in range(n_chip)]
            part = jnp.concatenate([norm[:, s : s + own_rows] for s in starts], axis=1)
            for z in range(n_pair):
                for slot in range(2):
                    at = (2 * z + (y ^ slot)) * columns
                    piece = jnp.concatenate([part[t * patches + at : t * patches + at + columns] for t in range(t_dev)], axis=0).astype(BF)
                    out_ref[((2 * z + y) * 2 + slot) * 2 + c] = piece
def norm_send(tokens, gain, bias, n_pair, n_chip, columns, own_rows, t_dev):
    devices = 4 * n_pair * n_chip
    return pl.pallas_call(functools.partial(norm_kernel,n_pair=n_pair,n_chip=n_chip,columns=columns,own_rows=own_rows,t_dev=t_dev),
        out_shape=jax.ShapeDtypeStruct((devices,t_dev*columns,tokens.shape[1]//4),BF),compiler_params=ROOM)(tokens,gain[None],bias[None])

def weights_kernel(chip_ref, w_ref, out_ref, win_ref, sem, *, n_chip):
    kinds, width, part = out_ref.shape
    window = win_ref.shape[2]
    chip = chip_ref[0]
    starts = [min(part * j // 128 * 128, width - window) for j in range(n_chip)]
    start = sum(jnp.where(chip == j, at, 0) for j, at in enumerate(starts))
    copies = [
        pltpu.make_async_copy(
            w_ref.at[:, pl.ds(pl.multiple_of(c * width + start, 128), window)], win_ref.at[c], sem.at[c]
        )
        for c in range(kinds)
    ]
    for copy in copies:
        copy.start()
    for copy in copies:
        copy.wait()
    for j in range(n_chip):

        @pl.when(chip == j)
        def _(j=j):
            before = part * j - starts[j]
            for c in range(kinds):
                out_ref[c] = win_ref[c, :, before : before + part]


def own_weights(w_qkv, chip, n_chip):
    width = w_qkv.shape[0]
    kinds, part = w_qkv.shape[1] // width, width // n_chip
    window = -(-(part + 64) // 128) * 128
    return pl.pallas_call(
        functools.partial(weights_kernel, n_chip=n_chip),
        grid_spec=pltpu.PrefetchScalarGridSpec(
            num_scalar_prefetch=1,
            grid=(1,),
            in_specs=[pl.BlockSpec(memory_space=pl.ANY)],
            out_specs=pl.BlockSpec((kinds, width, part), lambda i, s: (0, 0, 0)),
            scratch_shapes=[
                pltpu.VMEM((kinds, width, window), BF),
                pltpu.SemaphoreType.DMA((kinds,)),
            ],
        ),
        out_shape=pltpu.HBM((kinds, width, part), BF),
        compiler_params=ROOM,
    )(chip[None], pltpu.with_memory_space_constraint(w_qkv, pltpu.HBM))


def share_kernel(where_ref, *refs):
    grads_refs, (w_hbm, leave_ref, stay_hbm, turn_ref, w_ref, stay_ref, sem) = refs[:2], refs[2:]
    copies = [
        pltpu.make_async_copy(w_hbm.at[c], w_ref.at[c], sem.at[c]) for c in range(w_ref.shape[0])
    ]
    for copy in copies:
        copy.start()
    patch = where_ref[0]
    chip, core = patch // 2, patch % 2
    kinds = w_ref.shape[0]
    part = w_ref.shape[2] // 2
    n, group, _ = leave_ref.shape
    for side in range(2):

        @pl.when(core == side)
        def _(side=side):
            for pieces, at in ((grads_refs[:1], side * part), (grads_refs[1:], (1 - side) * part)):
                for c, grads in enumerate(kinds_of(pieces)):
                    rows = grads.astype(F32).T.astype(BF)
                    turn_ref[c, :, :, :, :, at : at + part] = rows.reshape(n, 2, 2, group, part)

    total = None
    for c in range(kinds):
        copies[c].wait()
        rows = jnp.concatenate(
            [turn_ref[c, :, which, core].reshape(n * group, 2 * part) for which in (1 - chip, chip)],
            axis=0,
        )
        one = lax.dot_general(rows, w_ref[c], COLS, preferred_element_type=F32)
        total = one if total is None else total + one
    stay_ref[...] = total[n * group :].reshape(stay_ref.shape)
    copy = pltpu.make_async_copy(stay_ref, stay_hbm, sem.at[kinds])
    copy.start()
    leave_ref[...] = total[: n * group].reshape(leave_ref.shape).astype(BF)
    copy.wait()


def kinds_of(refs):
    return [ref[i] for ref in refs for i in range(ref.shape[0])]


def whole_spec(array):
    return pl.BlockSpec(array.shape, lambda i, s: (0,) * array.ndim)


def share_send(pieces, weights, patch, group):
    kinds, width, double = weights.shape
    n = pieces[0].shape[-1] // (4 * group)
    return pl.pallas_call(
        share_kernel,
        grid_spec=pltpu.PrefetchScalarGridSpec(
            num_scalar_prefetch=1,
            grid=(1,),
            in_specs=[whole_spec(array) for array in pieces] + [pl.BlockSpec(memory_space=pltpu.HBM)],
            out_specs=[
                pl.BlockSpec((n, group, width), lambda i, s: (0, 0, 0)),
                pl.BlockSpec(memory_space=pltpu.HBM),
            ],
            scratch_shapes=[
                pltpu.VMEM((kinds, n, 2, 2, group, double), BF),
                pltpu.VMEM((kinds, width, double), BF),
                pltpu.VMEM((n, group, width), F32),
                pltpu.SemaphoreType.DMA((kinds + 1,)),
            ],
        ),
        out_shape=[
            jax.ShapeDtypeStruct((n, group, width), BF),
            pltpu.HBM((n, group, width), F32),
        ],
        compiler_params=ROOM,
    )(patch[None], *pieces, pltpu.with_memory_space_constraint(weights, pltpu.HBM))


def add_kernel(stay_hbm, come_ref, out_ref, stay_ref, sem):
    copy = pltpu.make_async_copy(stay_hbm, stay_ref, sem)
    copy.start()
    copy.wait()
    out_ref[...] = (stay_ref[...] + come_ref[...].astype(F32)).astype(BF)


def own_kernel(chip_ref, mine_ref, theirs_ref, *refs):
    norm = jnp.where(chip_ref[0] == 0, mine_ref[...], theirs_ref[...])
    part = refs[0].shape[1]
    for i, grads in enumerate(kinds_of(refs[:-1])):
        refs[-1][i * part : (i + 1) * part, :] = jnp.dot(grads, norm, preferred_element_type=F32)


def own_product(chip, mine, theirs, pieces):
    part = mine.shape[1]
    rows = part * sum(piece.shape[0] for piece in pieces)
    arrays = [pltpu.with_memory_space_constraint(x, pltpu.HBM) for x in (mine, theirs, *pieces)]
    return pl.pallas_call(
        own_kernel,
        grid_spec=pltpu.PrefetchScalarGridSpec(
            num_scalar_prefetch=1,
            grid=(1,),
            in_specs=[whole_spec(array) for array in arrays],
            out_specs=pl.BlockSpec((rows, part), lambda i, s: (0, 0)),
        ),
        out_shape=jax.ShapeDtypeStruct((rows, part), F32),
        compiler_params=ROOM,
    )(chip[None], *arrays)


def other_kernel(chip_ref, mine_ref, theirs_ref, acc_ref, *refs, factor, own_rows, relative):
    pieces, (out_ref, sum_ref) = refs[:-2], refs[-2:]
    norm = jnp.where(chip_ref[0] == 0, theirs_ref[...], mine_ref[...])
    part = pieces[0].shape[1]
    for i, grads in enumerate(kinds_of(pieces)):
        rows = slice(i * part, (i + 1) * part)
        total = acc_ref[rows, :] + jnp.dot(grads, norm, preferred_element_type=F32)
        sum_ref[rows, :] = total * factor
    full, left = divmod(sum_ref.shape[0], 128)
    packed = len(out_ref.shape) == 3 and out_ref.shape[2] == 128
    for n in range(full + (left > 0)):
        block = sum_ref[n * 128 : (n + 1) * 128, :].T if n < full else sum_ref[n * 128 :, :].T
        for k in range(out_ref.shape[0]):
            rows = block[k * own_rows : (k + 1) * own_rows].astype(BF)
            to = ((k // 2) ^ chip_ref[1]) * 2 + ((k % 2) ^ chip_ref[0]) if relative else k
            if not packed:
                out_ref[to, :, n * 128 : n * 128 + rows.shape[1]] = rows
            elif n < full:
                out_ref[to, n * own_rows : (n + 1) * own_rows, :] = rows
            else:
                rows = block[k * own_rows : (k + 1) * own_rows]
                both = jnp.concatenate([rows[: own_rows // 2], rows[own_rows // 2 :]], axis=1)
                out_ref[to, n * own_rows :, :] = both.astype(BF)


def packable(own_rows, lanes):
    return own_rows % 4 == 0 and lanes % 128 == 64


def other_product(place, mine, theirs, acc, pieces, own_rows, factor, relative):
    lanes, part = acc.shape
    chunk = (own_rows * lanes // 128, 128) if packable(own_rows, lanes) else (own_rows, lanes)
    shape = (part // own_rows,) + chunk
    mine, theirs = [pltpu.with_memory_space_constraint(x, pltpu.HBM) for x in (mine, theirs)]
    arrays = (mine, theirs, acc, *pieces)
    return pl.pallas_call(
        functools.partial(other_kernel, factor=factor, own_rows=own_rows, relative=relative),
        grid_spec=pltpu.PrefetchScalarGridSpec(
            num_scalar_prefetch=1,
            grid=(1,),
            in_specs=[whole_spec(array) for array in arrays],
            out_specs=pl.BlockSpec(shape, lambda i, s: (0, 0, 0)),
            scratch_shapes=[pltpu.VMEM((lanes, part), F32)],
        ),
        out_shape=jax.ShapeDtypeStruct(shape, BF),
        compiler_params=ROOM,
    )(place, *arrays)


def last_kernel(tm_ref, stay_ref, come_ref, x_ref, grad_ref, gain_ref, out_ref, *, columns, t_dev):
    n_pair, group, width = stay_ref.shape
    patches = x_ref.shape[0] // t_dev
    tm = tm_ref[0]
    first = tm % 2 == 0
    for z in range(n_pair):
        slot = (tm // 2) ^ z
        stay, come = stay_ref[slot].astype(F32), come_ref[slot].astype(F32)
        for y in range(2):
            d_norm = jnp.where(first == (y == 0), stay, come)
            for t in range(t_dev):
                at = t * patches + (2 * z + y) * columns
                rows = slice(at, at + columns)
                tokens = x_ref[rows, :].astype(F32)
                centered = tokens - jnp.mean(tokens, axis=-1, keepdims=True)
                variance = jnp.mean(centered * centered, axis=-1, keepdims=True)
                inverse = lax.rsqrt(variance + 1e-06)
                normed = centered * inverse
                scaled = d_norm[t * columns : (t + 1) * columns] * gain_ref[...]
                branch = inverse * (
                    scaled
                    - jnp.mean(scaled, axis=-1, keepdims=True)
                    - normed * jnp.mean(scaled * normed, axis=-1, keepdims=True)
                )
                out_ref[rows, :] = (grad_ref[rows, :].astype(F32) + branch).astype(BF)


def last(stay, come, tokens, grads, gain, tm, columns, t_dev):
    n_rows, width = tokens.shape
    part = pl.BlockSpec(stay.shape, lambda i, s: (0, 0, 0))
    rows = pl.BlockSpec((n_rows, width), lambda i, s: (0, 0))
    return pl.pallas_call(
        functools.partial(last_kernel, columns=columns, t_dev=t_dev),
        grid_spec=pltpu.PrefetchScalarGridSpec(
            num_scalar_prefetch=1,
            grid=(1,),
            in_specs=[part, part, rows, rows, pl.BlockSpec((1, width), lambda i, s: (0, 0))],
            out_specs=rows,
        ),
        out_shape=jax.ShapeDtypeStruct((n_rows, width), BF),
        compiler_params=ROOM,
    )(tm[None], stay, come, tokens, grads, gain[None])


def final_kernel(place_ref, *refs, part, kinds, n_chip):
    out_ref = refs[-1]
    own_rows = out_ref.shape[0]
    lanes = 2 * kinds * part
    count = (len(refs) - 1) // n_chip
    for x in range(n_chip):
        total = None
        for ref in refs[x * count : (x + 1) * count]:
            values = ref[...].astype(F32)
            total = values if total is None else total + values
        if packable(own_rows, lanes):
            full = lanes // 128
            blocks = [total[n * own_rows : (n + 1) * own_rows] for n in range(full)]
            both, half = total[full * own_rows :], own_rows // 2
            blocks.append(jnp.concatenate([both[:half, :64], both[:half, 64:]], axis=0))
            total = jnp.concatenate(blocks, axis=1)
        for core in range(2):
            for first in range(2):

                @pl.when((place_ref[0] == core) & (place_ref[1] == first))
                def _(core=core, first=first, total=total, x=x):
                    for r in range(2):
                        for c in range(kinds):
                            at = (c * n_chip * 2 + 2 * (x ^ first) + (r ^ core)) * part
                            src = (r * kinds + c) * part
                            out_ref[:, at : at + part] = total[:, src : src + part]


def final_sum(arrays, core, first, own_rows, part, kinds, n_chip):
    shape = (own_rows, 2 * n_chip * kinds * part)
    return pl.pallas_call(
        functools.partial(final_kernel, part=part, kinds=kinds, n_chip=n_chip),
        grid_spec=pltpu.PrefetchScalarGridSpec(
            num_scalar_prefetch=1,
            grid=(1,),
            in_specs=[whole_spec(array) for array in arrays],
            out_specs=pl.BlockSpec(shape, lambda i, s: (0, 0)),
        ),
        out_shape=jax.ShapeDtypeStruct(shape, F32),
        compiler_params=ROOM,
    )(jnp.stack([core, first]), *arrays)


def per_device(tokens, ln_gain, ln_bias, w_qkv, w_out, q_time, k_time, v_time, grad_out):
    t_dev, patches, width = tokens.shape
    frames, columns, part = q_time.shape
    n_tm = lax.axis_size("tm")
    n_patch = lax.axis_size("patch")
    n_pair = n_tm // 2
    n_chip = n_patch // 2
    devices = n_tm * n_patch
    n_tok = frames * columns
    own_rows = width // devices
    tm = lax.axis_index("tm")
    patch = lax.axis_index("patch")
    side = tm % 2
    core = patch % 2
    both = ("tm", "patch")

    def swap(values, axis, size, bit):
        return lax.ppermute(values, axis, [(i, i ^ bit) for i in range(size)])

    grad_rows = grad_out.reshape(-1, width)
    d_attn = jnp.einsum(
        "to,jfo->jtf", grad_rows, w_out.reshape(n_patch, part, width), preferred_element_type=F32
    ).astype(BF)
    d_attn = d_attn.reshape(n_patch, t_dev, n_tm, columns, part).transpose(2, 0, 1, 3, 4)
    d_attn, token_rows, w_late = lax.optimization_barrier((d_attn, tokens.reshape(-1, width), w_qkv))
    d_time = lax.all_to_all(
        d_attn.reshape(devices, t_dev, columns, part), both, 0, 0, tiled=True
    ).reshape(n_tok, part)

    sent = norm_send(token_rows, ln_gain, ln_bias, n_pair, n_chip, columns, own_rows, t_dev)
    weights = own_weights(w_late, patch // 2, n_chip)
    d_time, sent, weights = lax.optimization_barrier((d_time, sent, weights))
    mine = lax.all_to_all(sent, both, 0, 0, tiled=True).reshape(n_tok, width // 4)
    theirs = swap(mine, "patch", n_patch, 2)

    saved = [values.reshape(n_tok, part) for values in (q_time, k_time, v_time)]
    grads, *others = attend(*saved, d_time, columns)
    grads_core = swap(grads, "patch", n_patch, 1)
    pieces = [grads, grads_core]
    others = [swap(piece, "tm", n_tm, 1) for piece in others]

    leave, stay = share_send(pieces, weights, patch, t_dev * columns)
    come = swap(leave, "patch", n_patch, 2)
    share = pl.pallas_call(
        add_kernel,
        in_specs=[pl.BlockSpec(memory_space=space) for space in (pltpu.HBM, pltpu.VMEM)],
        out_shape=jax.ShapeDtypeStruct(leave.shape, BF),
        scratch_shapes=[pltpu.VMEM(stay.shape, F32), pltpu.SemaphoreType.DMA(())],
        compiler_params=ROOM,
    )(pltpu.with_memory_space_constraint(stay, pltpu.HBM), come)
    share = share.reshape((n_pair, 2) + share.shape[1:])
    spread = [lax.dynamic_index_in_dim(share, (tm // 2) ^ n, 0, keepdims=False) for n in range(n_pair)]
    spread = spread[:1] + [swap(spread[n], "tm", n_tm, 2 * n) for n in range(1, n_pair)]
    own = own_product(patch // 2, mine, theirs, pieces)
    others, theirs, own, early = lax.optimization_barrier((others, theirs, own, spread[2:]))
    others = list(others)
    spread = spread[:2] + early
    others += [swap(piece, "patch", n_patch, 1) for piece in others]

    factor = 1.0 / math.sqrt(frames * patches)
    across = n_pair == 4 and n_chip == 2
    place = jnp.stack([patch // 2, tm // 2])
    partial = other_product(place, mine, theirs, own, others, own_rows, factor, across)
    partial, spread = lax.optimization_barrier((partial, spread))
    if across:
        def send(values, dz, dx):
            flip = 2 * dz * n_patch + 2 * dx
            return lax.ppermute(values, both, [(i, i ^ flip) for i in range(devices)])

        passed = send(partial[6:8], 1, 0)
        summed = (partial[4:6].astype(F32) + passed.astype(F32)).astype(BF)
        near, summed = lax.optimization_barrier((partial[2:4], summed))
        own_chip = [partial[0], send(near[0], 1, 0), send(summed[0], 2, 0)]
        other_chip = [send(partial[1], 0, 1), send(near[1], 1, 1), send(summed[1], 2, 1)]
        summands, first = own_chip + other_chip, patch // 2
    else:
        groups = [
            [(2 * z + y) * n_patch + 2 * x + c for z in range(n_pair) for x in range(n_chip)]
            for y in range(2)
            for c in range(2)
        ]
        pieces = lax.all_to_all(partial, both, 0, 0, axis_index_groups=groups, tiled=True)
        summands = [pieces[z * n_chip + x] for x in range(n_chip) for z in range(n_pair)]
        first = 0 * core
    grad_w_qkv = final_sum(summands, core, first, own_rows, part, 3, n_chip)

    spread = jnp.stack(spread)
    stay = lax.dynamic_index_in_dim(spread, side, 1, keepdims=False)
    come = swap(lax.dynamic_index_in_dim(spread, 1 - side, 1, keepdims=False), "tm", n_tm, 1)
    grad_x = last(stay, come, tokens.reshape(-1, width), grad_rows, ln_gain, tm, columns, t_dev)
    grad_x = grad_x.reshape(t_dev, patches, width)
    return (grad_x, grad_w_qkv)


def solution(mesh):
    return jax.shard_map(
        per_device,
        mesh=mesh,
        in_specs=(
            P(("tm", "patch"), None, None),
            P(),
            P(),
            P(),
            P(),
            P(None, "tm", "patch"),
            P(None, "tm", "patch"),
            P(None, "tm", "patch"),
            P(("tm", "patch"), None, None),
        ),
        out_specs=(P(("tm", "patch"), None, None), P(("tm", "patch"), None)),
        check_vma=False,
    )
```
